128 devices in a mesh: vert: 64 (over z, y_hi, x, core), row: 2 (over y_lo).
Axes of the slice: x: 4, y: 4 (y_hi: 2, y_lo: 2; y = y_hi * 2 + y_lo), z: 4, core: 2. Of those that a mesh axis runs over, the one named last changes fastest.
Arguments:
- features: float32 [524288, 256], P(('vert', 'row')), may hold values from -6 to 6
- w_self: float32 [256, 256], replicated, may hold values from -0.375 to 0.375
- w_neigh: float32 [256, 256], replicated, may hold values from -0.75 to 0.75
- bias: float32 [256], replicated, may hold values from -3 to 3
- w_head: float32 [256], replicated, may hold values from -0.75 to 0.75
- tile_weights: float32 [16384, 128, 128], P(('vert', 'row')), may hold values from 0.01 to 1
- tile_dst: int32 [16384], P(('vert', 'row')), may hold values from 0 to 31
- tile_src: int32 [16384], P(('vert', 'row')), may hold values from 0 to 167
- tile_count: int32 [128], P(('vert', 'row')), may hold values from 16 to 128, as said below
- hub_block: int32 [128], P(('vert', 'row')), may hold values from 0 to 31
- send_rows: int32 [128, 128, 8], P(('vert', 'row')), may hold values from 0 to 4095
- send_count: int32 [128, 128], P(('vert', 'row')), may hold values from 1 to 8, as said below
- labels: int32 [524288], P(('vert', 'row')), may hold values from 0 to 1
Outputs:
- grad_self: float32 [256, 256], replicated
- grad_neigh: float32 [256, 256], replicated
- grad_bias: float32 [256], replicated
- grad_head: float32 [256], replicated
The draws below stay inside these ranges and needn't reach their ends.
Inputs may be any that keep to these rules, and one draw needn't show every extreme that they name: Tile t of a device is used when t < its tile_count; some device uses all 128 tiles and some 128 // 8. `send_count`: each sending device fills all 8 slots for at least one receiving device.
All inputs are finite; a program needn't handle non-finite values.
Results may differ from the reference program's by a relative error of at most 0.0003.
Values sent between devices are 32-bit elements; how exact they have to be, the bound alone decides.
A program may use at most 128 MiB of HBM per device.

```python
import math
import jax
import jax.numpy as jnp
from jax import lax

F = 256
BLK = 128
NB = 32
TILES = 128
CAP = 8
PEERS = 128
VERTS = 524288
SRC = 168


def draw_tile_count(key, part):
    first_key, second_key = jax.random.split(key)
    shifts = jax.random.randint(first_key, (PEERS,), 0, 4)
    counts = TILES // jnp.left_shift(jnp.ones((PEERS,), jnp.int32), shifts)
    order = jax.random.permutation(second_key, PEERS)
    counts = counts.at[order[0]].set(TILES)
    counts = counts.at[order[1]].set(TILES // 8)
    return counts.astype(jnp.int32)


def draw_send_count(key, part):
    first_key, second_key = jax.random.split(key)
    counts = jax.random.randint(first_key, (PEERS, PEERS), 1, CAP + 1)
    full_peer = jax.random.randint(second_key, (PEERS,), 0, PEERS)
    columns = jnp.arange(PEERS, dtype=jnp.int32)
    counts = jnp.where(columns[None, :] == full_peer[:, None], CAP, counts)
    return counts.astype(jnp.int32)


def touch_ends(array, own_key, smallest, top_value):
    longest = array.shape.index(max(array.shape))
    spots = []
    for shift in (0, 1):
        where = [jax.random.randint(jax.random.fold_in(own_key, axis), (), 0, length) for axis, length in enumerate(array.shape)]
        where[longest] = (where[longest] + shift) % array.shape[longest]
        spots.append(tuple(where))
    return array.at[spots[0]].set(smallest).at[spots[1]].set(top_value)


def block_scale(own_key, extent, cuts, smallest, top_value):
    level, own = 1.0, jax.random.fold_in(own_key, 6)
    for dim, parts in cuts:
        steps = jnp.exp(jax.random.uniform(jax.random.fold_in(own, dim), (parts,), jnp.float32, smallest / len(cuts), top_value / len(cuts)))
        level = level * jnp.repeat(steps, extent[dim] // parts).reshape([-1 if axis == dim else 1 for axis in range(len(extent))])
    return level


def scatter_about(own_key, shape, spread, limit, shards=(), held_as=jnp.bfloat16):
    entries = spread * jax.random.normal(own_key, shape, jnp.float32)
    if shards:
        entries = entries * block_scale(own_key, shape, shards, -0.22, 0.18)
    return jnp.clip(entries, -limit, limit).astype(held_as)


def setup_inputs(seed: int = 0) -> dict:
    seeds = jax.random.split(jax.random.key(seed), 14)
    return {
        "features": scatter_about(seeds[0], (VERTS, F), 1.0, 6.0, ((0, 128),), jnp.float32),
        "w_self": scatter_about(seeds[1], (F, F), F ** -0.5, 0.375, (), jnp.float32),
        "w_neigh": scatter_about(seeds[2], (F, F), (F // 4) ** -0.5, 0.75, (), jnp.float32),
        "bias": scatter_about(seeds[3], (F,), 0.5, 3.0, (), jnp.float32),
        "w_head": scatter_about(seeds[4], (F,), (F // 4) ** -0.5, 0.75, (), jnp.float32),
        "tile_weights": jnp.clip(jnp.exp(math.log(1.0) - 4.6051702 * jax.random.uniform(seeds[5], (PEERS * TILES, BLK, BLK), jnp.float32) ** block_scale(seeds[5], (PEERS * TILES, BLK, BLK), ((0, 128),), -0.2, 0.2)), 0.01, 1.0),
        "tile_dst": touch_ends(jax.random.randint(seeds[6], (PEERS * TILES,), 0, NB), jax.random.fold_in(seeds[6], 1), 0, NB - 1).astype(jnp.int32),
        "tile_src": touch_ends(jax.random.randint(seeds[7], (PEERS * TILES,), 0, SRC), jax.random.fold_in(seeds[7], 1), 0, SRC - 1).astype(jnp.int32),
        "tile_count": draw_tile_count(jax.random.fold_in(seeds[13], 71), 0),
        "hub_block": touch_ends(jax.random.randint(seeds[9], (PEERS,), 0, NB), jax.random.fold_in(seeds[9], 1), 0, NB - 1).astype(jnp.int32),
        "send_rows": touch_ends(jax.random.randint(seeds[10], (PEERS, PEERS, CAP), 0, NB * BLK), jax.random.fold_in(seeds[10], 1), 0, (NB * BLK) - 1).astype(jnp.int32),
        "send_count": draw_send_count(jax.random.fold_in(seeds[13], 71), 0),
        "labels": touch_ends(jax.random.randint(seeds[12], (VERTS,), 0, 2), jax.random.fold_in(seeds[12], 1), 0, 1).astype(jnp.int32),
    }


FULL_PRECISION = lax.Precision.HIGHEST

def reference(features, w_self, w_neigh, bias, w_head, tile_weights, tile_dst, tile_src, tile_count, hub_block, send_rows, send_count, labels):
    feats_three = features.reshape(PEERS, NB * BLK, F)
    blocks_four = features.reshape(PEERS, NB, BLK, F)
    device_ids = jnp.arange(PEERS, dtype=jnp.int32)
    hub_blocks = blocks_four[device_ids, hub_block]
    slot_index = jnp.arange(CAP, dtype=jnp.int32)
    block_ids = jnp.arange(NB, dtype=jnp.int32)
    tile_ids = jnp.arange(TILES, dtype=jnp.int32)

    def per_device(device):
        own_blocks = lax.dynamic_index_in_dim(blocks_four, device, 0, keepdims=False)
        listed = lax.dynamic_index_in_dim(send_rows, device, 1, keepdims=False)
        counts = lax.dynamic_index_in_dim(send_count, device, 1, keepdims=False)
        border = feats_three[device_ids[:, None], listed]
        alive = slot_index[None, :] < counts[:, None]
        border = jnp.where(alive[:, :, None], border, jnp.zeros_like(border))
        source_table = jnp.concatenate([own_blocks, border.reshape(-1, BLK, F), hub_blocks], 0)
        start = (device * TILES).astype(jnp.int32)
        weights_here = lax.dynamic_slice_in_dim(tile_weights, start, TILES, 0)
        dst_here = lax.dynamic_slice_in_dim(tile_dst, start, TILES, 0)
        src_here = lax.dynamic_slice_in_dim(tile_src, start, TILES, 0)
        count_here = lax.dynamic_index_in_dim(tile_count, device, 0, keepdims=False)
        active = tile_ids < count_here
        picked = source_table[src_here]
        contrib = jnp.einsum('tij,tjf->tif', weights_here, picked, precision=FULL_PRECISION)
        selector = ((dst_here[None, :] == block_ids[:, None]) & active[None, :]).astype(features.dtype)
        summed = jnp.einsum('bt,tif->bif', selector, contrib, precision=FULL_PRECISION)
        weight_sum = jnp.einsum('bt,ti->bi', selector, lax.optimization_barrier(jnp.sum(weights_here, axis=2)), precision=FULL_PRECISION)
        neigh_mean = (own_blocks + summed) / (1.0 + weight_sum)[:, :, None]
        return neigh_mean.reshape(NB * BLK, F)
    neigh_mean = lax.map(per_device, device_ids).reshape(VERTS, F)
    pre_act = jnp.dot(features, w_self, precision=FULL_PRECISION) + jnp.dot(neigh_mean, w_neigh, precision=FULL_PRECISION) + bias[None, :]
    sigmoid_pre = jax.nn.sigmoid(pre_act)
    hidden = pre_act * sigmoid_pre
    head_score = jnp.dot(hidden, w_head, precision=FULL_PRECISION)
    target = 2.0 * labels.astype(features.dtype) - 1.0
    loss_scale = 1.0 / math.sqrt(VERTS)
    dscore = (head_score - target) * loss_scale
    dpre = dscore[:, None] * w_head[None, :] * (sigmoid_pre * (1.0 + pre_act * (1.0 - sigmoid_pre)))
    grad_self = jnp.dot(features.T, dpre, precision=FULL_PRECISION)
    grad_neigh = jnp.dot(neigh_mean.T, dpre, precision=FULL_PRECISION)
    grad_bias = lax.optimization_barrier(jnp.sum(dpre, axis=0))
    grad_head = jnp.dot(hidden.T, dscore, precision=FULL_PRECISION)
    return (grad_self, grad_neigh, grad_bias, grad_head)
```

```python
import functools
import math

import jax
import jax.numpy as jnp
from jax import lax
from jax.experimental import pallas as pl
from jax.experimental.pallas import tpu as pltpu
from jax.sharding import PartitionSpec as P

MESH = pl.DeviceIdType.MESH
BF16 = jnp.bfloat16
F32 = jnp.float32

PART_START = (0, 88, 176)
PART_ROWS = (88, 88, 80)
PART_HALF = (48, 40, 40)
PART_AXES = ("xyz", "yzx", "zxy")
OFFSETS = (0, 3, 1, 2)


def my_place():
    vert = lax.axis_index("vert")
    row = lax.axis_index("row")
    core = lax.rem(vert, 2)
    x = lax.rem(lax.div(vert, 2), 4)
    y = lax.rem(lax.div(vert, 8), 2) * 2 + row
    z = lax.div(vert, 16)
    return {"x": x, "y": y, "z": z}, core


def device_at(place, core):
    x, y, z = place["x"], place["y"], place["z"]
    vert = ((z * 2 + lax.div(y, 2)) * 4 + x) * 2 + core
    return (vert, lax.rem(y, 2))


def shifted(place, axis, step):
    moved = dict(place)
    moved[axis] = lax.rem(place[axis] + step, 4)
    return moved


def gather_kernel(hub_ref, table_ref, own_sem, recv1, recv2, recv3, send1, send2, send3, pair_send, pair_recv):
    place, core = my_place()
    near = {}
    for axis in "xyz":
        for step in (1, 3):
            near[axis, step] = device_at(shifted(place, axis, step), core)
    sibling = device_at(place, 1 - core)

    barrier = pltpu.get_barrier_semaphore()
    for target in list(near.values()) + [sibling]:
        pl.semaphore_signal(barrier, inc=1, device_id=target, device_id_type=MESH)
    pl.semaphore_wait(barrier, 7)

    def slot(part, where, half=None):
        start, rows = PART_START[part], PART_ROWS[part]
        if half == 0:
            rows = PART_HALF[part]
        elif half == 1:
            start, rows = start + PART_HALF[part], rows - PART_HALF[part]
        at = []
        for axis in "zyx":
            offset = where.get(axis, 0)
            at.append(pl.ds(0, 4) if offset == "all" else lax.rem(place[axis] + offset, 4))
        return table_ref.at[(core, *at, pl.ds(start, rows), slice(None))]

    def remote(src, dst, send_sem, recv_sem, target):
        return pltpu.make_async_remote_copy(
            src_ref=src, dst_ref=dst, send_sem=send_sem, recv_sem=recv_sem,
            device_id=target, device_id_type=MESH,
        )

    def send_both(part, where, axis, send_sem, recv, from_hub=False):
        dst = slot(part, where)
        src = hub_ref.at[pl.ds(PART_START[part], PART_ROWS[part]), :] if from_hub else dst
        remote(src, dst, send_sem, recv.at[0], near[axis, 1]).start()
        remote(src, dst, send_sem, recv.at[1], near[axis, 3]).start()

    def arrived(part, where, axis, sem, half=None):
        ref = slot(part, where, half)
        remote(ref, ref, sem, sem, near[axis, 1]).wait_recv()

    def pass_on(part, where, axis, send_sem, recv, half):
        ref = slot(part, where, half)
        remote(ref, ref, send_sem, recv.at[2 + half], near[axis, 1 if half == 0 else 3]).start()

    def to_sibling(part, where):
        ref = slot(part, where)
        remote(ref, ref, pair_send, pair_recv, sibling).start()

    parts = range(3)
    own = pltpu.make_async_copy(
        hub_ref, table_ref.at[core, place["z"], place["y"], place["x"]], own_sem
    )
    own.start()
    for p in parts:
        first, second, _ = PART_AXES[p]
        send_both(p, {}, first, send1.at[p], recv1.at[p], from_hub=True)
        send_both(p, {}, second, send2.at[p], recv2.at[p, 0], from_hub=True)
    own.wait()

    for side, offset in ((0, 3), (1, 1)):
        unit = OFFSETS.index(offset)
        for p in parts:
            first, second, _ = PART_AXES[p]
            where = {first: offset}
            arrived(p, where, first, recv1.at[p, side])
            pass_on(p, where, first, send1.at[p], recv1.at[p], side)
            send_both(p, where, second, send2.at[p], recv2.at[p, unit])
    for p in parts:
        first, second, third = PART_AXES[p]
        where = {first: 2}
        arrived(p, where, first, recv1.at[p, 2], 0)
        arrived(p, where, first, recv1.at[p, 3], 1)
        send_both(p, where, second, send2.at[p], recv2.at[p, 3])
        line = {first: "all"}
        send_both(p, line, third, send3.at[p], recv3.at[p, 0])
        to_sibling(p, line)

    for unit in range(4):
        for side, offset in ((0, 3), (1, 1)):
            for p in parts:
                first, second, _ = PART_AXES[p]
                where = {first: OFFSETS[unit], second: offset}
                arrived(p, where, second, recv2.at[p, unit, side])
                pass_on(p, where, second, send2.at[p], recv2.at[p, unit], side)
    for side, offset in ((0, 3), (1, 1)):
        for p in parts:
            first, second, third = PART_AXES[p]
            line = {first: "all", second: offset}
            send_both(p, line, third, send3.at[p], recv3.at[p, 1 + side])
            to_sibling(p, line)
    for p in parts:
        first, second, third = PART_AXES[p]
        for unit in range(4):
            where = {first: OFFSETS[unit], second: 2}
            arrived(p, where, second, recv2.at[p, unit, 2], 0)
            arrived(p, where, second, recv2.at[p, unit, 3], 1)
        line = {first: "all", second: 2}
        send_both(p, line, third, send3.at[p], recv3.at[p, 3])
        to_sibling(p, line)

    for unit in range(4):
        for side, offset in ((0, 3), (1, 1)):
            for p in parts:
                first, second, third = PART_AXES[p]
                line = {first: "all", second: OFFSETS[unit], third: offset}
                arrived(p, line, third, recv3.at[p, unit, side])
                pass_on(p, line, third, send3.at[p], recv3.at[p, unit], side)
                to_sibling(p, line)
    for unit in range(4):
        for p in parts:
            first, second, third = PART_AXES[p]
            line = {first: "all", second: OFFSETS[unit], third: 2}
            arrived(p, line, third, recv3.at[p, unit, 2], 0)
            arrived(p, line, third, recv3.at[p, unit, 3], 1)
            to_sibling(p, line)

    for p in parts:
        rows = pl.ds(PART_START[p], PART_ROWS[p])
        for sem, ref in (
            (send1.at[p], table_ref.at[core, 0, 0, pl.ds(0, 3), rows, :]),
            (send2.at[p], table_ref.at[core, 0, pl.ds(0, 3), pl.ds(0, 4), rows, :]),
            (send3.at[p], table_ref.at[core, pl.ds(0, 3), pl.ds(0, 4), pl.ds(0, 4), rows, :]),
        ):
            pltpu.make_async_copy(ref, ref, sem).wait()
    mine, theirs = table_ref.at[core], table_ref.at[1 - core]
    pltpu.make_async_copy(mine, mine, pair_send).wait()
    pltpu.make_async_copy(theirs, theirs, pair_recv).wait()


def gather_hubs(hub):
    dma = pltpu.SemaphoreType.DMA
    return pl.pallas_call(
        gather_kernel,
        out_shape=jax.ShapeDtypeStruct((2, 4, 4, 4, 256, 128), F32),
        in_specs=[pl.BlockSpec(memory_space=pl.ANY)],
        out_specs=pl.BlockSpec(memory_space=pl.ANY),
        scratch_shapes=[
            dma, dma((3, 4)), dma((3, 4, 4)), dma((3, 4, 4)),
            dma((3,)), dma((3,)), dma((3,)), dma, dma,
        ],
        compiler_params=pltpu.CompilerParams(collective_id=0, has_side_effects=True),
        name="gather_hubs",
    )(hub)


GROUP = 4
RING = 4
CHUNK = 256


def split(value):
    high = value.astype(BF16)
    low = (value - high.astype(F32)).astype(BF16)
    return high, low


def dot3(a, b, dims=(((1,), (0,)), ((), ()))):
    a_high, a_low = a
    b_high, b_low = b
    dot = functools.partial(lax.dot_general, dimension_numbers=dims, preferred_element_type=F32)
    return dot(a_high, b_high) + (dot(a_low, b_high) + dot(a_high, b_low))


def layer_kernel(
    loss_scale, dst_ref, src_ref, count_ref,
    feat_hbm, border_hbm, table_hbm, weights_hbm, w_self_ref, w_neigh_ref, bias_ref, head_ref, labels_ref,
    grad_self_ref, grad_neigh_ref, grad_small_ref,
    feat, weights, ring, total, weight_total, self_high, self_low, neigh_high, neigh_low,
    feat_sem, weight_sem, ring_sem,
):
    tiles = weights.shape[0]
    blocks = feat.shape[0] // 128
    border_blocks = border_hbm.shape[0]
    count = count_ref[0]
    groups = lax.div(count + (GROUP - 1), GROUP)
    load_feat = pltpu.make_async_copy(feat_hbm, feat, feat_sem)

    def load_weights(group):
        at = pl.ds(group * GROUP, GROUP)
        return pltpu.make_async_copy(weights_hbm.at[at], weights.at[at], weight_sem.at[group])

    def fetch(group):
        spot = lax.rem(group, RING)
        for k in range(GROUP):
            src = src_ref[group * GROUP + k]
            sem = ring_sem.at[spot, k]

            def halves(ref, block):
                for side in range(2):
                    pltpu.make_async_copy(
                        ref.at[block, :, pl.ds(128 * side, 128)],
                        ring.at[spot, k, pl.ds(128 * side, 128), :],
                        sem,
                    ).start()

            @pl.when(src < blocks)
            def _():
                for side in range(2):
                    pltpu.make_async_copy(
                        feat_hbm.at[pl.ds(pl.multiple_of(src * 128, 128), 128), pl.ds(128 * side, 128)],
                        ring.at[spot, k, pl.ds(128 * side, 128), :],
                        sem,
                    ).start()

            @pl.when((src >= blocks) & (src < blocks + border_blocks))
            def _():
                halves(border_hbm, src - blocks)

            @pl.when(src >= blocks + border_blocks)
            def _():
                pltpu.make_async_copy(
                    table_hbm.at[src - (blocks + border_blocks)], ring.at[spot, k], sem
                ).start()

    for group in range(RING - 1):
        @pl.when(group < groups)
        def _():
            load_weights(group).start()
            fetch(group)

    @pl.loop(RING - 1, groups)
    def _(group):
        load_weights(group).start()

    load_feat.start()
    total[...] = jnp.zeros_like(total)
    weight_total[...] = jnp.zeros_like(weight_total)
    self_high[...], self_low[...] = split(w_self_ref[...])
    neigh_high[...], neigh_low[...] = split(w_neigh_ref[...])

    @pl.loop(0, groups)
    def _(group):
        spot = lax.rem(group, RING)
        load_weights(group).wait()
        for k in range(GROUP):
            pltpu.make_async_copy(table_hbm.at[0], ring.at[spot, k], ring_sem.at[spot, k]).wait()

        @pl.when(group + (RING - 1) < groups)
        def _():
            fetch(group + (RING - 1))

        for k in range(GROUP):
            tile = group * GROUP + k
            dst = jnp.where(tile < count, dst_ref[tile], blocks)
            weight = weights[tile]
            source = jnp.concatenate([ring[spot, k, 0:128, :], ring[spot, k, 128:256, :]], axis=1)
            total[dst] += dot3(split(weight), split(source))
            weight_total[dst] += weight

    load_feat.wait()
    labels = labels_ref[...].astype(F32)
    target_columns = (2.0 * labels - 1.0).T
    lane = lax.broadcasted_iota(jnp.int32, target_columns.shape, 1)
    grad_self_ref[...] = jnp.zeros_like(grad_self_ref)
    grad_neigh_ref[...] = jnp.zeros_like(grad_neigh_ref)
    grad_small_ref[...] = jnp.zeros_like(grad_small_ref)
    per_chunk = CHUNK // 128

    @pl.loop(0, blocks // per_chunk)
    def _(chunk):
        rows = pl.ds(pl.multiple_of(chunk * CHUNK, CHUNK), CHUNK)
        own = feat[rows, :]
        at = pl.ds(chunk * per_chunk, per_chunk)
        summed = total[at].reshape(CHUNK, 256)
        weight_sum = jnp.sum(weight_total[at].reshape(CHUNK, 128), axis=1, keepdims=True)
        mean = (own + summed) * (1.0 / (1.0 + weight_sum))
        own_parts, mean_parts = split(own), split(mean)
        pre = (
            dot3(own_parts, (self_high[...], self_low[...]))
            + dot3(mean_parts, (neigh_high[...], neigh_low[...]))
            + bias_ref[...]
        )
        gate = jax.nn.sigmoid(pre)
        hidden = pre * gate
        score = jnp.sum(hidden * head_ref[...], axis=1, keepdims=True)
        target = jnp.concatenate(
            [
                jnp.sum(jnp.where(lane == chunk * per_chunk + i, target_columns, 0.0), axis=1, keepdims=True)
                for i in range(per_chunk)
            ],
            axis=0,
        )
        dscore = (score - target) * loss_scale
        dpre = dscore * head_ref[...] * (gate * (1.0 + pre * (1.0 - gate)))
        dpre_parts = split(dpre)
        by_rows = (((0,), (0,)), ((), ()))
        grad_self_ref[...] += dot3(own_parts, dpre_parts, by_rows)
        grad_neigh_ref[...] += dot3(mean_parts, dpre_parts, by_rows)
        grad_small_ref[0:1, :] += jnp.sum(dpre, axis=0, keepdims=True)
        grad_small_ref[1:2, :] += jnp.sum(hidden * dscore, axis=0, keepdims=True)


def layer(loss_scale, dst, src, count, features, border, table, weights, w_self, w_neigh, bias, head, labels):
    tiles = weights.shape[0]
    vertices, width = features.shape
    blocks = vertices // 128
    dma = pltpu.SemaphoreType.DMA
    smem = pl.BlockSpec(memory_space=pltpu.SMEM)
    vmem = pl.BlockSpec(memory_space=pltpu.VMEM)
    hbm = pl.BlockSpec(memory_space=pl.ANY)
    return pl.pallas_call(
        functools.partial(layer_kernel, loss_scale),
        out_shape=(
            jax.ShapeDtypeStruct((width, width), F32),
            jax.ShapeDtypeStruct((width, width), F32),
            jax.ShapeDtypeStruct((8, width), F32),
        ),
        in_specs=[smem] * 3 + [hbm] * 4 + [vmem] * 5,
        out_specs=(vmem, vmem, vmem),
        scratch_shapes=[
            pltpu.VMEM((vertices, width), F32),
            pltpu.VMEM((tiles, 128, 128), F32),
            pltpu.VMEM((RING, GROUP, 256, 128), F32),
            pltpu.VMEM((blocks + 1, 128, width), F32),
            pltpu.VMEM((blocks + 1, 128, 128), F32),
            pltpu.VMEM((width, width), BF16),
            pltpu.VMEM((width, width), BF16),
            pltpu.VMEM((width, width), BF16),
            pltpu.VMEM((width, width), BF16),
            dma,
            dma((tiles // GROUP,)),
            dma((RING, GROUP)),
        ],
        compiler_params=pltpu.CompilerParams(vmem_limit_bytes=48 * 2**20),
        name="layer",
    )(dst, src, count, features, border, table, weights, w_self, w_neigh, bias, head, labels)


def on_device(
    features,
    w_self,
    w_neigh,
    bias,
    w_head,
    tile_weights,
    tile_dst,
    tile_src,
    tile_count,
    hub_block,
    send_rows,
    send_count,
    labels,
):
    axes = ("vert", "row")
    width = features.shape[1]
    slots = send_rows.shape[2]
    blocks = features.shape[0] // 128
    peers = lax.axis_size(axes)

    hub = lax.dynamic_slice(features, (hub_block[0] * 128, 0), (128, width))
    hub = hub.reshape(128, 2, 128).transpose(1, 0, 2).reshape(256, 128)
    outgoing = features[send_rows[0]]
    alive = jnp.arange(slots, dtype=jnp.int32)[None, :] < send_count[0][:, None]
    outgoing = jnp.where(alive[:, :, None], outgoing, jnp.zeros_like(outgoing))
    incoming = lax.all_to_all(outgoing, axes, split_axis=0, concat_axis=0, tiled=True)
    border = incoming.reshape(-1, 128, width)
    table = gather_hubs(hub).reshape(peers, 256, 128)

    first_hub = blocks + border.shape[0]
    number = tile_src - first_hub
    y_low, core, x, y_high, z = number & 1, (number >> 1) & 1, (number >> 2) & 3, (number >> 4) & 1, number >> 5
    entry = core * 64 + z * 16 + (y_high * 2 + y_low) * 4 + x
    src = jnp.where(number < 0, tile_src, entry + first_hub)

    loss_scale = 1.0 / math.sqrt(features.shape[0] * peers)
    grad_self, grad_neigh, grad_small = layer(
        loss_scale, tile_dst, src, tile_count, features, border, table, tile_weights,
        w_self, w_neigh, bias.reshape(1, width), w_head.reshape(1, width), labels.reshape(blocks, 128),
    )
    small = grad_small[0:2].reshape(peers, 1, -1)
    small = jnp.pad(small, ((0, 0), (0, 0), (0, 128 - small.shape[2])))
    flat = jnp.concatenate(
        [grad_self.reshape(peers, -1, 128), grad_neigh.reshape(peers, -1, 128), small], axis=1
    )
    flat = lax.all_to_all(flat, axes, split_axis=0, concat_axis=0, tiled=True)
    part = jnp.sum(flat, axis=0, keepdims=True)
    flat = lax.all_to_all(
        jnp.broadcast_to(part, flat.shape), axes, split_axis=0, concat_axis=0, tiled=True
    )
    quarter = width * width // peers // 128
    grad_self = flat[:, 0:quarter].reshape(width, width)
    grad_neigh = flat[:, quarter:2 * quarter].reshape(width, width)
    small = flat[:, 2 * quarter, 0:2 * width // peers].reshape(2, width)
    return (grad_self, grad_neigh, small[0], small[1])


def solution(mesh):
    in_specs = (
        P(("vert", "row"), None),
        P(),
        P(),
        P(),
        P(),
        P(("vert", "row"), None, None),
        P(("vert", "row")),
        P(("vert", "row")),
        P(("vert", "row")),
        P(("vert", "row")),
        P(("vert", "row"), None, None),
        P(("vert", "row"), None),
        P(("vert", "row")),
    )
    out_specs = (P(), P(), P(), P())
    return jax.shard_map(
        on_device, mesh=mesh, in_specs=in_specs, out_specs=out_specs, check_vma=False
    )
```

```python
import functools
import math

import jax
import jax.numpy as jnp
from jax import lax
from jax.experimental import pallas as pl
from jax.experimental.pallas import tpu as pltpu
from jax.sharding import PartitionSpec as P

MESH = pl.DeviceIdType.MESH
BF16 = jnp.bfloat16
F32 = jnp.float32

PART_START = (0, 88, 176)
PART_ROWS = (88, 88, 80)
PART_HALF = (48, 40, 40)
PART_AXES = ("xyz", "yzx", "zxy")
OFFSETS = (0, 3, 1, 2)


def my_place():
    vert = lax.axis_index("vert")
    row = lax.axis_index("row")
    core = lax.rem(vert, 2)
    x = lax.rem(lax.div(vert, 2), 4)
    y = lax.rem(lax.div(vert, 8), 2) * 2 + row
    z = lax.div(vert, 16)
    return {"x": x, "y": y, "z": z}, core


def device_at(place, core):
    x, y, z = place["x"], place["y"], place["z"]
    vert = ((z * 2 + lax.div(y, 2)) * 4 + x) * 2 + core
    return (vert, lax.rem(y, 2))


def shifted(place, axis, step):
    moved = dict(place)
    moved[axis] = lax.rem(place[axis] + step, 4)
    return moved


def gather_kernel(hub_ref, table_ref, own_sem, recv1, recv2, recv3, send1, send2, send3, pair_send, pair_recv):
    place, core = my_place()
    near = {}
    for axis in "xyz":
        for step in (1, 3):
            near[axis, step] = device_at(shifted(place, axis, step), core)
    sibling = device_at(place, 1 - core)

    barrier = pltpu.get_barrier_semaphore()
    for target in list(near.values()) + [sibling]:
        pl.semaphore_signal(barrier, inc=1, device_id=target, device_id_type=MESH)
    pl.semaphore_wait(barrier, 7)

    def slot(part, where, half=None):
        start, rows = PART_START[part], PART_ROWS[part]
        if half == 0:
            rows = PART_HALF[part]
        elif half == 1:
            start, rows = start + PART_HALF[part], rows - PART_HALF[part]
        at = []
        for axis in "zyx":
            offset = where.get(axis, 0)
            at.append(pl.ds(0, 4) if offset == "all" else lax.rem(place[axis] + offset, 4))
        return table_ref.at[(core, *at, pl.ds(start, rows), slice(None))]

    def remote(src, dst, send_sem, recv_sem, target):
        return pltpu.make_async_remote_copy(
            src_ref=src, dst_ref=dst, send_sem=send_sem, recv_sem=recv_sem,
            device_id=target, device_id_type=MESH,
        )

    def send_both(part, where, axis, send_sem, recv, from_hub=False):
        dst = slot(part, where)
        src = hub_ref.at[pl.ds(PART_START[part], PART_ROWS[part]), :] if from_hub else dst
        remote(src, dst, send_sem, recv.at[0], near[axis, 1]).start()
        remote(src, dst, send_sem, recv.at[1], near[axis, 3]).start()

    def arrived(part, where, axis, sem, half=None):
        ref = slot(part, where, half)
        remote(ref, ref, sem, sem, near[axis, 1]).wait_recv()

    def pass_on(part, where, axis, send_sem, recv, half):
        ref = slot(part, where, half)
        remote(ref, ref, send_sem, recv.at[2 + half], near[axis, 1 if half == 0 else 3]).start()

    def to_sibling(part, where):
        ref = slot(part, where)
        remote(ref, ref, pair_send, pair_recv, sibling).start()

    parts = range(3)
    own = pltpu.make_async_copy(
        hub_ref, table_ref.at[core, place["z"], place["y"], place["x"]], own_sem
    )
    own.start()
    for p in parts:
        first, second, _ = PART_AXES[p]
        send_both(p, {}, first, send1.at[p], recv1.at[p], from_hub=True)
        send_both(p, {}, second, send2.at[p], recv2.at[p, 0], from_hub=True)
    own.wait()

    for side, offset in ((0, 3), (1, 1)):
        unit = OFFSETS.index(offset)
        for p in parts:
            first, second, _ = PART_AXES[p]
            where = {first: offset}
            arrived(p, where, first, recv1.at[p, side])
            pass_on(p, where, first, send1.at[p], recv1.at[p], side)
            send_both(p, where, second, send2.at[p], recv2.at[p, unit])
    for p in parts:
        first, second, third = PART_AXES[p]
        where = {first: 2}
        arrived(p, where, first, recv1.at[p, 2], 0)
        arrived(p, where, first, recv1.at[p, 3], 1)
        send_both(p, where, second, send2.at[p], recv2.at[p, 3])
        line = {first: "all"}
        send_both(p, line, third, send3.at[p], recv3.at[p, 0])
        to_sibling(p, line)

    for unit in range(4):
        for side, offset in ((0, 3), (1, 1)):
            for p in parts:
                first, second, _ = PART_AXES[p]
                where = {first: OFFSETS[unit], second: offset}
                arrived(p, where, second, recv2.at[p, unit, side])
                pass_on(p, where, second, send2.at[p], recv2.at[p, unit], side)
    for side, offset in ((0, 3), (1, 1)):
        for p in parts:
            first, second, third = PART_AXES[p]
            line = {first: "all", second: offset}
            send_both(p, line, third, send3.at[p], recv3.at[p, 1 + side])
            to_sibling(p, line)
    for p in parts:
        first, second, third = PART_AXES[p]
        for unit in range(4):
            where = {first: OFFSETS[unit], second: 2}
            arrived(p, where, second, recv2.at[p, unit, 2], 0)
            arrived(p, where, second, recv2.at[p, unit, 3], 1)
        line = {first: "all", second: 2}
        send_both(p, line, third, send3.at[p], recv3.at[p, 3])
        to_sibling(p, line)

    for unit in range(4):
        for side, offset in ((0, 3), (1, 1)):
            for p in parts:
                first, second, third = PART_AXES[p]
                line = {first: "all", second: OFFSETS[unit], third: offset}
                arrived(p, line, third, recv3.at[p, unit, side])
                pass_on(p, line, third, send3.at[p], recv3.at[p, unit], side)
                to_sibling(p, line)
    for unit in range(4):
        for p in parts:
            first, second, third = PART_AXES[p]
            line = {first: "all", second: OFFSETS[unit], third: 2}
            arrived(p, line, third, recv3.at[p, unit, 2], 0)
            arrived(p, line, third, recv3.at[p, unit, 3], 1)
            to_sibling(p, line)

    for p in parts:
        rows = pl.ds(PART_START[p], PART_ROWS[p])
        for sem, ref in (
            (send1.at[p], table_ref.at[core, 0, 0, pl.ds(0, 3), rows, :]),
            (send2.at[p], table_ref.at[core, 0, pl.ds(0, 3), pl.ds(0, 4), rows, :]),
            (send3.at[p], table_ref.at[core, pl.ds(0, 3), pl.ds(0, 4), pl.ds(0, 4), rows, :]),
        ):
            pltpu.make_async_copy(ref, ref, sem).wait()
    mine, theirs = table_ref.at[core], table_ref.at[1 - core]
    pltpu.make_async_copy(mine, mine, pair_send).wait()
    pltpu.make_async_copy(theirs, theirs, pair_recv).wait()


def gather_hubs(hub):
    dma = pltpu.SemaphoreType.DMA
    return pl.pallas_call(
        gather_kernel,
        out_shape=jax.ShapeDtypeStruct((2, 4, 4, 4, 256, 128), F32),
        in_specs=[pl.BlockSpec(memory_space=pl.ANY)],
        out_specs=pl.BlockSpec(memory_space=pl.ANY),
        scratch_shapes=[
            dma, dma((3, 4)), dma((3, 4, 4)), dma((3, 4, 4)),
            dma((3,)), dma((3,)), dma((3,)), dma, dma,
        ],
        compiler_params=pltpu.CompilerParams(collective_id=0, has_side_effects=True),
        name="gather_hubs",
    )(hub)


GROUP = 4
RING = 4
CHUNK = 256


def split(value):
    high = value.astype(BF16)
    low = (value - high.astype(F32)).astype(BF16)
    return high, low


def dot3(a, b, dims=(((1,), (0,)), ((), ()))):
    a_high, a_low = a
    b_high, b_low = b
    dot = functools.partial(lax.dot_general, dimension_numbers=dims, preferred_element_type=F32)
    return dot(a_high, b_high) + (dot(a_low, b_high) + dot(a_high, b_low))


def layer_kernel(
    loss_scale, dst_ref, src_ref, count_ref,
    feat_hbm, border_hbm, table_hbm, weights_hbm, w_self_ref, w_neigh_ref, bias_ref, head_ref, labels_ref,
    grad_ref,
    grad_self_ref, grad_neigh_ref, grad_small_ref, feat, weights, ring, total, weight_total, self_high, self_low, neigh_high, neigh_low,
    feat_sem, weight_sem, ring_sem,
):
    tiles = weights.shape[0]
    blocks = feat.shape[0] // 128
    border_blocks = border_hbm.shape[0]
    count = count_ref[0]
    groups = lax.div(count + (GROUP - 1), GROUP)
    load_feat = pltpu.make_async_copy(feat_hbm, feat, feat_sem)

    def load_weights(group):
        at = pl.ds(group * GROUP, GROUP)
        return pltpu.make_async_copy(weights_hbm.at[at], weights.at[at], weight_sem.at[group])

    def fetch(group):
        spot = lax.rem(group, RING)
        for k in range(GROUP):
            src = src_ref[group * GROUP + k]
            sem = ring_sem.at[spot, k]

            def halves(ref, block):
                for side in range(2):
                    pltpu.make_async_copy(
                        ref.at[block, :, pl.ds(128 * side, 128)],
                        ring.at[spot, k, pl.ds(128 * side, 128), :],
                        sem,
                    ).start()

            @pl.when(src < blocks)
            def _():
                for side in range(2):
                    pltpu.make_async_copy(
                        feat_hbm.at[pl.ds(pl.multiple_of(src * 128, 128), 128), pl.ds(128 * side, 128)],
                        ring.at[spot, k, pl.ds(128 * side, 128), :],
                        sem,
                    ).start()

            @pl.when((src >= blocks) & (src < blocks + border_blocks))
            def _():
                halves(border_hbm, src - blocks)

            @pl.when(src >= blocks + border_blocks)
            def _():
                pltpu.make_async_copy(
                    table_hbm.at[src - (blocks + border_blocks)], ring.at[spot, k], sem
                ).start()

    for group in range(RING - 1):
        @pl.when(group < groups)
        def _():
            load_weights(group).start()
            fetch(group)

    @pl.loop(RING - 1, groups)
    def _(group):
        load_weights(group).start()

    load_feat.start()
    total[...] = jnp.zeros_like(total)
    weight_total[...] = jnp.zeros_like(weight_total)
    self_high[...], self_low[...] = split(w_self_ref[...])
    neigh_high[...], neigh_low[...] = split(w_neigh_ref[...])

    @pl.loop(0, groups)
    def _(group):
        spot = lax.rem(group, RING)
        load_weights(group).wait()
        for k in range(GROUP):
            pltpu.make_async_copy(table_hbm.at[0], ring.at[spot, k], ring_sem.at[spot, k]).wait()

        @pl.when(group + (RING - 1) < groups)
        def _():
            fetch(group + (RING - 1))

        for k in range(GROUP):
            tile = group * GROUP + k
            dst = jnp.where(tile < count, dst_ref[tile], blocks)
            weight = weights[tile]
            source = jnp.concatenate([ring[spot, k, 0:128, :], ring[spot, k, 128:256, :]], axis=1)
            total[dst] += dot3(split(weight), split(source))
            weight_total[dst] += weight

    load_feat.wait()
    labels = labels_ref[...].astype(F32)
    target_columns = (2.0 * labels - 1.0).T
    lane = lax.broadcasted_iota(jnp.int32, target_columns.shape, 1)
    grad_self_ref[...] = jnp.zeros_like(grad_self_ref)
    grad_neigh_ref[...] = jnp.zeros_like(grad_neigh_ref)
    grad_small_ref[...] = jnp.zeros_like(grad_small_ref)
    per_chunk = CHUNK // 128

    @pl.loop(0, blocks // per_chunk)
    def _(chunk):
        rows = pl.ds(pl.multiple_of(chunk * CHUNK, CHUNK), CHUNK)
        own = feat[rows, :]
        at = pl.ds(chunk * per_chunk, per_chunk)
        summed = total[at].reshape(CHUNK, 256)
        weight_sum = jnp.sum(weight_total[at].reshape(CHUNK, 128), axis=1, keepdims=True)
        mean = (own + summed) * (1.0 / (1.0 + weight_sum))
        own_parts, mean_parts = split(own), split(mean)
        pre = (
            dot3(own_parts, (self_high[...], self_low[...]))
            + dot3(mean_parts, (neigh_high[...], neigh_low[...]))
            + bias_ref[...]
        )
        gate = jax.nn.sigmoid(pre)
        hidden = pre * gate
        score = jnp.sum(hidden * head_ref[...], axis=1, keepdims=True)
        target = jnp.concatenate(
            [
                jnp.sum(jnp.where(lane == chunk * per_chunk + i, target_columns, 0.0), axis=1, keepdims=True)
                for i in range(per_chunk)
            ],
            axis=0,
        )
        dscore = (score - target) * loss_scale
        dpre = dscore * head_ref[...] * (gate * (1.0 + pre * (1.0 - gate)))
        dpre_parts = split(dpre)
        by_rows = (((0,), (0,)), ((), ()))
        grad_self_ref[...] += dot3(own_parts, dpre_parts, by_rows)
        grad_neigh_ref[...] += dot3(mean_parts, dpre_parts, by_rows)
        grad_small_ref[0:1, :] += jnp.sum(dpre, axis=0, keepdims=True)
        grad_small_ref[1:2, :] += jnp.sum(hidden * dscore, axis=0, keepdims=True)

    for i, ref in enumerate((grad_self_ref, grad_neigh_ref)):
        for side in range(2):
            grad_ref[pl.ds(512 * i + 256 * side, 256), :] = ref[:, 128 * side:128 * side + 128]
    grad_ref[1024:1032, :] = jnp.zeros((8, 128), F32)
    for i in range(4):
        side = 128 * (i % 2)
        grad_ref[1024 + i:1025 + i, :] = grad_small_ref[i // 2:i // 2 + 1, side:side + 128]


def layer(loss_scale, dst, src, count, features, border, table, weights, w_self, w_neigh, bias, head, labels):
    tiles = weights.shape[0]
    vertices, width = features.shape
    blocks = vertices // 128
    dma = pltpu.SemaphoreType.DMA
    smem = pl.BlockSpec(memory_space=pltpu.SMEM)
    vmem = pl.BlockSpec(memory_space=pltpu.VMEM)
    hbm = pl.BlockSpec(memory_space=pl.ANY)
    return pl.pallas_call(
        functools.partial(layer_kernel, loss_scale),
        out_shape=jax.ShapeDtypeStruct((1032, 128), F32),
        in_specs=[smem] * 3 + [hbm] * 4 + [vmem] * 5,
        out_specs=vmem,
        scratch_shapes=[
            pltpu.VMEM((width, width), F32),
            pltpu.VMEM((width, width), F32),
            pltpu.VMEM((8, width), F32),
            pltpu.VMEM((vertices, width), F32),
            pltpu.VMEM((tiles, 128, 128), F32),
            pltpu.VMEM((RING, GROUP, 256, 128), F32),
            pltpu.VMEM((blocks + 1, 128, width), F32),
            pltpu.VMEM((blocks + 1, 128, 128), F32),
            pltpu.VMEM((width, width), BF16),
            pltpu.VMEM((width, width), BF16),
            pltpu.VMEM((width, width), BF16),
            pltpu.VMEM((width, width), BF16),
            dma,
            dma((tiles // GROUP,)),
            dma((RING, GROUP)),
        ],
        compiler_params=pltpu.CompilerParams(vmem_limit_bytes=48 * 2**20),
        name="layer",
    )(dst, src, count, features, border, table, weights, w_self, w_neigh, bias, head, labels)


def sum_kernel(
    grad_ref, self_ref, neigh_ref, bias_ref, head_ref,
    pair_in, plane_out, plane_in, plane_sum, z_out, z_in, whole, send_sem, recv_sem,
):
    place, core = my_place()
    q = place["y"] * 4 + place["x"]
    z = place["z"]
    sibling = device_at(place, 1 - core)

    def plane_peer(step):
        other = lax.rem(q + step, 16)
        return other, device_at({"x": lax.rem(other, 4), "y": lax.div(other, 4), "z": z}, core)

    def z_peer(step):
        other = lax.rem(z + step, 4)
        return other, device_at(shifted(place, "z", step), core)

    barrier = pltpu.get_barrier_semaphore()
    targets = [sibling] + [plane_peer(s)[1] for s in range(1, 16)] + [z_peer(s)[1] for s in range(1, 4)]
    for target in targets:
        pl.semaphore_signal(barrier, inc=1, device_id=target, device_id_type=MESH)
    pl.semaphore_wait(barrier, len(targets))

    def send(stage, src, dst, target):
        pltpu.make_async_remote_copy(
            src_ref=src, dst_ref=dst, send_sem=send_sem.at[stage], recv_sem=recv_sem.at[stage],
            device_id=target, device_id_type=MESH,
        ).start()

    def received(stage, ref):
        pltpu.make_async_copy(ref, ref, recv_sem.at[stage]).wait()

    half, other_half = core * 512, (1 - core) * 512
    send(0, grad_ref.at[pl.ds(other_half, 512)], pair_in.at[pl.ds(0, 512)], sibling)
    send(0, grad_ref.at[pl.ds(1024, 8)], pair_in.at[pl.ds(512, 8)], sibling)
    received(0, pair_in)

    small = grad_ref[1024:1032, :] + pair_in[512:520, :]
    for step in range(1, 17):
        other, target = plane_peer(step)
        row = pl.multiple_of(other * 32, 32)
        buffer = plane_in if step == 16 else plane_out
        buffer[other, 0:32, :] = grad_ref[pl.ds(half + row, 32), :] + pair_in[pl.ds(row, 32), :]
        buffer[other, 32:40, :] = small
        if step < 16:
            send(1, plane_out.at[other], plane_in.at[q], target)
    received(1, plane_in.at[pl.ds(0, 15)])
    value = plane_in[0]
    for i in range(1, 16):
        value = value + plane_in[i]
    plane_sum[...] = value

    for step in range(1, 5):
        other, target = z_peer(step)
        buffer = z_in if step == 4 else z_out
        buffer[other, 0:8, :] = plane_sum[pl.ds(pl.multiple_of(other * 8, 8), 8), :]
        buffer[other, 8:16, :] = plane_sum[32:40, :]
        if step < 4:
            send(2, z_out.at[other], z_in.at[z], target)
    received(2, z_in.at[pl.ds(0, 3)])
    value = (z_in[0] + z_in[1]) + (z_in[2] + z_in[3])

    lot = half + q * 32
    mine = pl.ds(pl.multiple_of(lot + z * 8, 8), 8)
    whole[mine, :] = value[0:8]
    for step in range(1, 4):
        send(3, whole.at[mine], whole.at[mine], z_peer(step)[1])
    received(3, whole.at[pl.ds(0, 24)])
    mine = pl.ds(pl.multiple_of(lot, 32), 32)
    for step in range(1, 16):
        send(4, whole.at[mine], whole.at[mine], plane_peer(step)[1])
    received(4, whole.at[pl.ds(0, 480)])
    mine = pl.ds(pl.multiple_of(half, 512), 512)
    send(5, whole.at[mine], whole.at[mine], sibling)
    for i in range(4):
        ref = (bias_ref, head_ref)[i // 2]
        ref[0:1, 128 * (i % 2):128 * (i % 2) + 128] = value[8 + i:9 + i]
    received(5, whole.at[pl.ds(0, 512)])
    for i, ref in enumerate((self_ref, neigh_ref)):
        for side in range(2):
            ref[:, 128 * side:128 * side + 128] = whole[pl.ds(512 * i + 256 * side, 256), :]

    sent = (
        pair_in, plane_in.at[pl.ds(0, 15)], z_in.at[pl.ds(0, 3)],
        whole.at[pl.ds(0, 24)], whole.at[pl.ds(0, 480)], whole.at[pl.ds(0, 512)],
    )
    for stage, ref in enumerate(sent):
        pltpu.make_async_copy(ref, ref, send_sem.at[stage]).wait()


def sum_grads(grads):
    vmem = pl.BlockSpec(memory_space=pltpu.VMEM)
    dma = pltpu.SemaphoreType.DMA
    return pl.pallas_call(
        sum_kernel,
        out_shape=(
            jax.ShapeDtypeStruct((256, 256), F32),
            jax.ShapeDtypeStruct((256, 256), F32),
            jax.ShapeDtypeStruct((1, 256), F32),
            jax.ShapeDtypeStruct((1, 256), F32),
        ),
        in_specs=[vmem],
        out_specs=(vmem,) * 4,
        scratch_shapes=[
            pltpu.VMEM((520, 128), F32),
            pltpu.VMEM((16, 40, 128), F32),
            pltpu.VMEM((16, 40, 128), F32),
            pltpu.VMEM((40, 128), F32),
            pltpu.VMEM((4, 16, 128), F32),
            pltpu.VMEM((4, 16, 128), F32),
            pltpu.VMEM((1024, 128), F32),
            dma((6,)),
            dma((6,)),
        ],
        compiler_params=pltpu.CompilerParams(collective_id=1, has_side_effects=True),
        name="sum_grads",
    )(grads)


def on_device(
    features,
    w_self,
    w_neigh,
    bias,
    w_head,
    tile_weights,
    tile_dst,
    tile_src,
    tile_count,
    hub_block,
    send_rows,
    send_count,
    labels,
):
    axes = ("vert", "row")
    width = features.shape[1]
    slots = send_rows.shape[2]
    blocks = features.shape[0] // 128
    peers = lax.axis_size(axes)

    hub = lax.dynamic_slice(features, (hub_block[0] * 128, 0), (128, width))
    hub = hub.reshape(128, 2, 128).transpose(1, 0, 2).reshape(256, 128)
    outgoing = features[send_rows[0]]
    alive = jnp.arange(slots, dtype=jnp.int32)[None, :] < send_count[0][:, None]
    outgoing = jnp.where(alive[:, :, None], outgoing, jnp.zeros_like(outgoing))
    incoming = lax.all_to_all(outgoing, axes, split_axis=0, concat_axis=0, tiled=True)
    border = incoming.reshape(-1, 128, width)
    table = gather_hubs(hub).reshape(peers, 256, 128)

    first_hub = blocks + border.shape[0]
    number = tile_src - first_hub
    y_low, core, x, y_high, z = number & 1, (number >> 1) & 1, (number >> 2) & 3, (number >> 4) & 1, number >> 5
    entry = core * 64 + z * 16 + (y_high * 2 + y_low) * 4 + x
    src = jnp.where(number < 0, tile_src, entry + first_hub)

    loss_scale = 1.0 / math.sqrt(features.shape[0] * peers)
    grads = layer(
        loss_scale, tile_dst, src, tile_count, features, border, table, tile_weights,
        w_self, w_neigh, bias.reshape(1, width), w_head.reshape(1, width), labels.reshape(blocks, 128),
    )
    grad_self, grad_neigh, grad_bias, grad_head = sum_grads(grads)
    return (grad_self, grad_neigh, grad_bias.reshape(width), grad_head.reshape(width))


def solution(mesh):
    in_specs = (
        P(("vert", "row"), None),
        P(),
        P(),
        P(),
        P(),
        P(("vert", "row"), None, None),
        P(("vert", "row")),
        P(("vert", "row")),
        P(("vert", "row")),
        P(("vert", "row")),
        P(("vert", "row"), None, None),
        P(("vert", "row"), None),
        P(("vert", "row")),
    )
    out_specs = (P(), P(), P(), P())
    return jax.shard_map(
        on_device, mesh=mesh, in_specs=in_specs, out_specs=out_specs, check_vma=False
    )
```

```python
import functools
import math

import jax
import jax.numpy as jnp
from jax import lax
from jax.experimental import pallas as pl
from jax.experimental.pallas import tpu as pltpu
from jax.sharding import PartitionSpec as P

MESH = pl.DeviceIdType.MESH
BF16 = jnp.bfloat16
F32 = jnp.float32

PART_START = (0, 88, 176)
PART_ROWS = (88, 88, 80)
PART_HALF = (48, 40, 40)
PART_AXES = ("xyz", "yzx", "zxy")
OFFSETS = (0, 3, 1, 2)


def my_place():
    vert = lax.axis_index("vert")
    row = lax.axis_index("row")
    core = lax.rem(vert, 2)
    x = lax.rem(lax.div(vert, 2), 4)
    y = lax.rem(lax.div(vert, 8), 2) * 2 + row
    z = lax.div(vert, 16)
    return {"x": x, "y": y, "z": z}, core


def device_at(place, core):
    x, y, z = place["x"], place["y"], place["z"]
    vert = ((z * 2 + lax.div(y, 2)) * 4 + x) * 2 + core
    return (vert, lax.rem(y, 2))


def shifted(place, axis, step):
    moved = dict(place)
    moved[axis] = lax.rem(place[axis] + step, 4)
    return moved


def split(value):
    high = value.astype(BF16)
    low = (value - high.astype(F32)).astype(BF16)
    return high, low


def dot(a, b, dims=(((1,), (0,)), ((), ()))):
    return lax.dot_general(a, b, dims, preferred_element_type=F32)


CHUNK = 256
TILE_CHUNK = 8
TILE_SLOTS = 4


def gather_kernel(
    hub_block_ref, rows_ref, count_ref, feat_hbm, weights_hbm, w_self_ref, bias_ref,
    table_ref, local_ref, split_ref, sums_ref,
    hub, self_k, ring, out_core, by_core, by_x, by_y, by_z,
    own_sem, feat_sem, ring_sem, recv1, recv2, recv3, send1, send2, send3, pair_send, pair_recv,
    border_send, border_recv, border_own,
):
    place, core = my_place()
    x, y, z = place["x"], place["y"], place["z"]
    near = {}
    for axis in "xyz":
        for step in (1, 2, 3):
            near[axis, step] = device_at(shifted(place, axis, step), core)
    sibling = device_at(place, 1 - core)

    loads = []
    for side in range(2):
        load = pltpu.make_async_copy(
            feat_hbm.at[:, :, pl.ds(128 * side, 128)],
            local_ref.at[pl.ds(0, 32), pl.ds(128 * side, 128), :],
            feat_sem.at[side],
        )
        load.start()
        loads.append(load)

    def load_tiles(i):
        spot = lax.rem(i, TILE_SLOTS)
        return pltpu.make_async_copy(
            weights_hbm.at[pl.ds(i * TILE_CHUNK, TILE_CHUNK)], ring.at[spot], ring_sem.at[spot]
        )

    for i in range(TILE_SLOTS):
        load_tiles(i).start()

    barrier = pltpu.get_barrier_semaphore()
    targets = list(near.values()) + [sibling]
    for target in targets:
        pl.semaphore_signal(barrier, inc=1, device_id=target, device_id_type=MESH)

    for load in loads:
        load.wait()
    hub[...] = local_ref[hub_block_ref[0]]
    own = pltpu.make_async_copy(hub, table_ref.at[core, z, y, x], own_sem)
    own.start()
    pl.semaphore_wait(barrier, len(targets))

    def slot(part, where, half=None):
        start, rows = PART_START[part], PART_ROWS[part]
        if half == 0:
            rows = PART_HALF[part]
        elif half == 1:
            start, rows = start + PART_HALF[part], rows - PART_HALF[part]
        at = []
        for axis in "zyx":
            offset = where.get(axis, 0)
            at.append(pl.ds(0, 4) if offset == "all" else lax.rem(place[axis] + offset, 4))
        return table_ref.at[(core, *at, pl.ds(start, rows), slice(None))]

    def remote(src, dst, send_sem, recv_sem, target):
        return pltpu.make_async_remote_copy(
            src_ref=src, dst_ref=dst, send_sem=send_sem, recv_sem=recv_sem,
            device_id=target, device_id_type=MESH,
        )

    def send_both(part, where, axis, send_sem, recv):
        dst = slot(part, where)
        src = dst if where else hub.at[pl.ds(PART_START[part], PART_ROWS[part])]
        remote(src, dst, send_sem, recv.at[0], near[axis, 1]).start()
        remote(src, dst, send_sem, recv.at[1], near[axis, 3]).start()

    def arrived(part, where, axis, sem, half=None):
        ref = slot(part, where, half)
        remote(ref, ref, sem, sem, near[axis, 1]).wait_recv()

    def pass_on(part, where, axis, send_sem, recv, half):
        ref = slot(part, where, half)
        remote(ref, ref, send_sem, recv.at[2 + half], near[axis, 1 if half == 0 else 3]).start()

    def to_sibling(part, where):
        ref = slot(part, where)
        remote(ref, ref, pair_send, pair_recv, sibling).start()

    parts = range(3)

    slot_row = lax.broadcasted_iota(jnp.int32, (8, 128), 0)

    def pick_rows(to_core, store):
        @pl.loop(0, 64)
        def _(i):
            y_low = lax.rem(i, 2)
            to_x = lax.rem(lax.div(i, 2), 4)
            y_high = lax.rem(lax.div(i, 8), 2)
            to_z = lax.div(i, 16)
            number = ((to_z * 2 + y_high) * 4 + to_x) * 4 + to_core * 2 + y_low
            alive = slot_row < count_ref[0, number]
            refs = [store(to_z, y_high, side, to_x, y_low) for side in range(2)]
            for k in range(8):
                row = rows_ref[0, number, k]
                block = lax.shift_right_logical(row, 7)
                inside = row & 127
                for side in range(2):
                    refs[side][pl.ds(k, 1), :] = local_ref[block, pl.ds(inside + 128 * side, 1), :]
            for side in range(2):
                refs[side][...] = jnp.where(alive, refs[side][...], 0.0)

    def border_go(stage, src, dst, target):
        remote(src, dst, border_send.at[stage], border_recv.at[stage], target).start()

    def border_wait(stage, ref):
        pltpu.make_async_copy(ref, ref, border_recv.at[stage]).wait()

    def border_core():
        border_go(0, out_core, by_core.at[:, :, :, :, core], sibling)

    def border_x():
        border_wait(0, out_core)
        keep = pltpu.make_async_copy(by_core.at[:, :, :, x], by_x.at[:, :, :, x], border_own.at[0])
        keep.start()
        for step in (1, 2, 3):
            border_go(1, by_core.at[:, :, :, lax.rem(x + step, 4)], by_x.at[:, :, :, x], near["x", step])
        keep.wait()

    def border_y():
        border_wait(1, by_x.at[pl.ds(0, 3)])
        yh, yl = lax.div(y, 2), lax.rem(y, 2)
        keep = pltpu.make_async_copy(
            by_x.at[:, yh, :, :, :, yl], by_y.at[:, yh, :, :, :, yl], border_own.at[1]
        )
        keep.start()
        for step in (1, 2, 3):
            to = lax.rem(y + step, 4)
            border_go(
                2, by_x.at[:, lax.div(to, 2), :, :, :, lax.rem(to, 2)],
                by_y.at[:, yh, :, :, :, yl], near["y", step],
            )
        keep.wait()

    def border_z():
        border_wait(2, by_y.at[pl.ds(0, 3)])
        keep = pltpu.make_async_copy(by_y.at[z], by_z.at[z], border_own.at[2])
        keep.start()
        for step in (1, 2, 3):
            border_go(3, by_y.at[lax.rem(z + step, 4)], by_z.at[z], near["z", step])
        keep.wait()

    def border_end():
        border_wait(3, by_z.at[pl.ds(0, 3)])
        for i in range(8):
            local_ref[32 + i] = by_z[i // 2, i % 2].reshape(256, 128)

    def pre_chunks(start, stop):
        @pl.loop(start, stop)
        def _(chunk):
            own = []
            for i in range(CHUNK // 128):
                block = local_ref[chunk * (CHUNK // 128) + i]
                own.append(jnp.concatenate([block[0:128], block[128:256]], axis=1))
            high, low = split(jnp.concatenate(own, axis=0))
            value = dot(jnp.concatenate([high, low, high], axis=1), self_k[...]) + bias_ref[...]
            for i in range(CHUNK // 128):
                for side in range(2):
                    local_ref[40 + chunk * (CHUNK // 128) + i, 128 * side:128 * side + 128, :] = value[
                        128 * i:128 * i + 128, 128 * side:128 * side + 128
                    ]

    lane = lax.broadcasted_iota(jnp.int32, (128, 128), 1)

    def tile_chunks(start, stop):
        @pl.loop(start, stop)
        def _(i):
            load_tiles(i).wait()
            spot = lax.rem(i, TILE_SLOTS)
            sums = sums_ref[...]
            for k in range(TILE_CHUNK):
                tile = i * TILE_CHUNK + k
                weight = ring[spot, k]
                high, low = split(weight)
                split_ref[tile, :, 0:128] = high
                split_ref[tile, :, 128:256] = low
                sums = jnp.where(lane == tile, jnp.sum(weight, axis=1, keepdims=True), sums)
            sums_ref[...] = sums

            @pl.when(i + TILE_SLOTS < 128 // TILE_CHUNK)
            def _():
                load_tiles(i + TILE_SLOTS).start()

    for p in parts:
        first, second, _ = PART_AXES[p]
        send_both(p, {}, first, send1.at[p], recv1.at[p])
        send_both(p, {}, second, send2.at[p], recv2.at[p, 0])

    sums_ref[...] = jnp.zeros_like(sums_ref)
    pick_rows(1 - core, lambda tz, yh, side, tx, yl: out_core.at[tz, yh, side, tx, yl])
    border_core()

    own.wait()
    for side, offset in ((0, 3), (1, 1)):
        unit = OFFSETS.index(offset)
        for p in parts:
            first, second, _ = PART_AXES[p]
            where = {first: offset}
            arrived(p, where, first, recv1.at[p, side])
            pass_on(p, where, first, send1.at[p], recv1.at[p], side)
            send_both(p, where, second, send2.at[p], recv2.at[p, unit])
    pick_rows(core, lambda tz, yh, side, tx, yl: by_core.at[tz, yh, side, tx, core, yl])
    border_x()
    for p in parts:
        first, second, third = PART_AXES[p]
        where = {first: 2}
        arrived(p, where, first, recv1.at[p, 2], 0)
        arrived(p, where, first, recv1.at[p, 3], 1)
        send_both(p, where, second, send2.at[p], recv2.at[p, 3])
        line = {first: "all"}
        send_both(p, line, third, send3.at[p], recv3.at[p, 0])
        to_sibling(p, line)
    self_high, self_low = split(w_self_ref[...])
    self_k[0:256, :] = self_high
    self_k[256:512, :] = self_high
    self_k[512:768, :] = self_low

    for unit in range(4):
        if unit == 2:
            border_y()
        for side, offset in ((0, 3), (1, 1)):
            for p in parts:
                first, second, _ = PART_AXES[p]
                where = {first: OFFSETS[unit], second: offset}
                arrived(p, where, second, recv2.at[p, unit, side])
                pass_on(p, where, second, send2.at[p], recv2.at[p, unit], side)
    for side, offset in ((0, 3), (1, 1)):
        for p in parts:
            first, second, third = PART_AXES[p]
            line = {first: "all", second: offset}
            send_both(p, line, third, send3.at[p], recv3.at[p, 1 + side])
            to_sibling(p, line)
    border_z()
    for p in parts:
        first, second, third = PART_AXES[p]
        for unit in range(4):
            where = {first: OFFSETS[unit], second: 2}
            arrived(p, where, second, recv2.at[p, unit, 2], 0)
            arrived(p, where, second, recv2.at[p, unit, 3], 1)
        line = {first: "all", second: 2}
        send_both(p, line, third, send3.at[p], recv3.at[p, 3])
        to_sibling(p, line)

    for unit in range(4):
        pre_chunks(4 * unit, 4 * unit + 4)
        for side, offset in ((0, 3), (1, 1)):
            for p in parts:
                first, second, third = PART_AXES[p]
                line = {first: "all", second: OFFSETS[unit], third: offset}
                arrived(p, line, third, recv3.at[p, unit, side])
                pass_on(p, line, third, send3.at[p], recv3.at[p, unit], side)
                to_sibling(p, line)
        if unit < 2:
            tile_chunks(8 * unit, 8 * unit + 8)
        if unit == 2:
            border_end()
    for unit in range(4):
        for p in parts:
            first, second, third = PART_AXES[p]
            line = {first: "all", second: OFFSETS[unit], third: 2}
            arrived(p, line, third, recv3.at[p, unit, 2], 0)
            arrived(p, line, third, recv3.at[p, unit, 3], 1)
            to_sibling(p, line)

    for p in parts:
        rows = pl.ds(PART_START[p], PART_ROWS[p])
        for sem, ref in (
            (send1.at[p], table_ref.at[core, 0, 0, pl.ds(0, 3), rows, :]),
            (send2.at[p], table_ref.at[core, 0, pl.ds(0, 3), pl.ds(0, 4), rows, :]),
            (send3.at[p], table_ref.at[core, pl.ds(0, 3), pl.ds(0, 4), pl.ds(0, 4), rows, :]),
        ):
            pltpu.make_async_copy(ref, ref, sem).wait()
    for stage, ref in enumerate((out_core, by_x.at[pl.ds(0, 3)], by_y.at[pl.ds(0, 3)], by_z.at[pl.ds(0, 3)])):
        pltpu.make_async_copy(ref, ref, border_send.at[stage]).wait()
    mine, theirs = table_ref.at[core], table_ref.at[1 - core]
    pltpu.make_async_copy(mine, mine, pair_send).wait()
    pltpu.make_async_copy(theirs, theirs, pair_recv).wait()


def gather(hub_block, send_rows, send_count, features, weights, w_self, bias):
    dma = pltpu.SemaphoreType.DMA
    smem = pl.BlockSpec(memory_space=pltpu.SMEM)
    vmem = pl.BlockSpec(memory_space=pltpu.VMEM)
    hbm = pl.BlockSpec(memory_space=pl.ANY)
    border = pltpu.VMEM((4, 2, 2, 4, 2, 2, 8, 128), F32)
    return pl.pallas_call(
        gather_kernel,
        out_shape=(
            jax.ShapeDtypeStruct((2, 4, 4, 4, 256, 128), F32),
            pltpu.VMEM((72, 256, 128), F32),
            pltpu.VMEM((128, 128, 256), BF16),
            pltpu.VMEM((128, 128), F32),
        ),
        in_specs=[smem] * 3 + [hbm] * 2 + [vmem] * 2,
        out_specs=(hbm,) + (vmem,) * 3,
        scratch_shapes=[
            pltpu.VMEM((256, 128), F32),
            pltpu.VMEM((768, 256), BF16),
            pltpu.VMEM((TILE_SLOTS, TILE_CHUNK, 128, 128), F32),
            pltpu.VMEM((4, 2, 2, 4, 2, 8, 128), F32),
            border, border, border, border,
            dma, dma((2,)), dma((TILE_SLOTS,)), dma((3, 4)), dma((3, 4, 4)), dma((3, 4, 4)),
            dma((3,)), dma((3,)), dma((3,)), dma, dma,
            dma((4,)), dma((4,)), dma((3,)),
        ],
        compiler_params=pltpu.CompilerParams(
            collective_id=0, has_side_effects=True, vmem_limit_bytes=34 * 2**20
        ),
        name="gather",
    )(hub_block, send_rows, send_count, features, weights, w_self, bias)


GROUP = 4


def layer_kernel(
    loss_scale, dst_ref, src_ref, count_ref,
    table_hbm, local_ref, split_ref, sums_ref, dst_row_ref, w_neigh_ref, head_ref, labels_ref,
    grad_ref,
    table_ref, neigh_k, total, grad_self, grad_neigh, grad_small, near_tiles, hub_tiles, table_sem,
):
    tiles = split_ref.shape[0]
    blocks = total.shape[0] - 1
    first_hub = blocks + 8
    count = count_ref[0]

    table_loads = [
        pltpu.make_async_copy(table_hbm.at[i // 4, i % 4], table_ref.at[i // 4, i % 4], table_sem.at[i])
        for i in range(8)
    ]
    for load in table_loads:
        load.start()
    total[...] = jnp.zeros_like(total)
    neigh_high, neigh_low = split(w_neigh_ref[...])
    neigh_k[0:256, :] = neigh_high
    neigh_k[256:512, :] = neigh_high
    neigh_k[512:768, :] = neigh_low

    def sort_tile(tile, ends):
        near_end, hub_end = ends
        near_tiles[near_end] = tile
        hub_tiles[hub_end] = tile
        near = jnp.where(src_ref[tile] < first_hub, 1, 0)
        return near_end + near, hub_end + (1 - near)

    near_count, hub_count = lax.fori_loop(0, count, sort_tile, (0, 0))

    def wide(block):
        return jnp.concatenate([block[0:128], block[128:256]], axis=1)

    def near_source(src):
        return wide(local_ref[src])

    def hub_source(src):
        number = src - first_hub
        return wide(table_ref[
            lax.shift_right_logical(number, 1) & 1,
            lax.shift_right_logical(number, 5),
            (lax.shift_right_logical(number, 4) & 1) * 2 + (number & 1),
            lax.shift_right_logical(number, 2) & 3,
        ])

    for listed, amount, source in ((near_tiles, near_count, near_source), (hub_tiles, hub_count, hub_source)):
        if listed is hub_tiles:
            for load in table_loads:
                load.wait()

        @pl.loop(0, lax.div(amount + (GROUP - 1), GROUP))
        def _(group):
            products, targets = [], []
            for k in range(GROUP):
                at = group * GROUP + k
                tile = listed[jnp.minimum(at, amount - 1)]
                targets.append(jnp.where(at < amount, dst_ref[tile], blocks))
                weight = split_ref[tile]
                high, low = split(source(src_ref[tile]))
                products.append(
                    dot(
                        jnp.concatenate([weight, weight[:, 0:128]], axis=1),
                        jnp.concatenate([high, high, low], axis=0),
                    )
                )
            for k in range(GROUP):
                total[targets[k]] += products[k]

    by_lanes = (((1,), (1,)), ((), ()))
    tile_lane = lax.broadcasted_iota(jnp.int32, (blocks, tiles), 1)
    block_row = lax.broadcasted_iota(jnp.int32, (blocks, tiles), 0)
    chosen = (dst_row_ref[...] == block_row) & (tile_lane < count)
    chosen = jnp.where(chosen, 1.0, 0.0).astype(BF16)
    sums_high, sums_low = split(sums_ref[...])
    sums_rest = (sums_ref[...] - sums_high.astype(F32) - sums_low.astype(F32)).astype(BF16)
    scales = 1.0 / (
        1.0 + (dot(sums_high, chosen, by_lanes) + dot(sums_low, chosen, by_lanes) + dot(sums_rest, chosen, by_lanes))
    )
    target_columns = (2.0 * labels_ref[...].astype(F32) - 1.0).T
    lane = lax.broadcasted_iota(jnp.int32, target_columns.shape, 1)

    grad_self[...] = jnp.zeros_like(grad_self)
    grad_neigh[...] = jnp.zeros_like(grad_neigh)
    grad_small[...] = jnp.zeros_like(grad_small)
    per_chunk = CHUNK // 128

    @pl.loop(0, blocks // per_chunk)
    def _(chunk):
        rows = pl.ds(pl.multiple_of(chunk * CHUNK, CHUNK), CHUNK)
        own, mean, target, pre = [], [], [], []
        for i in range(per_chunk):
            b = chunk * per_chunk + i
            block = wide(local_ref[b])
            scale = jnp.sum(jnp.where(lane == b, scales, 0.0), axis=1, keepdims=True)
            own.append(block)
            pre.append(wide(local_ref[first_hub + b]))
            mean.append((block + total[b]) * scale)
            target.append(jnp.sum(jnp.where(lane == b, target_columns, 0.0), axis=1, keepdims=True))
        own, mean, target, pre = (jnp.concatenate(v, axis=0) for v in (own, mean, target, pre))
        own_high, own_low = split(own)
        mean_high, mean_low = split(mean)
        pre = pre + dot(jnp.concatenate([mean_high, mean_low, mean_high], axis=1), neigh_k[...])
        gate = jax.nn.sigmoid(pre)
        hidden = pre * gate
        score = jnp.sum(hidden * head_ref[...], axis=1, keepdims=True)
        dscore = (score - target) * loss_scale
        dpre = dscore * head_ref[...] * (gate * (1.0 + pre * (1.0 - gate)))
        d_high, d_low = split(dpre)
        by_rows = (((0,), (0,)), ((), ()))
        right = jnp.concatenate([d_high, d_high, d_low], axis=0)
        grad_self[...] += dot(jnp.concatenate([own_high, own_low, own_high], axis=0), right, by_rows)
        grad_neigh[...] += dot(jnp.concatenate([mean_high, mean_low, mean_high], axis=0), right, by_rows)
        grad_small[0:1, :] += jnp.sum(dpre, axis=0, keepdims=True)
        grad_small[1:2, :] += jnp.sum(hidden * dscore, axis=0, keepdims=True)

    for i, ref in enumerate((grad_self, grad_neigh)):
        for side in range(2):
            grad_ref[pl.ds(512 * i + 256 * side, 256), :] = ref[:, 128 * side:128 * side + 128]
    grad_ref[1024:1032, :] = jnp.zeros((8, 128), F32)
    for i in range(4):
        side = 128 * (i % 2)
        grad_ref[1024 + i:1025 + i, :] = grad_small[i // 2:i // 2 + 1, side:side + 128]


def layer(loss_scale, dst, src, count, table, local, weights, sums, w_neigh, head, labels):
    smem = pl.BlockSpec(memory_space=pltpu.SMEM)
    vmem = pl.BlockSpec(memory_space=pltpu.VMEM)
    width = w_neigh.shape[0]
    blocks = labels.shape[0]
    return pl.pallas_call(
        functools.partial(layer_kernel, loss_scale),
        out_shape=pltpu.VMEM((1032, 128), F32),
        in_specs=[smem] * 3 + [pl.BlockSpec(memory_space=pl.ANY)] + [vmem] * 7,
        out_specs=vmem,
        scratch_shapes=[
            pltpu.VMEM(table.shape, F32),
            pltpu.VMEM((3 * width, width), BF16),
            pltpu.VMEM((blocks + 1, 128, width), F32),
            pltpu.VMEM((width, width), F32),
            pltpu.VMEM((width, width), F32),
            pltpu.VMEM((8, width), F32),
            pltpu.SMEM((dst.shape[0] + 1,), jnp.int32),
            pltpu.SMEM((dst.shape[0] + 1,), jnp.int32),
            pltpu.SemaphoreType.DMA((8,)),
        ],
        compiler_params=pltpu.CompilerParams(vmem_limit_bytes=30 * 2**20),
        name="layer",
    )(dst, src, count, table, local, weights, sums, dst.reshape(1, -1), w_neigh, head, labels)


def sum_kernel(
    grad_ref, whole,
    pair_in, plane_out, plane_in, plane_sum, z_out, z_in, send_sem, recv_sem,
):
    place, core = my_place()
    q = place["y"] * 4 + place["x"]
    z = place["z"]
    sibling = device_at(place, 1 - core)

    def plane_peer(step):
        other = lax.rem(q + step, 16)
        return other, device_at({"x": lax.rem(other, 4), "y": lax.div(other, 4), "z": z}, core)

    def z_peer(step):
        other = lax.rem(z + step, 4)
        return other, device_at(shifted(place, "z", step), core)

    barrier = pltpu.get_barrier_semaphore()
    targets = [sibling] + [plane_peer(s)[1] for s in range(1, 16)] + [z_peer(s)[1] for s in range(1, 4)]
    for target in targets:
        pl.semaphore_signal(barrier, inc=1, device_id=target, device_id_type=MESH)
    pl.semaphore_wait(barrier, len(targets))

    def send(stage, src, dst, target):
        pltpu.make_async_remote_copy(
            src_ref=src, dst_ref=dst, send_sem=send_sem.at[stage], recv_sem=recv_sem.at[stage],
            device_id=target, device_id_type=MESH,
        ).start()

    def received(stage, ref):
        pltpu.make_async_copy(ref, ref, recv_sem.at[stage]).wait()

    half, other_half = core * 512, (1 - core) * 512
    send(0, grad_ref.at[pl.ds(other_half, 512)], pair_in.at[pl.ds(0, 512)], sibling)
    send(0, grad_ref.at[pl.ds(1024, 8)], pair_in.at[pl.ds(512, 8)], sibling)
    received(0, pair_in)

    small = grad_ref[1024:1032, :] + pair_in[512:520, :]
    for step in range(1, 17):
        other, target = plane_peer(step)
        row = pl.multiple_of(other * 32, 32)
        buffer = plane_in if step == 16 else plane_out
        buffer[other, 0:32, :] = grad_ref[pl.ds(half + row, 32), :] + pair_in[pl.ds(row, 32), :]
        buffer[other, 32:40, :] = small
        if step < 16:
            send(1, plane_out.at[other], plane_in.at[q], target)
    received(1, plane_in.at[pl.ds(0, 15)])
    value = plane_in[0]
    for i in range(1, 16):
        value = value + plane_in[i]
    plane_sum[...] = value

    for step in range(1, 5):
        other, target = z_peer(step)
        buffer = z_in if step == 4 else z_out
        buffer[other, 0:8, :] = plane_sum[pl.ds(pl.multiple_of(other * 8, 8), 8), :]
        buffer[other, 8:16, :] = plane_sum[32:40, :]
        if step < 4:
            send(2, z_out.at[other], z_in.at[z], target)
    received(2, z_in.at[pl.ds(0, 3)])
    value = (z_in[0] + z_in[1]) + (z_in[2] + z_in[3])

    lot = half + q * 32
    mine = pl.ds(pl.multiple_of(lot + z * 8, 8), 8)
    whole[mine, :] = value[0:8]
    for step in range(1, 4):
        send(3, whole.at[mine], whole.at[mine], z_peer(step)[1])
    received(3, whole.at[pl.ds(0, 24)])
    mine = pl.ds(pl.multiple_of(lot, 32), 32)
    for step in range(1, 16):
        send(4, whole.at[mine], whole.at[mine], plane_peer(step)[1])
    received(4, whole.at[pl.ds(0, 480)])
    mine = pl.ds(pl.multiple_of(half, 512), 512)
    send(5, whole.at[mine], whole.at[mine], sibling)
    whole[1024:1032, :] = value[8:16]
    received(5, whole.at[pl.ds(0, 512)])

    sent = (
        pair_in, plane_in.at[pl.ds(0, 15)], z_in.at[pl.ds(0, 3)],
        whole.at[pl.ds(0, 24)], whole.at[pl.ds(0, 480)], whole.at[pl.ds(0, 512)],
    )
    for stage, ref in enumerate(sent):
        pltpu.make_async_copy(ref, ref, send_sem.at[stage]).wait()


def sum_grads(grads):
    vmem = pl.BlockSpec(memory_space=pltpu.VMEM)
    dma = pltpu.SemaphoreType.DMA
    return pl.pallas_call(
        sum_kernel,
        out_shape=pltpu.VMEM((1032, 128), F32),
        in_specs=[vmem],
        out_specs=vmem,
        scratch_shapes=[
            pltpu.VMEM((520, 128), F32),
            pltpu.VMEM((16, 40, 128), F32),
            pltpu.VMEM((16, 40, 128), F32),
            pltpu.VMEM((40, 128), F32),
            pltpu.VMEM((4, 16, 128), F32),
            pltpu.VMEM((4, 16, 128), F32),
            dma((6,)),
            dma((6,)),
        ],
        compiler_params=pltpu.CompilerParams(
            collective_id=1, has_side_effects=True, vmem_limit_bytes=8 * 2**20
        ),
        name="sum_grads",
    )(grads)


def unpack_kernel(whole, self_ref, neigh_ref, bias_ref, head_ref):
    for i, ref in enumerate((self_ref, neigh_ref)):
        for side in range(2):
            ref[:, 128 * side:128 * side + 128] = whole[pl.ds(512 * i + 256 * side, 256), :]
    for i in range(4):
        ref = (bias_ref, head_ref)[i // 2]
        ref[128 * (i % 2):128 * (i % 2) + 128] = whole[1024 + i, :]


def unpack(whole):
    vmem = pl.BlockSpec(memory_space=pltpu.VMEM)
    return pl.pallas_call(
        unpack_kernel,
        out_shape=(
            jax.ShapeDtypeStruct((256, 256), F32),
            jax.ShapeDtypeStruct((256, 256), F32),
            jax.ShapeDtypeStruct((256,), F32),
            jax.ShapeDtypeStruct((256,), F32),
        ),
        in_specs=[vmem],
        out_specs=(vmem,) * 4,
        compiler_params=pltpu.CompilerParams(vmem_limit_bytes=4 * 2**20),
        name="unpack",
    )(whole)


def on_device(
    features,
    w_self,
    w_neigh,
    bias,
    w_head,
    tile_weights,
    tile_dst,
    tile_src,
    tile_count,
    hub_block,
    send_rows,
    send_count,
    labels,
):
    width = features.shape[1]
    blocks = features.shape[0] // 128
    vertex_total = features.shape[0] * lax.axis_size(("vert", "row"))
    loss_scale = 1.0 / math.sqrt(vertex_total)
    table, local, weights, sums = gather(
        hub_block, send_rows, send_count, features.reshape(blocks, 128, width), tile_weights,
        w_self, bias.reshape(1, width),
    )
    grads = layer(
        loss_scale, tile_dst, tile_src, tile_count, table, local, weights, sums,
        w_neigh, w_head.reshape(1, width), labels.reshape(blocks, 128),
    )
    return unpack(sum_grads(grads))


def solution(mesh):
    in_specs = (
        P(("vert", "row"), None),
        P(),
        P(),
        P(),
        P(),
        P(("vert", "row"), None, None),
        P(("vert", "row")),
        P(("vert", "row")),
        P(("vert", "row")),
        P(("vert", "row")),
        P(("vert", "row"), None, None),
        P(("vert", "row"), None),
        P(("vert", "row")),
    )
    out_specs = (P(), P(), P(), P())
    return jax.shard_map(
        on_device, mesh=mesh, in_specs=in_specs, out_specs=out_specs, check_vma=False
    )
```

```python
import functools
import math

import jax
import jax.numpy as jnp
from jax import lax
from jax.experimental import pallas as pl
from jax.experimental.pallas import tpu as pltpu
from jax.sharding import PartitionSpec as P

MESH = pl.DeviceIdType.MESH
BF16 = jnp.bfloat16
F32 = jnp.float32

PART_START = (0, 88, 176)
PART_ROWS = (88, 88, 80)
PART_HALF = (48, 40, 40)
PART_AXES = ("xyz", "yzx", "zxy")
OFFSETS = (0, 3, 1, 2)


def my_place():
    vert = lax.axis_index("vert")
    row = lax.axis_index("row")
    core = lax.rem(vert, 2)
    x = lax.rem(lax.div(vert, 2), 4)
    y = lax.rem(lax.div(vert, 8), 2) * 2 + row
    z = lax.div(vert, 16)
    return {"x": x, "y": y, "z": z}, core


def device_at(place, core):
    x, y, z = place["x"], place["y"], place["z"]
    vert = ((z * 2 + lax.div(y, 2)) * 4 + x) * 2 + core
    return (vert, lax.rem(y, 2))


def shifted(place, axis, step):
    moved = dict(place)
    moved[axis] = lax.rem(place[axis] + step, 4)
    return moved


def split(value):
    high = value.astype(BF16)
    low = (value - high.astype(F32)).astype(BF16)
    return high, low


def dot(a, b, dims=(((1,), (0,)), ((), ()))):
    return lax.dot_general(a, b, dims, preferred_element_type=F32)


CHUNK = 256
TILE_CHUNK = 8
TILE_SLOTS = 4


def gather_kernel(
    hub_block_ref, rows_ref, count_ref, feat_hbm, weights_hbm, w_self_ref, bias_ref,
    table_ref, local_ref, split_ref, sums_ref,
    hub, self_k, ring, outbox, inbox,
    own_sem, feat_sem, ring_sem, recv1, recv2, recv3, send1, send2, send3, pair_send, pair_recv,
    border_send, border_recv,
):
    place, core = my_place()
    x, y, z = place["x"], place["y"], place["z"]
    near = {}
    for axis in "xyz":
        for step in (1, 3):
            near[axis, step] = device_at(shifted(place, axis, step), core)
    sibling = device_at(place, 1 - core)
    me = lax.axis_index("vert") * 2 + lax.axis_index("row")

    def other(step):
        number = lax.rem(me + step, 128)
        return number, (lax.div(number, 2), lax.rem(number, 2))

    loads = []
    for side in range(2):
        load = pltpu.make_async_copy(
            feat_hbm.at[:, :, pl.ds(128 * side, 128)],
            local_ref.at[pl.ds(0, 32), pl.ds(128 * side, 128), :],
            feat_sem.at[side],
        )
        load.start()
        loads.append(load)

    def load_tiles(i):
        spot = lax.rem(i, TILE_SLOTS)
        return pltpu.make_async_copy(
            weights_hbm.at[pl.ds(i * TILE_CHUNK, TILE_CHUNK)], ring.at[spot], ring_sem.at[spot]
        )

    for i in range(TILE_SLOTS):
        load_tiles(i).start()

    barrier = pltpu.get_barrier_semaphore()

    @pl.loop(1, 128)
    def _(step):
        pl.semaphore_signal(barrier, inc=1, device_id=other(step)[1], device_id_type=MESH)


    for load in loads:
        load.wait()
    hub[...] = local_ref[hub_block_ref[0]]
    own = pltpu.make_async_copy(hub, table_ref.at[core, z, y, x], own_sem)
    own.start()
    pl.semaphore_wait(barrier, 127)

    def slot(part, where, half=None):
        start, rows = PART_START[part], PART_ROWS[part]
        if half == 0:
            rows = PART_HALF[part]
        elif half == 1:
            start, rows = start + PART_HALF[part], rows - PART_HALF[part]
        at = []
        for axis in "zyx":
            offset = where.get(axis, 0)
            at.append(pl.ds(0, 4) if offset == "all" else lax.rem(place[axis] + offset, 4))
        return table_ref.at[(core, *at, pl.ds(start, rows), slice(None))]

    def remote(src, dst, send_sem, recv_sem, target):
        return pltpu.make_async_remote_copy(
            src_ref=src, dst_ref=dst, send_sem=send_sem, recv_sem=recv_sem,
            device_id=target, device_id_type=MESH,
        )

    def send_both(part, where, axis, send_sem, recv):
        dst = slot(part, where)
        src = dst if where else hub.at[pl.ds(PART_START[part], PART_ROWS[part])]
        remote(src, dst, send_sem, recv.at[0], near[axis, 1]).start()
        remote(src, dst, send_sem, recv.at[1], near[axis, 3]).start()

    def arrived(part, where, axis, sem, half=None):
        ref = slot(part, where, half)
        remote(ref, ref, sem, sem, near[axis, 1]).wait_recv()

    def pass_on(part, where, axis, send_sem, recv, half):
        ref = slot(part, where, half)
        remote(ref, ref, send_sem, recv.at[2 + half], near[axis, 1 if half == 0 else 3]).start()

    def to_sibling(part, where):
        ref = slot(part, where)
        remote(ref, ref, pair_send, pair_recv, sibling).start()

    parts = range(3)

    slot_row = lax.broadcasted_iota(jnp.int32, (8, 128), 0)

    def border_go(first, stop):
        @pl.loop(first, stop)
        def _(step):
            number, target = other(step)
            alive = slot_row < count_ref[0, number]
            for k in range(8):
                row = rows_ref[0, number, k]
                block = lax.shift_right_logical(row, 7)
                inside = row & 127
                for side in range(2):
                    outbox[number, side, pl.ds(k, 1), :] = local_ref[block, pl.ds(inside + 128 * side, 1), :]
            for side in range(2):
                outbox[number, side] = jnp.where(alive, outbox[number, side], 0.0)
            if first == 128:
                inbox[number] = outbox[number]
            else:
                remote(outbox.at[number], inbox.at[me], border_send, border_recv, target).start()

    def border_end():
        arrived_all = inbox.at[pl.ds(0, 127)]
        pltpu.make_async_copy(arrived_all, arrived_all, border_recv).wait()

        @pl.loop(0, 8)
        def _(i):
            for k in range(16):
                for side in range(2):
                    local_ref[32 + i, 128 * side + 8 * k:128 * side + 8 * k + 8, :] = inbox[16 * i + k, side]

    def pre_chunks(start, stop):
        @pl.loop(start, stop)
        def _(chunk):
            own = []
            for i in range(CHUNK // 128):
                block = local_ref[chunk * (CHUNK // 128) + i]
                own.append(jnp.concatenate([block[0:128], block[128:256]], axis=1))
            high, low = split(jnp.concatenate(own, axis=0))
            value = dot(jnp.concatenate([high, low, high], axis=1), self_k[...]) + bias_ref[...]
            for i in range(CHUNK // 128):
                for side in range(2):
                    local_ref[40 + chunk * (CHUNK // 128) + i, 128 * side:128 * side + 128, :] = value[
                        128 * i:128 * i + 128, 128 * side:128 * side + 128
                    ]

    lane = lax.broadcasted_iota(jnp.int32, (128, 128), 1)

    def tile_chunks(start, stop):
        @pl.loop(start, stop)
        def _(i):
            load_tiles(i).wait()
            spot = lax.rem(i, TILE_SLOTS)
            sums = sums_ref[...]
            for k in range(TILE_CHUNK):
                tile = i * TILE_CHUNK + k
                weight = ring[spot, k]
                high, low = split(weight)
                split_ref[tile, :, 0:128] = high
                split_ref[tile, :, 128:256] = low
                sums = jnp.where(lane == tile, jnp.sum(weight, axis=1, keepdims=True), sums)
            sums_ref[...] = sums

            @pl.when(i + TILE_SLOTS < 128 // TILE_CHUNK)
            def _():
                load_tiles(i + TILE_SLOTS).start()

    for p in parts:
        first, second, _ = PART_AXES[p]
        send_both(p, {}, first, send1.at[p], recv1.at[p])
        send_both(p, {}, second, send2.at[p], recv2.at[p, 0])

    sums_ref[...] = jnp.zeros_like(sums_ref)
    border_go(1, 65)
    own.wait()
    for side, offset in ((0, 3), (1, 1)):
        unit = OFFSETS.index(offset)
        for p in parts:
            first, second, _ = PART_AXES[p]
            where = {first: offset}
            arrived(p, where, first, recv1.at[p, side])
            pass_on(p, where, first, send1.at[p], recv1.at[p], side)
            send_both(p, where, second, send2.at[p], recv2.at[p, unit])
    border_go(65, 128)
    border_go(128, 129)
    for p in parts:
        first, second, third = PART_AXES[p]
        where = {first: 2}
        arrived(p, where, first, recv1.at[p, 2], 0)
        arrived(p, where, first, recv1.at[p, 3], 1)
        send_both(p, where, second, send2.at[p], recv2.at[p, 3])
        line = {first: "all"}
        send_both(p, line, third, send3.at[p], recv3.at[p, 0])
        to_sibling(p, line)
    self_high, self_low = split(w_self_ref[...])
    self_k[0:256, :] = self_high
    self_k[256:512, :] = self_high
    self_k[512:768, :] = self_low

    for unit in range(4):
        for side, offset in ((0, 3), (1, 1)):
            for p in parts:
                first, second, _ = PART_AXES[p]
                where = {first: OFFSETS[unit], second: offset}
                arrived(p, where, second, recv2.at[p, unit, side])
                pass_on(p, where, second, send2.at[p], recv2.at[p, unit], side)
    for side, offset in ((0, 3), (1, 1)):
        for p in parts:
            first, second, third = PART_AXES[p]
            line = {first: "all", second: offset}
            send_both(p, line, third, send3.at[p], recv3.at[p, 1 + side])
            to_sibling(p, line)
    for p in parts:
        first, second, third = PART_AXES[p]
        for unit in range(4):
            where = {first: OFFSETS[unit], second: 2}
            arrived(p, where, second, recv2.at[p, unit, 2], 0)
            arrived(p, where, second, recv2.at[p, unit, 3], 1)
        line = {first: "all", second: 2}
        send_both(p, line, third, send3.at[p], recv3.at[p, 3])
        to_sibling(p, line)

    for unit in range(4):
        pre_chunks(4 * unit, 4 * unit + 4)
        for side, offset in ((0, 3), (1, 1)):
            for p in parts:
                first, second, third = PART_AXES[p]
                line = {first: "all", second: OFFSETS[unit], third: offset}
                arrived(p, line, third, recv3.at[p, unit, side])
                pass_on(p, line, third, send3.at[p], recv3.at[p, unit], side)
                to_sibling(p, line)
        if unit < 2:
            tile_chunks(8 * unit, 8 * unit + 8)
        if unit == 2:
            border_end()
    for unit in range(4):
        for p in parts:
            first, second, third = PART_AXES[p]
            line = {first: "all", second: OFFSETS[unit], third: 2}
            arrived(p, line, third, recv3.at[p, unit, 2], 0)
            arrived(p, line, third, recv3.at[p, unit, 3], 1)
            to_sibling(p, line)

    for p in parts:
        rows = pl.ds(PART_START[p], PART_ROWS[p])
        for sem, ref in (
            (send1.at[p], table_ref.at[core, 0, 0, pl.ds(0, 3), rows, :]),
            (send2.at[p], table_ref.at[core, 0, pl.ds(0, 3), pl.ds(0, 4), rows, :]),
            (send3.at[p], table_ref.at[core, pl.ds(0, 3), pl.ds(0, 4), pl.ds(0, 4), rows, :]),
        ):
            pltpu.make_async_copy(ref, ref, sem).wait()
    sent = outbox.at[pl.ds(0, 127)]
    pltpu.make_async_copy(sent, sent, border_send).wait()
    mine, theirs = table_ref.at[core], table_ref.at[1 - core]
    pltpu.make_async_copy(mine, mine, pair_send).wait()
    pltpu.make_async_copy(theirs, theirs, pair_recv).wait()


def gather(hub_block, send_rows, send_count, features, weights, w_self, bias):
    dma = pltpu.SemaphoreType.DMA
    smem = pl.BlockSpec(memory_space=pltpu.SMEM)
    vmem = pl.BlockSpec(memory_space=pltpu.VMEM)
    hbm = pl.BlockSpec(memory_space=pl.ANY)
    border = pltpu.VMEM((128, 2, 8, 128), F32)
    return pl.pallas_call(
        gather_kernel,
        out_shape=(
            jax.ShapeDtypeStruct((2, 4, 4, 4, 256, 128), F32),
            pltpu.VMEM((72, 256, 128), F32),
            pltpu.VMEM((128, 128, 256), BF16),
            pltpu.VMEM((128, 128), F32),
        ),
        in_specs=[smem] * 3 + [hbm] * 2 + [vmem] * 2,
        out_specs=(hbm,) + (vmem,) * 3,
        scratch_shapes=[
            pltpu.VMEM((256, 128), F32),
            pltpu.VMEM((768, 256), BF16),
            pltpu.VMEM((TILE_SLOTS, TILE_CHUNK, 128, 128), F32),
            border, border,
            dma, dma((2,)), dma((TILE_SLOTS,)), dma((3, 4)), dma((3, 4, 4)), dma((3, 4, 4)),
            dma((3,)), dma((3,)), dma((3,)), dma, dma,
            dma, dma,
        ],
        compiler_params=pltpu.CompilerParams(
            collective_id=0, has_side_effects=True, vmem_limit_bytes=34 * 2**20
        ),
        name="gather",
    )(hub_block, send_rows, send_count, features, weights, w_self, bias)


GROUP = 4


def layer_kernel(
    loss_scale, dst_ref, src_ref, count_ref,
    table_hbm, local_ref, split_ref, sums_ref, dst_row_ref, w_neigh_ref, head_ref, labels_ref,
    grad_ref,
    table_ref, neigh_k, total, grad_self, grad_neigh, grad_small, near_tiles, hub_tiles, table_sem,
):
    tiles = split_ref.shape[0]
    blocks = total.shape[0] - 1
    first_hub = blocks + 8
    count = count_ref[0]

    table_loads = [
        pltpu.make_async_copy(table_hbm.at[i // 4, i % 4], table_ref.at[i // 4, i % 4], table_sem.at[i])
        for i in range(8)
    ]
    for load in table_loads:
        load.start()
    total[...] = jnp.zeros_like(total)
    neigh_high, neigh_low = split(w_neigh_ref[...])
    neigh_k[0:256, :] = neigh_high
    neigh_k[256:512, :] = neigh_high
    neigh_k[512:768, :] = neigh_low

    def sort_tile(tile, ends):
        near_end, hub_end = ends
        near_tiles[near_end] = tile
        hub_tiles[hub_end] = tile
        near = jnp.where(src_ref[tile] < first_hub, 1, 0)
        return near_end + near, hub_end + (1 - near)

    near_count, hub_count = lax.fori_loop(0, count, sort_tile, (0, 0))

    def wide(block):
        return jnp.concatenate([block[0:128], block[128:256]], axis=1)

    def near_source(src):
        return wide(local_ref[src])

    def hub_source(src):
        number = src - first_hub
        return wide(table_ref[
            lax.shift_right_logical(number, 1) & 1,
            lax.shift_right_logical(number, 5),
            (lax.shift_right_logical(number, 4) & 1) * 2 + (number & 1),
            lax.shift_right_logical(number, 2) & 3,
        ])

    for listed, amount, source in ((near_tiles, near_count, near_source), (hub_tiles, hub_count, hub_source)):
        if listed is hub_tiles:
            for load in table_loads:
                load.wait()

        @pl.loop(0, lax.div(amount + (GROUP - 1), GROUP))
        def _(group):
            products, targets = [], []
            for k in range(GROUP):
                at = group * GROUP + k
                tile = listed[jnp.minimum(at, amount - 1)]
                targets.append(jnp.where(at < amount, dst_ref[tile], blocks))
                weight = split_ref[tile]
                high, low = split(source(src_ref[tile]))
                products.append(
                    dot(
                        jnp.concatenate([weight, weight[:, 0:128]], axis=1),
                        jnp.concatenate([high, high, low], axis=0),
                    )
                )
            for k in range(GROUP):
                total[targets[k]] += products[k]

    by_lanes = (((1,), (1,)), ((), ()))
    tile_lane = lax.broadcasted_iota(jnp.int32, (blocks, tiles), 1)
    block_row = lax.broadcasted_iota(jnp.int32, (blocks, tiles), 0)
    chosen = (dst_row_ref[...] == block_row) & (tile_lane < count)
    chosen = jnp.where(chosen, 1.0, 0.0).astype(BF16)
    sums_high, sums_low = split(sums_ref[...])
    sums_rest = (sums_ref[...] - sums_high.astype(F32) - sums_low.astype(F32)).astype(BF16)
    scales = 1.0 / (
        1.0 + (dot(sums_high, chosen, by_lanes) + dot(sums_low, chosen, by_lanes) + dot(sums_rest, chosen, by_lanes))
    )
    target_columns = (2.0 * labels_ref[...].astype(F32) - 1.0).T
    lane = lax.broadcasted_iota(jnp.int32, target_columns.shape, 1)

    grad_self[...] = jnp.zeros_like(grad_self)
    grad_neigh[...] = jnp.zeros_like(grad_neigh)
    grad_small[...] = jnp.zeros_like(grad_small)
    per_chunk = CHUNK // 128

    @pl.loop(0, blocks // per_chunk)
    def _(chunk):
        rows = pl.ds(pl.multiple_of(chunk * CHUNK, CHUNK), CHUNK)
        own, mean, target, pre = [], [], [], []
        for i in range(per_chunk):
            b = chunk * per_chunk + i
            block = wide(local_ref[b])
            scale = jnp.sum(jnp.where(lane == b, scales, 0.0), axis=1, keepdims=True)
            own.append(block)
            pre.append(wide(local_ref[first_hub + b]))
            mean.append((block + total[b]) * scale)
            target.append(jnp.sum(jnp.where(lane == b, target_columns, 0.0), axis=1, keepdims=True))
        own, mean, target, pre = (jnp.concatenate(v, axis=0) for v in (own, mean, target, pre))
        own_high, own_low = split(own)
        mean_high, mean_low = split(mean)
        pre = pre + dot(jnp.concatenate([mean_high, mean_low, mean_high], axis=1), neigh_k[...])
        gate = jax.nn.sigmoid(pre)
        hidden = pre * gate
        score = jnp.sum(hidden * head_ref[...], axis=1, keepdims=True)
        dscore = (score - target) * loss_scale
        dpre = dscore * head_ref[...] * (gate * (1.0 + pre * (1.0 - gate)))
        d_high, d_low = split(dpre)
        by_rows = (((0,), (0,)), ((), ()))
        right = jnp.concatenate([d_high, d_high, d_low], axis=0)
        grad_self[...] += dot(jnp.concatenate([own_high, own_low, own_high], axis=0), right, by_rows)
        grad_neigh[...] += dot(jnp.concatenate([mean_high, mean_low, mean_high], axis=0), right, by_rows)
        grad_small[0:1, :] += jnp.sum(dpre, axis=0, keepdims=True)
        grad_small[1:2, :] += jnp.sum(hidden * dscore, axis=0, keepdims=True)

    for i, ref in enumerate((grad_self, grad_neigh)):
        for side in range(2):
            grad_ref[pl.ds(512 * i + 256 * side, 256), :] = ref[:, 128 * side:128 * side + 128]
    grad_ref[1024:1032, :] = jnp.zeros((8, 128), F32)
    for i in range(4):
        side = 128 * (i % 2)
        grad_ref[1024 + i:1025 + i, :] = grad_small[i // 2:i // 2 + 1, side:side + 128]


def layer(loss_scale, dst, src, count, table, local, weights, sums, w_neigh, head, labels):
    smem = pl.BlockSpec(memory_space=pltpu.SMEM)
    vmem = pl.BlockSpec(memory_space=pltpu.VMEM)
    width = w_neigh.shape[0]
    blocks = labels.shape[0]
    return pl.pallas_call(
        functools.partial(layer_kernel, loss_scale),
        out_shape=pltpu.VMEM((1032, 128), F32),
        in_specs=[smem] * 3 + [pl.BlockSpec(memory_space=pl.ANY)] + [vmem] * 7,
        out_specs=vmem,
        scratch_shapes=[
            pltpu.VMEM(table.shape, F32),
            pltpu.VMEM((3 * width, width), BF16),
            pltpu.VMEM((blocks + 1, 128, width), F32),
            pltpu.VMEM((width, width), F32),
            pltpu.VMEM((width, width), F32),
            pltpu.VMEM((8, width), F32),
            pltpu.SMEM((dst.shape[0] + 1,), jnp.int32),
            pltpu.SMEM((dst.shape[0] + 1,), jnp.int32),
            pltpu.SemaphoreType.DMA((8,)),
        ],
        compiler_params=pltpu.CompilerParams(vmem_limit_bytes=30 * 2**20),
        name="layer",
    )(dst, src, count, table, local, weights, sums, dst.reshape(1, -1), w_neigh, head, labels)


def sum_kernel(
    grad_ref, whole,
    pair_in, plane_out, plane_in, plane_sum, z_out, z_in, send_sem, recv_sem,
):
    place, core = my_place()
    q = place["y"] * 4 + place["x"]
    z = place["z"]
    sibling = device_at(place, 1 - core)

    def plane_peer(step):
        other = lax.rem(q + step, 16)
        return other, device_at({"x": lax.rem(other, 4), "y": lax.div(other, 4), "z": z}, core)

    def z_peer(step):
        other = lax.rem(z + step, 4)
        return other, device_at(shifted(place, "z", step), core)

    barrier = pltpu.get_barrier_semaphore()
    targets = [sibling] + [plane_peer(s)[1] for s in range(1, 16)] + [z_peer(s)[1] for s in range(1, 4)]
    for target in targets:
        pl.semaphore_signal(barrier, inc=1, device_id=target, device_id_type=MESH)
    pl.semaphore_wait(barrier, len(targets))

    def send(stage, src, dst, target):
        pltpu.make_async_remote_copy(
            src_ref=src, dst_ref=dst, send_sem=send_sem.at[stage], recv_sem=recv_sem.at[stage],
            device_id=target, device_id_type=MESH,
        ).start()

    def received(stage, ref):
        pltpu.make_async_copy(ref, ref, recv_sem.at[stage]).wait()

    half, other_half = core * 512, (1 - core) * 512
    send(0, grad_ref.at[pl.ds(other_half, 512)], pair_in.at[pl.ds(0, 512)], sibling)
    send(0, grad_ref.at[pl.ds(1024, 8)], pair_in.at[pl.ds(512, 8)], sibling)
    received(0, pair_in)

    small = grad_ref[1024:1032, :] + pair_in[512:520, :]
    for step in range(1, 17):
        other, target = plane_peer(step)
        row = pl.multiple_of(other * 32, 32)
        buffer = plane_in if step == 16 else plane_out
        buffer[other, 0:32, :] = grad_ref[pl.ds(half + row, 32), :] + pair_in[pl.ds(row, 32), :]
        buffer[other, 32:40, :] = small
        if step < 16:
            send(1, plane_out.at[other], plane_in.at[q], target)
    received(1, plane_in.at[pl.ds(0, 15)])
    value = plane_in[0]
    for i in range(1, 16):
        value = value + plane_in[i]
    plane_sum[...] = value

    for step in range(1, 5):
        other, target = z_peer(step)
        buffer = z_in if step == 4 else z_out
        buffer[other, 0:8, :] = plane_sum[pl.ds(pl.multiple_of(other * 8, 8), 8), :]
        buffer[other, 8:16, :] = plane_sum[32:40, :]
        if step < 4:
            send(2, z_out.at[other], z_in.at[z], target)
    received(2, z_in.at[pl.ds(0, 3)])
    value = (z_in[0] + z_in[1]) + (z_in[2] + z_in[3])

    lot = half + q * 32
    mine = pl.ds(pl.multiple_of(lot + z * 8, 8), 8)
    whole[mine, :] = value[0:8]
    for step in range(1, 4):
        send(3, whole.at[mine], whole.at[mine], z_peer(step)[1])
    received(3, whole.at[pl.ds(0, 24)])
    mine = pl.ds(pl.multiple_of(lot, 32), 32)
    for step in range(1, 16):
        send(4, whole.at[mine], whole.at[mine], plane_peer(step)[1])
    received(4, whole.at[pl.ds(0, 480)])
    mine = pl.ds(pl.multiple_of(half, 512), 512)
    send(5, whole.at[mine], whole.at[mine], sibling)
    whole[1024:1032, :] = value[8:16]
    received(5, whole.at[pl.ds(0, 512)])

    sent = (
        pair_in, plane_in.at[pl.ds(0, 15)], z_in.at[pl.ds(0, 3)],
        whole.at[pl.ds(0, 24)], whole.at[pl.ds(0, 480)], whole.at[pl.ds(0, 512)],
    )
    for stage, ref in enumerate(sent):
        pltpu.make_async_copy(ref, ref, send_sem.at[stage]).wait()


def sum_grads(grads):
    vmem = pl.BlockSpec(memory_space=pltpu.VMEM)
    dma = pltpu.SemaphoreType.DMA
    return pl.pallas_call(
        sum_kernel,
        out_shape=pltpu.VMEM((1032, 128), F32),
        in_specs=[vmem],
        out_specs=vmem,
        scratch_shapes=[
            pltpu.VMEM((520, 128), F32),
            pltpu.VMEM((16, 40, 128), F32),
            pltpu.VMEM((16, 40, 128), F32),
            pltpu.VMEM((40, 128), F32),
            pltpu.VMEM((4, 16, 128), F32),
            pltpu.VMEM((4, 16, 128), F32),
            dma((6,)),
            dma((6,)),
        ],
        compiler_params=pltpu.CompilerParams(
            collective_id=1, has_side_effects=True, vmem_limit_bytes=8 * 2**20
        ),
        name="sum_grads",
    )(grads)


def unpack_kernel(whole, self_ref, neigh_ref, bias_ref, head_ref):
    for i, ref in enumerate((self_ref, neigh_ref)):
        for side in range(2):
            ref[:, 128 * side:128 * side + 128] = whole[pl.ds(512 * i + 256 * side, 256), :]
    for i in range(4):
        ref = (bias_ref, head_ref)[i // 2]
        ref[128 * (i % 2):128 * (i % 2) + 128] = whole[1024 + i, :]


def unpack(whole):
    vmem = pl.BlockSpec(memory_space=pltpu.VMEM)
    return pl.pallas_call(
        unpack_kernel,
        out_shape=(
            jax.ShapeDtypeStruct((256, 256), F32),
            jax.ShapeDtypeStruct((256, 256), F32),
            jax.ShapeDtypeStruct((256,), F32),
            jax.ShapeDtypeStruct((256,), F32),
        ),
        in_specs=[vmem],
        out_specs=(vmem,) * 4,
        compiler_params=pltpu.CompilerParams(vmem_limit_bytes=4 * 2**20),
        name="unpack",
    )(whole)


def on_device(
    features,
    w_self,
    w_neigh,
    bias,
    w_head,
    tile_weights,
    tile_dst,
    tile_src,
    tile_count,
    hub_block,
    send_rows,
    send_count,
    labels,
):
    width = features.shape[1]
    blocks = features.shape[0] // 128
    vertex_total = features.shape[0] * lax.axis_size(("vert", "row"))
    loss_scale = 1.0 / math.sqrt(vertex_total)
    table, local, weights, sums = gather(
        hub_block, send_rows, send_count, features.reshape(blocks, 128, width), tile_weights,
        w_self, bias.reshape(1, width),
    )
    grads = layer(
        loss_scale, tile_dst, tile_src, tile_count, table, local, weights, sums,
        w_neigh, w_head.reshape(1, width), labels.reshape(blocks, 128),
    )
    return unpack(sum_grads(grads))


def solution(mesh):
    in_specs = (
        P(("vert", "row"), None),
        P(),
        P(),
        P(),
        P(),
        P(("vert", "row"), None, None),
        P(("vert", "row")),
        P(("vert", "row")),
        P(("vert", "row")),
        P(("vert", "row")),
        P(("vert", "row"), None, None),
        P(("vert", "row"), None),
        P(("vert", "row")),
    )
    out_specs = (P(), P(), P(), P())
    return jax.shard_map(
        on_device, mesh=mesh, in_specs=in_specs, out_specs=out_specs, check_vma=False
    )
```

```python
import functools
import math

import jax
import jax.numpy as jnp
from jax import lax
from jax.experimental import pallas as pl
from jax.experimental.pallas import tpu as pltpu
from jax.sharding import PartitionSpec as P

MESH = pl.DeviceIdType.MESH
BF16 = jnp.bfloat16
F32 = jnp.float32

PART_START = (0, 88, 176)
PART_ROWS = (88, 88, 80)
PART_HALF = (48, 40, 40)
PART_AXES = ("xyz", "yzx", "zxy")
OFFSETS = (0, 3, 1, 2)


def my_place():
    vert = lax.axis_index("vert")
    row = lax.axis_index("row")
    core = lax.rem(vert, 2)
    x = lax.rem(lax.div(vert, 2), 4)
    y = lax.rem(lax.div(vert, 8), 2) * 2 + row
    z = lax.div(vert, 16)
    return {"x": x, "y": y, "z": z}, core


def device_at(place, core):
    x, y, z = place["x"], place["y"], place["z"]
    vert = ((z * 2 + lax.div(y, 2)) * 4 + x) * 2 + core
    return (vert, lax.rem(y, 2))


def shifted(place, axis, step):
    moved = dict(place)
    moved[axis] = lax.rem(place[axis] + step, 4)
    return moved


def split(value):
    high = value.astype(BF16)
    low = (value - high.astype(F32)).astype(BF16)
    return high, low


def dot(a, b, dims=(((1,), (0,)), ((), ()))):
    return lax.dot_general(a, b, dims, preferred_element_type=F32)


GATHER_VMEM, TILES_VMEM, LAYER_VMEM = 34, 30, 30
CHUNK = 256
TILE_CHUNK = 8
TILE_SLOTS = 4


def gather_kernel(
    hub_block_ref, rows_ref, count_ref, feat_hbm, weights_hbm, w_self_ref, bias_ref,
    table_ref, local_ref, split_ref, sums_ref,
    hub, self_k, ring, outbox, inbox,
    own_sem, feat_sem, ring_sem, recv1, recv2, recv3, send1, send2, send3, pair_send, pair_recv,
    border_send, border_recv,
):
    place, core = my_place()
    x, y, z = place["x"], place["y"], place["z"]
    near = {}
    for axis in "xyz":
        for step in (1, 3):
            near[axis, step] = device_at(shifted(place, axis, step), core)
    sibling = device_at(place, 1 - core)
    me = lax.axis_index("vert") * 2 + lax.axis_index("row")

    def other(step):
        number = lax.rem(me + step, 128)
        return number, (lax.div(number, 2), lax.rem(number, 2))

    loads = []
    for side in range(2):
        load = pltpu.make_async_copy(
            feat_hbm.at[:, :, pl.ds(128 * side, 128)],
            local_ref.at[pl.ds(0, 32), pl.ds(128 * side, 128), :],
            feat_sem.at[side],
        )
        load.start()
        loads.append(load)

    def load_tiles(i):
        spot = lax.rem(i, TILE_SLOTS)
        return pltpu.make_async_copy(
            weights_hbm.at[pl.ds(i * TILE_CHUNK, TILE_CHUNK)], ring.at[spot], ring_sem.at[spot]
        )

    for i in range(TILE_SLOTS):
        load_tiles(i).start()

    barrier = pltpu.get_barrier_semaphore()

    @pl.loop(1, 128)
    def _(step):
        pl.semaphore_signal(barrier, inc=1, device_id=other(step)[1], device_id_type=MESH)


    for load in loads:
        load.wait()
    hub[...] = local_ref[hub_block_ref[0]]
    own = pltpu.make_async_copy(hub, table_ref.at[core, z, y, x], own_sem)
    own.start()
    pl.semaphore_wait(barrier, 127)

    def slot(part, where, half=None):
        start, rows = PART_START[part], PART_ROWS[part]
        if half == 0:
            rows = PART_HALF[part]
        elif half == 1:
            start, rows = start + PART_HALF[part], rows - PART_HALF[part]
        at = []
        for axis in "zyx":
            offset = where.get(axis, 0)
            at.append(pl.ds(0, 4) if offset == "all" else lax.rem(place[axis] + offset, 4))
        return table_ref.at[(core, *at, pl.ds(start, rows), slice(None))]

    def remote(src, dst, send_sem, recv_sem, target):
        return pltpu.make_async_remote_copy(
            src_ref=src, dst_ref=dst, send_sem=send_sem, recv_sem=recv_sem,
            device_id=target, device_id_type=MESH,
        )

    def send_both(part, where, axis, send_sem, recv):
        dst = slot(part, where)
        src = dst if where else hub.at[pl.ds(PART_START[part], PART_ROWS[part])]
        remote(src, dst, send_sem, recv.at[0], near[axis, 1]).start()
        remote(src, dst, send_sem, recv.at[1], near[axis, 3]).start()

    def arrived(part, where, axis, sem, half=None):
        ref = slot(part, where, half)
        remote(ref, ref, sem, sem, near[axis, 1]).wait_recv()

    def pass_on(part, where, axis, send_sem, recv, half):
        ref = slot(part, where, half)
        remote(ref, ref, send_sem, recv.at[2 + half], near[axis, 1 if half == 0 else 3]).start()

    def to_sibling(part, where):
        ref = slot(part, where)
        remote(ref, ref, pair_send, pair_recv, sibling).start()

    parts = range(3)

    slot_row = lax.broadcasted_iota(jnp.int32, (8, 128), 0)

    def border_go(first, stop):
        @pl.loop(first, stop)
        def _(step):
            number, target = other(step)
            alive = slot_row < count_ref[0, number]
            for k in range(8):
                row = rows_ref[0, number, k]
                block = lax.shift_right_logical(row, 7)
                inside = row & 127
                for side in range(2):
                    outbox[number, side, pl.ds(k, 1), :] = local_ref[block, pl.ds(inside + 128 * side, 1), :]
            for side in range(2):
                outbox[number, side] = jnp.where(alive, outbox[number, side], 0.0)
            if first == 128:
                inbox[number] = outbox[number]
            else:
                remote(outbox.at[number], inbox.at[me], border_send, border_recv, target).start()

    def border_end():
        arrived_all = inbox.at[pl.ds(0, 127)]
        pltpu.make_async_copy(arrived_all, arrived_all, border_recv).wait()

        @pl.loop(0, 8)
        def _(i):
            for k in range(16):
                for side in range(2):
                    local_ref[32 + i, 128 * side + 8 * k:128 * side + 8 * k + 8, :] = inbox[16 * i + k, side]

    def pre_chunks(start, stop):
        @pl.loop(start, stop)
        def _(chunk):
            own = []
            for i in range(CHUNK // 128):
                block = local_ref[chunk * (CHUNK // 128) + i]
                own.append(jnp.concatenate([block[0:128], block[128:256]], axis=1))
            high, low = split(jnp.concatenate(own, axis=0))
            value = dot(jnp.concatenate([high, low, high], axis=1), self_k[...]) + bias_ref[...]
            for i in range(CHUNK // 128):
                for side in range(2):
                    local_ref[40 + chunk * (CHUNK // 128) + i, 128 * side:128 * side + 128, :] = value[
                        128 * i:128 * i + 128, 128 * side:128 * side + 128
                    ]

    lane = lax.broadcasted_iota(jnp.int32, (128, 128), 1)

    def tile_chunks(start, stop):
        @pl.loop(start, stop)
        def _(i):
            load_tiles(i).wait()
            spot = lax.rem(i, TILE_SLOTS)
            sums = sums_ref[...]
            for k in range(TILE_CHUNK):
                tile = i * TILE_CHUNK + k
                weight = ring[spot, k]
                high, low = split(weight)
                split_ref[tile, :, 0:128] = high
                split_ref[tile, :, 128:256] = low
                sums = jnp.where(lane == tile, jnp.sum(weight, axis=1, keepdims=True), sums)
            sums_ref[...] = sums

            @pl.when(i + TILE_SLOTS < 128 // TILE_CHUNK)
            def _():
                load_tiles(i + TILE_SLOTS).start()

    for p in parts:
        first, second, _ = PART_AXES[p]
        send_both(p, {}, first, send1.at[p], recv1.at[p])
        send_both(p, {}, second, send2.at[p], recv2.at[p, 0])

    sums_ref[...] = jnp.zeros_like(sums_ref)
    border_go(1, 65)
    own.wait()
    for side, offset in ((0, 3), (1, 1)):
        unit = OFFSETS.index(offset)
        for p in parts:
            first, second, _ = PART_AXES[p]
            where = {first: offset}
            arrived(p, where, first, recv1.at[p, side])
            pass_on(p, where, first, send1.at[p], recv1.at[p], side)
            send_both(p, where, second, send2.at[p], recv2.at[p, unit])
    border_go(65, 128)
    border_go(128, 129)
    for p in parts:
        first, second, third = PART_AXES[p]
        where = {first: 2}
        arrived(p, where, first, recv1.at[p, 2], 0)
        arrived(p, where, first, recv1.at[p, 3], 1)
        send_both(p, where, second, send2.at[p], recv2.at[p, 3])
        line = {first: "all"}
        send_both(p, line, third, send3.at[p], recv3.at[p, 0])
        to_sibling(p, line)
    self_high, self_low = split(w_self_ref[...])
    self_k[0:256, :] = self_high
    self_k[256:512, :] = self_high
    self_k[512:768, :] = self_low

    for unit in range(4):
        for side, offset in ((0, 3), (1, 1)):
            for p in parts:
                first, second, _ = PART_AXES[p]
                where = {first: OFFSETS[unit], second: offset}
                arrived(p, where, second, recv2.at[p, unit, side])
                pass_on(p, where, second, send2.at[p], recv2.at[p, unit], side)
    for side, offset in ((0, 3), (1, 1)):
        for p in parts:
            first, second, third = PART_AXES[p]
            line = {first: "all", second: offset}
            send_both(p, line, third, send3.at[p], recv3.at[p, 1 + side])
            to_sibling(p, line)
    for p in parts:
        first, second, third = PART_AXES[p]
        for unit in range(4):
            where = {first: OFFSETS[unit], second: 2}
            arrived(p, where, second, recv2.at[p, unit, 2], 0)
            arrived(p, where, second, recv2.at[p, unit, 3], 1)
        line = {first: "all", second: 2}
        send_both(p, line, third, send3.at[p], recv3.at[p, 3])
        to_sibling(p, line)

    for unit in range(4):
        pre_chunks(4 * unit, 4 * unit + 4)
        for side, offset in ((0, 3), (1, 1)):
            for p in parts:
                first, second, third = PART_AXES[p]
                line = {first: "all", second: OFFSETS[unit], third: offset}
                arrived(p, line, third, recv3.at[p, unit, side])
                pass_on(p, line, third, send3.at[p], recv3.at[p, unit], side)
                to_sibling(p, line)
        if unit < 2:
            tile_chunks(8 * unit, 8 * unit + 8)
        if unit == 2:
            border_end()
    for unit in range(4):
        for p in parts:
            first, second, third = PART_AXES[p]
            line = {first: "all", second: OFFSETS[unit], third: 2}
            arrived(p, line, third, recv3.at[p, unit, 2], 0)
            arrived(p, line, third, recv3.at[p, unit, 3], 1)
            to_sibling(p, line)

    for p in parts:
        rows = pl.ds(PART_START[p], PART_ROWS[p])
        for sem, ref in (
            (send1.at[p], table_ref.at[core, 0, 0, pl.ds(0, 3), rows, :]),
            (send2.at[p], table_ref.at[core, 0, pl.ds(0, 3), pl.ds(0, 4), rows, :]),
            (send3.at[p], table_ref.at[core, pl.ds(0, 3), pl.ds(0, 4), pl.ds(0, 4), rows, :]),
        ):
            pltpu.make_async_copy(ref, ref, sem).wait()
    sent = outbox.at[pl.ds(0, 127)]
    pltpu.make_async_copy(sent, sent, border_send).wait()
    mine, theirs = table_ref.at[core], table_ref.at[1 - core]
    pltpu.make_async_copy(mine, mine, pair_send).wait()
    pltpu.make_async_copy(theirs, theirs, pair_recv).wait()


def gather(hub_block, send_rows, send_count, features, weights, w_self, bias):
    dma = pltpu.SemaphoreType.DMA
    smem = pl.BlockSpec(memory_space=pltpu.SMEM)
    vmem = pl.BlockSpec(memory_space=pltpu.VMEM)
    hbm = pl.BlockSpec(memory_space=pl.ANY)
    border = pltpu.VMEM((128, 2, 8, 128), F32)
    return pl.pallas_call(
        gather_kernel,
        out_shape=(
            jax.ShapeDtypeStruct((2, 4, 4, 4, 256, 128), F32),
            pltpu.VMEM((72, 256, 128), F32),
            pltpu.VMEM((128, 128, 256), BF16),
            pltpu.VMEM((128, 128), F32),
        ),
        in_specs=[smem] * 3 + [hbm] * 2 + [vmem] * 2,
        out_specs=(hbm,) + (vmem,) * 3,
        scratch_shapes=[
            pltpu.VMEM((256, 128), F32),
            pltpu.VMEM((768, 256), BF16),
            pltpu.VMEM((TILE_SLOTS, TILE_CHUNK, 128, 128), F32),
            border, border,
            dma, dma((2,)), dma((TILE_SLOTS,)), dma((3, 4)), dma((3, 4, 4)), dma((3, 4, 4)),
            dma((3,)), dma((3,)), dma((3,)), dma, dma,
            dma, dma,
        ],
        compiler_params=pltpu.CompilerParams(
            collective_id=0, has_side_effects=True, vmem_limit_bytes=GATHER_VMEM * 2**20
        ),
        name="gather",
    )(hub_block, send_rows, send_count, features, weights, w_self, bias)


GROUP = 4


def tiles_kernel(
    dst_ref, src_ref, count_ref,
    table_hbm, local_ref, split_ref, sums_ref, dst_row_ref,
    total, scales_ref,
    table_ref, near_tiles, low_tiles, high_tiles, table_sem,
):
    tiles = split_ref.shape[0]
    blocks = total.shape[0] - 1
    first_hub = blocks + 8
    count = count_ref[0]

    table_loads = [
        pltpu.make_async_copy(table_hbm.at[i // 4, i % 4], table_ref.at[i // 4, i % 4], table_sem.at[i])
        for i in range(8)
    ]
    for load in table_loads:
        load.start()
    total[...] = jnp.zeros_like(total)

    def sort_tile(tile, ends):
        src = src_ref[tile]
        near = jnp.where(src < first_hub, 1, 0)
        high = (1 - near) * (lax.shift_right_logical(src - first_hub, 1) & 1)
        kinds = (near, 1 - near - high, high)
        for listed, end in zip((near_tiles, low_tiles, high_tiles), ends):
            listed[end] = tile
        return tuple(end + kind for end, kind in zip(ends, kinds))

    amounts = lax.fori_loop(0, count, sort_tile, (0, 0, 0))

    def wide(block):
        return jnp.concatenate([block[0:128], block[128:256]], axis=1)

    def near_source(src):
        return wide(local_ref[src])

    def hub_source(src):
        number = src - first_hub
        return wide(table_ref[
            lax.shift_right_logical(number, 1) & 1,
            lax.shift_right_logical(number, 5),
            (lax.shift_right_logical(number, 4) & 1) * 2 + (number & 1),
            lax.shift_right_logical(number, 2) & 3,
        ])

    by_lanes = (((1,), (1,)), ((), ()))
    tile_lane = lax.broadcasted_iota(jnp.int32, (blocks, tiles), 1)
    block_row = lax.broadcasted_iota(jnp.int32, (blocks, tiles), 0)
    chosen = (dst_row_ref[...] == block_row) & (tile_lane < count)
    chosen = jnp.where(chosen, 1.0, 0.0).astype(BF16)
    sums_high, sums_low = split(sums_ref[...])
    sums_rest = (sums_ref[...] - sums_high.astype(F32) - sums_low.astype(F32)).astype(BF16)
    scales_ref[...] = 1.0 / (
        1.0 + (dot(sums_high, chosen, by_lanes) + dot(sums_low, chosen, by_lanes) + dot(sums_rest, chosen, by_lanes))
    )

    work = ((near_tiles, near_source, ()), (low_tiles, hub_source, table_loads[:4]), (high_tiles, hub_source, table_loads[4:]))
    for (listed, source, loads), amount in zip(work, amounts):
        for load in loads:
            load.wait()

        @pl.loop(0, lax.div(amount + (GROUP - 1), GROUP))
        def _(group):
            products, targets = [], []
            for k in range(GROUP):
                at = group * GROUP + k
                tile = listed[jnp.minimum(at, amount - 1)]
                targets.append(jnp.where(at < amount, dst_ref[tile], blocks))
                weight = split_ref[tile]
                high, low = split(source(src_ref[tile]))
                products.append(
                    dot(
                        jnp.concatenate([weight, weight[:, 0:128]], axis=1),
                        jnp.concatenate([high, high, low], axis=0),
                    )
                )
            for k in range(GROUP):
                total[targets[k]] += products[k]


def add_tiles(dst, src, count, table, local, weights, sums, blocks):
    smem = pl.BlockSpec(memory_space=pltpu.SMEM)
    vmem = pl.BlockSpec(memory_space=pltpu.VMEM)
    listed = pltpu.SMEM((dst.shape[0] + 1,), jnp.int32)
    return pl.pallas_call(
        tiles_kernel,
        out_shape=(pltpu.VMEM((blocks + 1, 128, 256), F32), pltpu.VMEM((128, blocks), F32)),
        in_specs=[smem] * 3 + [pl.BlockSpec(memory_space=pl.ANY)] + [vmem] * 4,
        out_specs=(vmem, vmem),
        scratch_shapes=[
            pltpu.VMEM(table.shape, F32), listed, listed, listed, pltpu.SemaphoreType.DMA((8,)),
        ],
        compiler_params=pltpu.CompilerParams(vmem_limit_bytes=TILES_VMEM * 2**20),
        name="add_tiles",
    )(dst, src, count, table, local, weights, sums, dst.reshape(1, -1))


LAYER_CHUNK = 512


def layer_kernel(
    loss_scale, total, scales_ref, local_ref, w_neigh_ref, head_ref, labels_ref,
    whole,
    neigh_k, grad_self, grad_neigh, grad_small, grads, pair_in, lots_in, small_in,
    send_sem, recv_sem,
):
    place, core = my_place()
    number = (place["z"] * 4 + place["y"]) * 4 + place["x"]
    sibling = device_at(place, 1 - core)

    def peer(step):
        other = lax.rem(number + step, 64)
        at = {"x": lax.rem(other, 4), "y": lax.rem(lax.div(other, 4), 4), "z": lax.div(other, 16)}
        return other, device_at(at, core)

    barrier = pltpu.get_barrier_semaphore()
    pl.semaphore_signal(barrier, inc=1, device_id=sibling, device_id_type=MESH)

    @pl.loop(1, 64)
    def _(step):
        pl.semaphore_signal(barrier, inc=1, device_id=peer(step)[1], device_id_type=MESH)

    blocks = labels_ref.shape[0]
    neigh_high, neigh_low = split(w_neigh_ref[...])
    neigh_k[0:256, :] = neigh_high
    neigh_k[256:512, :] = neigh_high
    neigh_k[512:768, :] = neigh_low
    target_columns = (2.0 * labels_ref[...].astype(F32) - 1.0).T
    lane = lax.broadcasted_iota(jnp.int32, target_columns.shape, 1)
    grad_self[...] = jnp.zeros_like(grad_self)
    grad_neigh[...] = jnp.zeros_like(grad_neigh)
    grad_small[...] = jnp.zeros_like(grad_small)
    per_chunk = LAYER_CHUNK // 128

    def wide(block):
        return jnp.concatenate([block[0:128], block[128:256]], axis=1)

    @pl.loop(0, blocks // per_chunk)
    def _(chunk):
        own, mean, target, pre = [], [], [], []
        for i in range(per_chunk):
            b = chunk * per_chunk + i
            block = wide(local_ref[b])
            scale = jnp.sum(jnp.where(lane == b, scales_ref[...], 0.0), axis=1, keepdims=True)
            own.append(block)
            pre.append(wide(local_ref[blocks + 8 + b]))
            mean.append((block + total[b]) * scale)
            target.append(jnp.sum(jnp.where(lane == b, target_columns, 0.0), axis=1, keepdims=True))
        own, mean, target, pre = (jnp.concatenate(v, axis=0) for v in (own, mean, target, pre))
        own_high, own_low = split(own)
        mean_high, mean_low = split(mean)
        pre = pre + dot(jnp.concatenate([mean_high, mean_low, mean_high], axis=1), neigh_k[...])
        gate = jax.nn.sigmoid(pre)
        hidden = pre * gate
        score = jnp.sum(hidden * head_ref[...], axis=1, keepdims=True)
        dscore = (score - target) * loss_scale
        dpre = dscore * head_ref[...] * (gate * (1.0 + pre * (1.0 - gate)))
        d_high, d_low = split(dpre)
        by_rows = (((0,), (0,)), ((), ()))
        right = jnp.concatenate([d_high, d_high, d_low], axis=0)
        grad_self[...] += dot(jnp.concatenate([own_high, own_low, own_high], axis=0), right, by_rows)
        grad_neigh[...] += dot(jnp.concatenate([mean_high, mean_low, mean_high], axis=0), right, by_rows)
        grad_small[0:1, :] += jnp.sum(dpre, axis=0, keepdims=True)
        grad_small[1:2, :] += jnp.sum(hidden * dscore, axis=0, keepdims=True)

    for i, ref in enumerate((grad_self, grad_neigh)):
        for side in range(2):
            grads[pl.ds(512 * i + 256 * side, 256), :] = ref[:, 128 * side:128 * side + 128]
    grads[1024:1032, :] = jnp.zeros((8, 128), F32)
    for i in range(4):
        side = 128 * (i % 2)
        grads[1024 + i:1025 + i, :] = grad_small[i // 2:i // 2 + 1, side:side + 128]

    pl.semaphore_wait(barrier, 64)

    def send(stage, src, dst, target):
        pltpu.make_async_remote_copy(
            src_ref=src, dst_ref=dst, send_sem=send_sem.at[stage], recv_sem=recv_sem.at[stage],
            device_id=target, device_id_type=MESH,
        ).start()

    def received(stage, ref):
        pltpu.make_async_copy(ref, ref, recv_sem.at[stage]).wait()

    def sent(stage, ref):
        pltpu.make_async_copy(ref, ref, send_sem.at[stage]).wait()

    half, other_half = core * 512, (1 - core) * 512
    small = pl.ds(1024, 8)
    send(0, grads.at[pl.ds(other_half, 512)], pair_in.at[pl.ds(0, 512)], sibling)
    send(0, grads.at[small], pair_in.at[pl.ds(512, 8)], sibling)
    received(0, pair_in)
    pair_in[0:512, :] += grads[pl.ds(half, 512), :]
    pair_in[512:520, :] += grads[1024:1032, :]

    def lot(other):
        return pl.ds(pl.multiple_of(other * 8, 8), 8)

    first = (core == 0) & (number == 0)
    feeds_first = (core == 0) & (number != 0)

    @pl.when(feeds_first)
    def _():
        send(4, pair_in.at[pl.ds(512, 8)], small_in.at[number], device_at({"x": 0, "y": 0, "z": 0}, core))

    @pl.loop(1, 64)
    def _(step):
        other, target = peer(step)
        send(1, pair_in.at[lot(other)], lots_in.at[number], target)

    lots_in[number] = pair_in[lot(number), :]
    received(1, lots_in.at[pl.ds(0, 63)])
    mine = pl.ds(pl.multiple_of(half + number * 8, 8), 8)
    whole[mine, :] = jnp.sum(lots_in[...], axis=0)

    @pl.loop(1, 64)
    def _(step):
        send(2, whole.at[mine], whole.at[mine], peer(step)[1])

    @pl.when(first)
    def _():
        small_in[0] = pair_in[512:520, :]
        received(4, small_in.at[pl.ds(0, 63)])
        whole[1024:1032, :] = jnp.sum(small_in[...], axis=0)

        @pl.loop(1, 64)
        def _(step):
            send(5, whole.at[small], whole.at[small], peer(step)[1])

    received(2, whole.at[pl.ds(0, 504)])
    matrix = pl.ds(pl.multiple_of(half, 512), 512)
    send(3, whole.at[matrix], whole.at[matrix], sibling)

    @pl.when(feeds_first)
    def _():
        received(5, whole.at[small])

    @pl.when(core == 0)
    def _():
        send(6, whole.at[small], whole.at[small], sibling)

    @pl.when(core == 1)
    def _():
        received(6, whole.at[small])

    received(3, whole.at[pl.ds(0, 512)])
    sent(0, pair_in)
    sent(1, lots_in.at[pl.ds(0, 63)])
    sent(2, whole.at[pl.ds(0, 504)])
    sent(3, whole.at[pl.ds(0, 512)])

    @pl.when(feeds_first)
    def _():
        sent(4, small_in.at[0])

    @pl.when(first)
    def _():
        sent(5, small_in.at[pl.ds(0, 63)])

    @pl.when(core == 0)
    def _():
        sent(6, whole.at[small])


def layer(loss_scale, total, scales, local, w_neigh, head, labels):
    vmem = pl.BlockSpec(memory_space=pltpu.VMEM)
    dma = pltpu.SemaphoreType.DMA
    width = w_neigh.shape[0]
    return pl.pallas_call(
        functools.partial(layer_kernel, loss_scale),
        out_shape=pltpu.VMEM((1032, 128), F32),
        in_specs=[vmem] * 6,
        out_specs=vmem,
        scratch_shapes=[
            pltpu.VMEM((3 * width, width), BF16),
            pltpu.VMEM((width, width), F32),
            pltpu.VMEM((width, width), F32),
            pltpu.VMEM((8, width), F32),
            pltpu.VMEM((1032, 128), F32),
            pltpu.VMEM((520, 128), F32),
            pltpu.VMEM((64, 8, 128), F32),
            pltpu.VMEM((64, 8, 128), F32),
            dma((7,)),
            dma((7,)),
        ],
        compiler_params=pltpu.CompilerParams(
            collective_id=1, has_side_effects=True, vmem_limit_bytes=LAYER_VMEM * 2**20
        ),
        name="layer",
    )(total, scales, local, w_neigh, head, labels)


def unpack_kernel(whole, self_ref, neigh_ref, bias_ref, head_ref):
    for i, ref in enumerate((self_ref, neigh_ref)):
        for side in range(2):
            ref[:, 128 * side:128 * side + 128] = whole[pl.ds(512 * i + 256 * side, 256), :]
    for i in range(4):
        ref = (bias_ref, head_ref)[i // 2]
        ref[128 * (i % 2):128 * (i % 2) + 128] = whole[1024 + i, :]


def unpack(whole):
    vmem = pl.BlockSpec(memory_space=pltpu.VMEM)
    return pl.pallas_call(
        unpack_kernel,
        out_shape=(
            jax.ShapeDtypeStruct((256, 256), F32),
            jax.ShapeDtypeStruct((256, 256), F32),
            jax.ShapeDtypeStruct((256,), F32),
            jax.ShapeDtypeStruct((256,), F32),
        ),
        in_specs=[vmem],
        out_specs=(vmem,) * 4,
        compiler_params=pltpu.CompilerParams(vmem_limit_bytes=4 * 2**20),
        name="unpack",
    )(whole)


def on_device(
    features,
    w_self,
    w_neigh,
    bias,
    w_head,
    tile_weights,
    tile_dst,
    tile_src,
    tile_count,
    hub_block,
    send_rows,
    send_count,
    labels,
):
    width = features.shape[1]
    blocks = features.shape[0] // 128
    vertex_total = features.shape[0] * lax.axis_size(("vert", "row"))
    loss_scale = 1.0 / math.sqrt(vertex_total)
    table, local, weights, sums = gather(
        hub_block, send_rows, send_count, features.reshape(blocks, 128, width), tile_weights,
        w_self, bias.reshape(1, width),
    )
    total, scales = add_tiles(tile_dst, tile_src, tile_count, table, local, weights, sums, blocks)
    return unpack(layer(loss_scale, total, scales, local, w_neigh, w_head.reshape(1, width), labels.reshape(blocks, 128)))


def solution(mesh):
    in_specs = (
        P(("vert", "row"), None),
        P(),
        P(),
        P(),
        P(),
        P(("vert", "row"), None, None),
        P(("vert", "row")),
        P(("vert", "row")),
        P(("vert", "row")),
        P(("vert", "row")),
        P(("vert", "row"), None, None),
        P(("vert", "row"), None),
        P(("vert", "row")),
    )
    out_specs = (P(), P(), P(), P())
    return jax.shard_map(
        on_device, mesh=mesh, in_specs=in_specs, out_specs=out_specs, check_vma=False
    )
```

```python
import functools
import math

import jax
import jax.numpy as jnp
from jax import lax
from jax.experimental import pallas as pl
from jax.experimental.pallas import tpu as pltpu
from jax.sharding import PartitionSpec as P

MESH = pl.DeviceIdType.MESH
BF16 = jnp.bfloat16
F32 = jnp.float32

PART_START = (0, 88, 176)
PART_ROWS = (88, 88, 80)
PART_HALF = (48, 40, 40)
PART_AXES = ("xyz", "yzx", "zxy")
OFFSETS = (0, 3, 1, 2)


def my_place():
    vert = lax.axis_index("vert")
    row = lax.axis_index("row")
    core = lax.rem(vert, 2)
    x = lax.rem(lax.div(vert, 2), 4)
    y = lax.rem(lax.div(vert, 8), 2) * 2 + row
    z = lax.div(vert, 16)
    return {"x": x, "y": y, "z": z}, core


def device_at(place, core):
    x, y, z = place["x"], place["y"], place["z"]
    vert = ((z * 2 + lax.div(y, 2)) * 4 + x) * 2 + core
    return (vert, lax.rem(y, 2))


def shifted(place, axis, step):
    moved = dict(place)
    moved[axis] = lax.rem(place[axis] + step, 4)
    return moved


def split(value):
    high = value.astype(BF16)
    low = (value - high.astype(F32)).astype(BF16)
    return high, low


def dot(a, b, dims=(((1,), (0,)), ((), ()))):
    return lax.dot_general(a, b, dims, preferred_element_type=F32)


GATHER_VMEM, TILES_VMEM, LAYER_VMEM = 34, 30, 30
CHUNK = 256
TILE_CHUNK = 8
TILE_SLOTS = 4


def gather_kernel(
    hub_block_ref, rows_hbm, count_hbm, feat_hbm, weights_hbm, self_hbm, bias_hbm,
    table_ref, local_ref, split_ref, sums_ref,
    rows_ref, count_ref, w_self_ref, bias_ref, small_sem, hub, self_k, ring, outbox, inbox,
    own_sem, feat_sem, ring_sem, recv1, recv2, recv3, send1, send2, send3, pair_send, pair_recv,
    border_send, border_recv,
):
    place, core = my_place()
    x, y, z = place["x"], place["y"], place["z"]
    near = {}
    for axis in "xyz":
        for step in (1, 3):
            near[axis, step] = device_at(shifted(place, axis, step), core)
    sibling = device_at(place, 1 - core)
    me = lax.axis_index("vert") * 2 + lax.axis_index("row")

    def other(step):
        number = lax.rem(me + step, 128)
        return number, (lax.div(number, 2), lax.rem(number, 2))

    small_loads = [
        pltpu.make_async_copy(src, dst, small_sem.at[i])
        for i, (src, dst) in enumerate((
            (rows_hbm, rows_ref), (count_hbm, count_ref), (self_hbm, w_self_ref), (bias_hbm, bias_ref),
        ))
    ]
    loads = []
    for side in range(2):
        load = pltpu.make_async_copy(
            feat_hbm.at[:, :, pl.ds(128 * side, 128)],
            local_ref.at[pl.ds(0, 32), pl.ds(128 * side, 128), :],
            feat_sem.at[side],
        )
        load.start()
        loads.append(load)

    def load_tiles(i):
        spot = lax.rem(i, TILE_SLOTS)
        return pltpu.make_async_copy(
            weights_hbm.at[pl.ds(i * TILE_CHUNK, TILE_CHUNK)], ring.at[spot], ring_sem.at[spot]
        )

    for load in small_loads:
        load.start()
    for i in range(TILE_SLOTS):
        load_tiles(i).start()

    barrier = pltpu.get_barrier_semaphore()

    @pl.loop(1, 128)
    def _(step):
        pl.semaphore_signal(barrier, inc=1, device_id=other(step)[1], device_id_type=MESH)


    for load in loads:
        load.wait()
    hub[...] = local_ref[hub_block_ref[0]]
    for load in small_loads:
        load.wait()
    own = pltpu.make_async_copy(hub, table_ref.at[core, z, y, x], own_sem)
    own.start()
    pl.semaphore_wait(barrier, 127)

    def slot(part, where, half=None):
        start, rows = PART_START[part], PART_ROWS[part]
        if half == 0:
            rows = PART_HALF[part]
        elif half == 1:
            start, rows = start + PART_HALF[part], rows - PART_HALF[part]
        at = []
        for axis in "zyx":
            offset = where.get(axis, 0)
            at.append(pl.ds(0, 4) if offset == "all" else lax.rem(place[axis] + offset, 4))
        return table_ref.at[(core, *at, pl.ds(start, rows), slice(None))]

    def remote(src, dst, send_sem, recv_sem, target):
        return pltpu.make_async_remote_copy(
            src_ref=src, dst_ref=dst, send_sem=send_sem, recv_sem=recv_sem,
            device_id=target, device_id_type=MESH,
        )

    def send_both(part, where, axis, send_sem, recv):
        dst = slot(part, where)
        src = dst if where else hub.at[pl.ds(PART_START[part], PART_ROWS[part])]
        remote(src, dst, send_sem, recv.at[0], near[axis, 1]).start()
        remote(src, dst, send_sem, recv.at[1], near[axis, 3]).start()

    def arrived(part, where, axis, sem, half=None):
        ref = slot(part, where, half)
        remote(ref, ref, sem, sem, near[axis, 1]).wait_recv()

    def pass_on(part, where, axis, send_sem, recv, half):
        ref = slot(part, where, half)
        remote(ref, ref, send_sem, recv.at[2 + half], near[axis, 1 if half == 0 else 3]).start()

    def to_sibling(part, where):
        ref = slot(part, where)
        remote(ref, ref, pair_send, pair_recv, sibling).start()

    parts = range(3)

    slot_row = lax.broadcasted_iota(jnp.int32, (8, 128), 0)

    def border_go(first, stop):
        @pl.loop(first, stop)
        def _(step):
            number, target = other(step)
            alive = slot_row < count_ref[0, number]
            for k in range(8):
                row = rows_ref[k, number]
                block = lax.shift_right_logical(row, 7)
                inside = row & 127
                for side in range(2):
                    outbox[number, side, pl.ds(k, 1), :] = local_ref[block, pl.ds(inside + 128 * side, 1), :]
            for side in range(2):
                outbox[number, side] = jnp.where(alive, outbox[number, side], 0.0)
            if first == 128:
                inbox[number] = outbox[number]
            else:
                remote(outbox.at[number], inbox.at[me], border_send, border_recv, target).start()

    def border_end():
        arrived_all = inbox.at[pl.ds(0, 127)]
        pltpu.make_async_copy(arrived_all, arrived_all, border_recv).wait()

        @pl.loop(0, 8)
        def _(i):
            for k in range(16):
                for side in range(2):
                    local_ref[32 + i, 128 * side + 8 * k:128 * side + 8 * k + 8, :] = inbox[16 * i + k, side]

    def pre_chunks(start, stop):
        @pl.loop(start, stop)
        def _(chunk):
            own = []
            for i in range(CHUNK // 128):
                block = local_ref[chunk * (CHUNK // 128) + i]
                own.append(jnp.concatenate([block[0:128], block[128:256]], axis=1))
            high, low = split(jnp.concatenate(own, axis=0))
            value = dot(jnp.concatenate([high, low, high], axis=1), self_k[...]) + bias_ref[...]
            for i in range(CHUNK // 128):
                for side in range(2):
                    local_ref[40 + chunk * (CHUNK // 128) + i, 128 * side:128 * side + 128, :] = value[
                        128 * i:128 * i + 128, 128 * side:128 * side + 128
                    ]

    lane = lax.broadcasted_iota(jnp.int32, (128, 128), 1)

    def tile_chunks(start, stop):
        @pl.loop(start, stop)
        def _(i):
            load_tiles(i).wait()
            spot = lax.rem(i, TILE_SLOTS)
            sums = sums_ref[...]
            for k in range(TILE_CHUNK):
                tile = i * TILE_CHUNK + k
                weight = ring[spot, k]
                high, low = split(weight)
                split_ref[tile, :, 0:128] = high
                split_ref[tile, :, 128:256] = low
                sums = jnp.where(lane == tile, jnp.sum(weight, axis=1, keepdims=True), sums)
            sums_ref[...] = sums

            @pl.when(i + TILE_SLOTS < 128 // TILE_CHUNK)
            def _():
                load_tiles(i + TILE_SLOTS).start()

    for p in parts:
        first, second, _ = PART_AXES[p]
        send_both(p, {}, first, send1.at[p], recv1.at[p])
        send_both(p, {}, second, send2.at[p], recv2.at[p, 0])

    sums_ref[...] = jnp.zeros_like(sums_ref)
    border_go(1, 65)
    own.wait()
    for side, offset in ((0, 3), (1, 1)):
        unit = OFFSETS.index(offset)
        for p in parts:
            first, second, _ = PART_AXES[p]
            where = {first: offset}
            arrived(p, where, first, recv1.at[p, side])
            pass_on(p, where, first, send1.at[p], recv1.at[p], side)
            send_both(p, where, second, send2.at[p], recv2.at[p, unit])
    border_go(65, 128)
    border_go(128, 129)
    for p in parts:
        first, second, third = PART_AXES[p]
        where = {first: 2}
        arrived(p, where, first, recv1.at[p, 2], 0)
        arrived(p, where, first, recv1.at[p, 3], 1)
        send_both(p, where, second, send2.at[p], recv2.at[p, 3])
        line = {first: "all"}
        send_both(p, line, third, send3.at[p], recv3.at[p, 0])
        to_sibling(p, line)
    self_high, self_low = split(w_self_ref[...])
    self_k[0:256, :] = self_high
    self_k[256:512, :] = self_high
    self_k[512:768, :] = self_low

    for unit in range(4):
        for side, offset in ((0, 3), (1, 1)):
            for p in parts:
                first, second, _ = PART_AXES[p]
                where = {first: OFFSETS[unit], second: offset}
                arrived(p, where, second, recv2.at[p, unit, side])
                pass_on(p, where, second, send2.at[p], recv2.at[p, unit], side)
    for side, offset in ((0, 3), (1, 1)):
        for p in parts:
            first, second, third = PART_AXES[p]
            line = {first: "all", second: offset}
            send_both(p, line, third, send3.at[p], recv3.at[p, 1 + side])
            to_sibling(p, line)
    for p in parts:
        first, second, third = PART_AXES[p]
        for unit in range(4):
            where = {first: OFFSETS[unit], second: 2}
            arrived(p, where, second, recv2.at[p, unit, 2], 0)
            arrived(p, where, second, recv2.at[p, unit, 3], 1)
        line = {first: "all", second: 2}
        send_both(p, line, third, send3.at[p], recv3.at[p, 3])
        to_sibling(p, line)

    for unit in range(4):
        pre_chunks(4 * unit, 4 * unit + 4)
        for side, offset in ((0, 3), (1, 1)):
            for p in parts:
                first, second, third = PART_AXES[p]
                line = {first: "all", second: OFFSETS[unit], third: offset}
                arrived(p, line, third, recv3.at[p, unit, side])
                pass_on(p, line, third, send3.at[p], recv3.at[p, unit], side)
                to_sibling(p, line)
        if unit < 2:
            tile_chunks(8 * unit, 8 * unit + 8)
        if unit == 2:
            border_end()
    for unit in range(4):
        for p in parts:
            first, second, third = PART_AXES[p]
            line = {first: "all", second: OFFSETS[unit], third: 2}
            arrived(p, line, third, recv3.at[p, unit, 2], 0)
            arrived(p, line, third, recv3.at[p, unit, 3], 1)
            to_sibling(p, line)

    for p in parts:
        rows = pl.ds(PART_START[p], PART_ROWS[p])
        for sem, ref in (
            (send1.at[p], table_ref.at[core, 0, 0, pl.ds(0, 3), rows, :]),
            (send2.at[p], table_ref.at[core, 0, pl.ds(0, 3), pl.ds(0, 4), rows, :]),
            (send3.at[p], table_ref.at[core, pl.ds(0, 3), pl.ds(0, 4), pl.ds(0, 4), rows, :]),
        ):
            pltpu.make_async_copy(ref, ref, sem).wait()
    sent = outbox.at[pl.ds(0, 127)]
    pltpu.make_async_copy(sent, sent, border_send).wait()
    mine, theirs = table_ref.at[core], table_ref.at[1 - core]
    pltpu.make_async_copy(mine, mine, pair_send).wait()
    pltpu.make_async_copy(theirs, theirs, pair_recv).wait()


def gather(hub_block, send_rows, send_count, features, weights, w_self, bias):
    dma = pltpu.SemaphoreType.DMA
    smem = pl.BlockSpec(memory_space=pltpu.SMEM)
    vmem = pl.BlockSpec(memory_space=pltpu.VMEM)
    hbm = pl.BlockSpec(memory_space=pl.ANY)
    far = pl.BlockSpec(memory_space=pltpu.HBM)
    border = pltpu.VMEM((128, 2, 8, 128), F32)
    pin = functools.partial(pltpu.with_memory_space_constraint, memory_space=pltpu.HBM)
    return pl.pallas_call(
        gather_kernel,
        out_shape=(
            jax.ShapeDtypeStruct((2, 4, 4, 4, 256, 128), F32),
            pltpu.VMEM((72, 256, 128), F32),
            pltpu.VMEM((128, 128, 256), BF16),
            pltpu.VMEM((128, 128), F32),
        ),
        in_specs=[smem] + [far] * 2 + [hbm] * 2 + [far] * 2,
        out_specs=(hbm,) + (vmem,) * 3,
        scratch_shapes=[
            pltpu.SMEM(send_rows.shape, jnp.int32),
            pltpu.SMEM(send_count.shape, jnp.int32),
            pltpu.VMEM(w_self.shape, F32),
            pltpu.VMEM(bias.shape, F32),
            dma((4,)),
            pltpu.VMEM((256, 128), F32),
            pltpu.VMEM((768, 256), BF16),
            pltpu.VMEM((TILE_SLOTS, TILE_CHUNK, 128, 128), F32),
            border, border,
            dma, dma((2,)), dma((TILE_SLOTS,)), dma((3, 4)), dma((3, 4, 4)), dma((3, 4, 4)),
            dma((3,)), dma((3,)), dma((3,)), dma, dma,
            dma, dma,
        ],
        compiler_params=pltpu.CompilerParams(
            collective_id=0, has_side_effects=True, vmem_limit_bytes=GATHER_VMEM * 2**20
        ),
        name="gather",
    )(hub_block, pin(send_rows), pin(send_count), features, weights, pin(w_self), pin(bias))


GROUP = 4


def tiles_kernel(
    dst_ref, src_ref, count_ref,
    table_hbm, local_ref, split_ref, sums_ref, dst_row_ref,
    total, scales_ref,
    table_ref, near_tiles, low_tiles, high_tiles, table_sem,
):
    tiles = split_ref.shape[0]
    blocks = total.shape[0] - 1
    first_hub = blocks + 8
    count = count_ref[0]

    table_loads = [
        pltpu.make_async_copy(table_hbm.at[i // 4, i % 4], table_ref.at[i // 4, i % 4], table_sem.at[i])
        for i in range(8)
    ]
    for load in table_loads:
        load.start()
    total[...] = jnp.zeros_like(total)

    def sort_tile(tile, ends):
        src = src_ref[tile]
        near = jnp.where(src < first_hub, 1, 0)
        high = (1 - near) * (lax.shift_right_logical(src - first_hub, 1) & 1)
        kinds = (near, 1 - near - high, high)
        for listed, end in zip((near_tiles, low_tiles, high_tiles), ends):
            listed[end] = tile
        return tuple(end + kind for end, kind in zip(ends, kinds))

    amounts = lax.fori_loop(0, count, sort_tile, (0, 0, 0))

    def wide(block):
        return jnp.concatenate([block[0:128], block[128:256]], axis=1)

    def near_source(src):
        return wide(local_ref[src])

    def hub_source(src):
        number = src - first_hub
        return wide(table_ref[
            lax.shift_right_logical(number, 1) & 1,
            lax.shift_right_logical(number, 5),
            (lax.shift_right_logical(number, 4) & 1) * 2 + (number & 1),
            lax.shift_right_logical(number, 2) & 3,
        ])

    by_lanes = (((1,), (1,)), ((), ()))
    tile_lane = lax.broadcasted_iota(jnp.int32, (blocks, tiles), 1)
    block_row = lax.broadcasted_iota(jnp.int32, (blocks, tiles), 0)
    chosen = (dst_row_ref[...] == block_row) & (tile_lane < count)
    chosen = jnp.where(chosen, 1.0, 0.0).astype(BF16)
    sums_high, sums_low = split(sums_ref[...])
    sums_rest = (sums_ref[...] - sums_high.astype(F32) - sums_low.astype(F32)).astype(BF16)
    scales_ref[...] = 1.0 / (
        1.0 + (dot(sums_high, chosen, by_lanes) + dot(sums_low, chosen, by_lanes) + dot(sums_rest, chosen, by_lanes))
    )

    work = ((near_tiles, near_source, ()), (low_tiles, hub_source, table_loads[:4]), (high_tiles, hub_source, table_loads[4:]))
    for (listed, source, loads), amount in zip(work, amounts):
        for load in loads:
            load.wait()

        @pl.loop(0, lax.div(amount + (GROUP - 1), GROUP))
        def _(group):
            products, targets = [], []
            for k in range(GROUP):
                at = group * GROUP + k
                tile = listed[jnp.minimum(at, amount - 1)]
                targets.append(jnp.where(at < amount, dst_ref[tile], blocks))
                weight = split_ref[tile]
                high, low = split(source(src_ref[tile]))
                products.append(
                    dot(
                        jnp.concatenate([weight, weight[:, 0:128]], axis=1),
                        jnp.concatenate([high, high, low], axis=0),
                    )
                )
            for k in range(GROUP):
                total[targets[k]] += products[k]


def add_tiles(dst, src, count, table, local, weights, sums, blocks):
    smem = pl.BlockSpec(memory_space=pltpu.SMEM)
    vmem = pl.BlockSpec(memory_space=pltpu.VMEM)
    listed = pltpu.SMEM((dst.shape[0] + 1,), jnp.int32)
    return pl.pallas_call(
        tiles_kernel,
        out_shape=(pltpu.VMEM((blocks + 1, 128, 256), F32), pltpu.VMEM((128, blocks), F32)),
        in_specs=[smem] * 3 + [pl.BlockSpec(memory_space=pl.ANY)] + [vmem] * 4,
        out_specs=(vmem, vmem),
        scratch_shapes=[
            pltpu.VMEM(table.shape, F32), listed, listed, listed, pltpu.SemaphoreType.DMA((8,)),
        ],
        compiler_params=pltpu.CompilerParams(vmem_limit_bytes=TILES_VMEM * 2**20),
        name="add_tiles",
    )(dst, src, count, table, local, weights, sums, dst.reshape(1, -1))


LAYER_CHUNK = 1024


def layer_kernel(
    loss_scale, total, scales_ref, local_ref, w_neigh_ref, head_ref, labels_ref,
    whole,
    neigh_k, grad_self, grad_neigh, grad_small, grads, pair_in, lots_in, small_in,
    send_sem, recv_sem,
):
    place, core = my_place()
    number = (place["z"] * 4 + place["y"]) * 4 + place["x"]
    sibling = device_at(place, 1 - core)

    def peer(step):
        other = lax.rem(number + step, 64)
        at = {"x": lax.rem(other, 4), "y": lax.rem(lax.div(other, 4), 4), "z": lax.div(other, 16)}
        return other, device_at(at, core)

    barrier = pltpu.get_barrier_semaphore()
    pl.semaphore_signal(barrier, inc=1, device_id=sibling, device_id_type=MESH)

    @pl.loop(1, 64)
    def _(step):
        pl.semaphore_signal(barrier, inc=1, device_id=peer(step)[1], device_id_type=MESH)

    blocks = labels_ref.shape[0]
    neigh_high, neigh_low = split(w_neigh_ref[...])
    neigh_k[0:256, :] = neigh_high
    neigh_k[256:512, :] = neigh_high
    neigh_k[512:768, :] = neigh_low
    target_columns = (2.0 * labels_ref[...].astype(F32) - 1.0).T
    lane = lax.broadcasted_iota(jnp.int32, target_columns.shape, 1)
    grad_self[...] = jnp.zeros_like(grad_self)
    grad_neigh[...] = jnp.zeros_like(grad_neigh)
    grad_small[...] = jnp.zeros_like(grad_small)
    per_chunk = LAYER_CHUNK // 128

    def wide(block):
        return jnp.concatenate([block[0:128], block[128:256]], axis=1)

    @pl.loop(0, blocks // per_chunk)
    def _(chunk):
        own, mean, target, pre = [], [], [], []
        for i in range(per_chunk):
            b = chunk * per_chunk + i
            block = wide(local_ref[b])
            scale = jnp.sum(jnp.where(lane == b, scales_ref[...], 0.0), axis=1, keepdims=True)
            own.append(block)
            pre.append(wide(local_ref[blocks + 8 + b]))
            mean.append((block + total[b]) * scale)
            target.append(jnp.sum(jnp.where(lane == b, target_columns, 0.0), axis=1, keepdims=True))
        own, mean, target, pre = (jnp.concatenate(v, axis=0) for v in (own, mean, target, pre))
        own_high, own_low = split(own)
        mean_high, mean_low = split(mean)
        pre = pre + dot(jnp.concatenate([mean_high, mean_low, mean_high], axis=1), neigh_k[...])
        gate = jax.nn.sigmoid(pre)
        hidden = pre * gate
        score = jnp.sum(hidden * head_ref[...], axis=1, keepdims=True)
        dscore = (score - target) * loss_scale
        dpre = dscore * head_ref[...] * (gate * (1.0 + pre * (1.0 - gate)))
        d_high, d_low = split(dpre)
        by_rows = (((0,), (0,)), ((), ()))
        right = jnp.concatenate([d_high, d_high, d_low], axis=0)
        grad_self[...] += dot(jnp.concatenate([own_high, own_low, own_high], axis=0), right, by_rows)
        grad_neigh[...] += dot(jnp.concatenate([mean_high, mean_low, mean_high], axis=0), right, by_rows)
        grad_small[0:1, :] += jnp.sum(dpre, axis=0, keepdims=True)
        grad_small[1:2, :] += jnp.sum(hidden * dscore, axis=0, keepdims=True)

    for i, ref in enumerate((grad_self, grad_neigh)):
        for side in range(2):
            grads[pl.ds(512 * i + 256 * side, 256), :] = ref[:, 128 * side:128 * side + 128]
    grads[1024:1032, :] = jnp.zeros((8, 128), F32)
    for i in range(4):
        side = 128 * (i % 2)
        grads[1024 + i:1025 + i, :] = grad_small[i // 2:i // 2 + 1, side:side + 128]

    pl.semaphore_wait(barrier, 64)

    def send(stage, src, dst, target):
        pltpu.make_async_remote_copy(
            src_ref=src, dst_ref=dst, send_sem=send_sem.at[stage], recv_sem=recv_sem.at[stage],
            device_id=target, device_id_type=MESH,
        ).start()

    def received(stage, ref):
        pltpu.make_async_copy(ref, ref, recv_sem.at[stage]).wait()

    def sent(stage, ref):
        pltpu.make_async_copy(ref, ref, send_sem.at[stage]).wait()

    half, other_half = core * 512, (1 - core) * 512
    small = pl.ds(1024, 8)
    send(0, grads.at[pl.ds(other_half, 512)], pair_in.at[pl.ds(0, 512)], sibling)
    send(0, grads.at[small], pair_in.at[pl.ds(512, 8)], sibling)
    received(0, pair_in)
    pair_in[0:512, :] += grads[pl.ds(half, 512), :]
    pair_in[512:520, :] += grads[1024:1032, :]

    def lot(other):
        return pl.ds(pl.multiple_of(other * 8, 8), 8)

    first = (core == 0) & (number == 0)
    feeds_first = (core == 0) & (number != 0)

    @pl.when(feeds_first)
    def _():
        send(4, pair_in.at[pl.ds(512, 8)], small_in.at[number], device_at({"x": 0, "y": 0, "z": 0}, core))

    @pl.loop(1, 64)
    def _(step):
        other, target = peer(step)
        send(1, pair_in.at[lot(other)], lots_in.at[number], target)

    lots_in[number] = pair_in[lot(number), :]
    received(1, lots_in.at[pl.ds(0, 63)])
    mine = pl.ds(pl.multiple_of(half + number * 8, 8), 8)
    whole[mine, :] = jnp.sum(lots_in[...], axis=0)

    def from_plane(z):
        return recv_sem.at[7 + z]

    @pl.loop(1, 64)
    def _(step):
        pltpu.make_async_remote_copy(
            src_ref=whole.at[mine], dst_ref=whole.at[mine], send_sem=send_sem.at[2],
            recv_sem=from_plane(place["z"]), device_id=peer(step)[1], device_id_type=MESH,
        ).start()

    @pl.when(first)
    def _():
        small_in[0] = pair_in[512:520, :]
        received(4, small_in.at[pl.ds(0, 63)])
        whole[1024:1032, :] = jnp.sum(small_in[...], axis=0)

        @pl.loop(1, 64)
        def _(step):
            send(5, whole.at[small], whole.at[small], peer(step)[1])

    for step in (0, 1, 3, 2):
        z = lax.rem(place["z"] + step, 4)
        amount = whole.at[pl.ds(0, 128 if step else 120)]
        pltpu.make_async_copy(amount, amount, from_plane(z)).wait()
        plane = pl.ds(pl.multiple_of(half + z * 128, 128), 128)
        send(3, whole.at[plane], whole.at[plane], sibling)

    @pl.when(feeds_first)
    def _():
        received(5, whole.at[small])

    @pl.when(core == 0)
    def _():
        send(6, whole.at[small], whole.at[small], sibling)

    @pl.when(core == 1)
    def _():
        received(6, whole.at[small])

    received(3, whole.at[pl.ds(0, 512)])
    sent(0, pair_in)
    sent(1, lots_in.at[pl.ds(0, 63)])
    sent(2, whole.at[pl.ds(0, 504)])
    sent(3, whole.at[pl.ds(0, 512)])

    @pl.when(feeds_first)
    def _():
        sent(4, small_in.at[0])

    @pl.when(first)
    def _():
        sent(5, small_in.at[pl.ds(0, 63)])

    @pl.when(core == 0)
    def _():
        sent(6, whole.at[small])


def layer(loss_scale, total, scales, local, w_neigh, head, labels):
    vmem = pl.BlockSpec(memory_space=pltpu.VMEM)
    dma = pltpu.SemaphoreType.DMA
    width = w_neigh.shape[0]
    return pl.pallas_call(
        functools.partial(layer_kernel, loss_scale),
        out_shape=pltpu.VMEM((1032, 128), F32),
        in_specs=[vmem] * 6,
        out_specs=vmem,
        scratch_shapes=[
            pltpu.VMEM((3 * width, width), BF16),
            pltpu.VMEM((width, width), F32),
            pltpu.VMEM((width, width), F32),
            pltpu.VMEM((8, width), F32),
            pltpu.VMEM((1032, 128), F32),
            pltpu.VMEM((520, 128), F32),
            pltpu.VMEM((64, 8, 128), F32),
            pltpu.VMEM((64, 8, 128), F32),
            dma((7,)),
            dma((11,)),
        ],
        compiler_params=pltpu.CompilerParams(
            collective_id=1, has_side_effects=True, vmem_limit_bytes=LAYER_VMEM * 2**20
        ),
        name="layer",
    )(total, scales, local, w_neigh, head, labels)


def unpack_kernel(whole, self_ref, neigh_ref, bias_ref, head_ref):
    for i, ref in enumerate((self_ref, neigh_ref)):
        for side in range(2):
            ref[:, 128 * side:128 * side + 128] = whole[pl.ds(512 * i + 256 * side, 256), :]
    for i in range(4):
        ref = (bias_ref, head_ref)[i // 2]
        ref[128 * (i % 2):128 * (i % 2) + 128] = whole[1024 + i, :]


def unpack(whole):
    vmem = pl.BlockSpec(memory_space=pltpu.VMEM)
    return pl.pallas_call(
        unpack_kernel,
        out_shape=(
            jax.ShapeDtypeStruct((256, 256), F32),
            jax.ShapeDtypeStruct((256, 256), F32),
            jax.ShapeDtypeStruct((256,), F32),
            jax.ShapeDtypeStruct((256,), F32),
        ),
        in_specs=[vmem],
        out_specs=(vmem,) * 4,
        compiler_params=pltpu.CompilerParams(vmem_limit_bytes=4 * 2**20),
        name="unpack",
    )(whole)


def on_device(
    features,
    w_self,
    w_neigh,
    bias,
    w_head,
    tile_weights,
    tile_dst,
    tile_src,
    tile_count,
    hub_block,
    send_rows,
    send_count,
    labels,
):
    width = features.shape[1]
    blocks = features.shape[0] // 128
    vertex_total = features.shape[0] * lax.axis_size(("vert", "row"))
    loss_scale = 1.0 / math.sqrt(vertex_total)
    table, local, weights, sums = gather(
        hub_block, send_rows[0].T, send_count, features.reshape(blocks, 128, width), tile_weights,
        w_self, bias.reshape(1, width),
    )
    total, scales = add_tiles(tile_dst, tile_src, tile_count, table, local, weights, sums, blocks)
    return unpack(layer(loss_scale, total, scales, local, w_neigh, w_head.reshape(1, width), labels.reshape(blocks, 128)))


def solution(mesh):
    in_specs = (
        P(("vert", "row"), None),
        P(),
        P(),
        P(),
        P(),
        P(("vert", "row"), None, None),
        P(("vert", "row")),
        P(("vert", "row")),
        P(("vert", "row")),
        P(("vert", "row")),
        P(("vert", "row"), None, None),
        P(("vert", "row"), None),
        P(("vert", "row")),
    )
    out_specs = (P(), P(), P(), P())
    return jax.shard_map(
        on_device, mesh=mesh, in_specs=in_specs, out_specs=out_specs, check_vma=False
    )
```

```python
import functools
import math

import jax
import jax.numpy as jnp
from jax import lax
from jax.experimental import pallas as pl
from jax.experimental.pallas import tpu as pltpu
from jax.sharding import PartitionSpec as P

MESH = pl.DeviceIdType.MESH
BF16 = jnp.bfloat16
F32 = jnp.float32

PART_START = (0, 88, 176)
PART_ROWS = (88, 88, 80)
PART_HALF = (48, 40, 40)
PART_AXES = ("xyz", "yzx", "zxy")
OFFSETS = (0, 3, 1, 2)


def my_place():
    vert = lax.axis_index("vert")
    row = lax.axis_index("row")
    core = lax.rem(vert, 2)
    x = lax.rem(lax.div(vert, 2), 4)
    y = lax.rem(lax.div(vert, 8), 2) * 2 + row
    z = lax.div(vert, 16)
    return {"x": x, "y": y, "z": z}, core


def device_at(place, core):
    x, y, z = place["x"], place["y"], place["z"]
    vert = ((z * 2 + lax.div(y, 2)) * 4 + x) * 2 + core
    return (vert, lax.rem(y, 2))


def shifted(place, axis, step):
    moved = dict(place)
    moved[axis] = lax.rem(place[axis] + step, 4)
    return moved


def split(value):
    high = value.astype(BF16)
    low = (value - high.astype(F32)).astype(BF16)
    return high, low


def dot(a, b, dims=(((1,), (0,)), ((), ()))):
    return lax.dot_general(a, b, dims, preferred_element_type=F32)


GATHER_VMEM, TILES_VMEM, LAYER_VMEM = 20, 12, 20
CHUNK = 256
TILE_CHUNK = 8
TILE_SLOTS = 4


def gather_kernel(
    hub_block_ref, rows_hbm, count_hbm, feat_hbm, weights_hbm, self_hbm, bias_hbm,
    table_ref, local_ref, split_ref, sums_ref,
    rows_ref, count_ref, w_self_ref, bias_ref, small_sem, hub, self_k, ring, outbox, inbox,
    own_sem, feat_sem, ring_sem, recv1, recv2, recv3, send1, send2, send3, pair_send, pair_recv,
    border_send, border_recv,
):
    place, core = my_place()
    x, y, z = place["x"], place["y"], place["z"]
    near = {}
    for axis in "xyz":
        for step in (1, 3):
            near[axis, step] = device_at(shifted(place, axis, step), core)
    sibling = device_at(place, 1 - core)
    me = lax.axis_index("vert") * 2 + lax.axis_index("row")

    def other(step):
        number = lax.rem(me + step, 128)
        return number, (lax.div(number, 2), lax.rem(number, 2))

    small_loads = [
        pltpu.make_async_copy(src, dst, small_sem.at[i])
        for i, (src, dst) in enumerate((
            (rows_hbm, rows_ref), (count_hbm, count_ref), (self_hbm, w_self_ref), (bias_hbm, bias_ref),
        ))
    ]
    loads = []
    for side in range(2):
        load = pltpu.make_async_copy(
            feat_hbm.at[:, :, pl.ds(128 * side, 128)],
            local_ref.at[pl.ds(0, 32), pl.ds(128 * side, 128), :],
            feat_sem.at[side],
        )
        load.start()
        loads.append(load)

    def load_tiles(i):
        spot = lax.rem(i, TILE_SLOTS)
        return pltpu.make_async_copy(
            weights_hbm.at[pl.ds(i * TILE_CHUNK, TILE_CHUNK)], ring.at[spot], ring_sem.at[spot]
        )

    for load in small_loads:
        load.start()
    for i in range(TILE_SLOTS):
        load_tiles(i).start()

    barrier = pltpu.get_barrier_semaphore()

    @pl.loop(1, 128)
    def _(step):
        pl.semaphore_signal(barrier, inc=1, device_id=other(step)[1], device_id_type=MESH)


    for load in loads:
        load.wait()
    hub[...] = local_ref[hub_block_ref[0]]
    for load in small_loads:
        load.wait()
    own = pltpu.make_async_copy(hub, table_ref.at[core, z, y, x], own_sem)
    own.start()
    pl.semaphore_wait(barrier, 127)

    def slot(part, where, half=None):
        start, rows = PART_START[part], PART_ROWS[part]
        if half == 0:
            rows = PART_HALF[part]
        elif half == 1:
            start, rows = start + PART_HALF[part], rows - PART_HALF[part]
        at = []
        for axis in "zyx":
            offset = where.get(axis, 0)
            at.append(pl.ds(0, 4) if offset == "all" else lax.rem(place[axis] + offset, 4))
        return table_ref.at[(core, *at, pl.ds(start, rows), slice(None))]

    def remote(src, dst, send_sem, recv_sem, target):
        return pltpu.make_async_remote_copy(
            src_ref=src, dst_ref=dst, send_sem=send_sem, recv_sem=recv_sem,
            device_id=target, device_id_type=MESH,
        )

    def send_both(part, where, axis, send_sem, recv):
        dst = slot(part, where)
        src = dst if where else hub.at[pl.ds(PART_START[part], PART_ROWS[part])]
        remote(src, dst, send_sem, recv.at[0], near[axis, 1]).start()
        remote(src, dst, send_sem, recv.at[1], near[axis, 3]).start()

    def arrived(part, where, axis, sem, half=None):
        ref = slot(part, where, half)
        remote(ref, ref, sem, sem, near[axis, 1]).wait_recv()

    def pass_on(part, where, axis, send_sem, recv, half):
        ref = slot(part, where, half)
        remote(ref, ref, send_sem, recv.at[2 + half], near[axis, 1 if half == 0 else 3]).start()

    def to_sibling(part, where):
        ref = slot(part, where)
        remote(ref, ref, pair_send, pair_recv, sibling).start()

    parts = range(3)

    slot_row = lax.broadcasted_iota(jnp.int32, (8, 128), 0)

    def border_go(first, stop):
        @pl.loop(first, stop)
        def _(step):
            number, target = other(step)
            alive = slot_row < count_ref[0, number]
            for k in range(8):
                row = rows_ref[k, number]
                block = lax.shift_right_logical(row, 7)
                inside = row & 127
                for side in range(2):
                    outbox[number, side, pl.ds(k, 1), :] = local_ref[block, pl.ds(inside + 128 * side, 1), :]
            for side in range(2):
                outbox[number, side] = jnp.where(alive, outbox[number, side], 0.0)
            if first == 128:
                inbox[number] = outbox[number]
            else:
                remote(outbox.at[number], inbox.at[me], border_send, border_recv, target).start()

    def border_end():
        arrived_all = inbox.at[pl.ds(0, 127)]
        pltpu.make_async_copy(arrived_all, arrived_all, border_recv).wait()

        @pl.loop(0, 8)
        def _(i):
            for k in range(16):
                for side in range(2):
                    local_ref[32 + i, 128 * side + 8 * k:128 * side + 8 * k + 8, :] = inbox[16 * i + k, side]

    def pre_chunks(start, stop):
        @pl.loop(start, stop)
        def _(chunk):
            own = []
            for i in range(CHUNK // 128):
                block = local_ref[chunk * (CHUNK // 128) + i]
                own.append(jnp.concatenate([block[0:128], block[128:256]], axis=1))
            high, low = split(jnp.concatenate(own, axis=0))
            value = dot(jnp.concatenate([high, low, high], axis=1), self_k[...]) + bias_ref[...]
            for i in range(CHUNK // 128):
                for side in range(2):
                    local_ref[40 + chunk * (CHUNK // 128) + i, 128 * side:128 * side + 128, :] = value[
                        128 * i:128 * i + 128, 128 * side:128 * side + 128
                    ]

    lane = lax.broadcasted_iota(jnp.int32, (128, 128), 1)

    def tile_chunks(start, stop):
        @pl.loop(start, stop)
        def _(i):
            load_tiles(i).wait()
            spot = lax.rem(i, TILE_SLOTS)
            sums = sums_ref[...]
            for k in range(TILE_CHUNK):
                tile = i * TILE_CHUNK + k
                weight = ring[spot, k]
                high, low = split(weight)
                split_ref[tile, :, 0:128] = high
                split_ref[tile, :, 128:256] = low
                sums = jnp.where(lane == tile, jnp.sum(weight, axis=1, keepdims=True), sums)
            sums_ref[...] = sums

            @pl.when(i + TILE_SLOTS < 128 // TILE_CHUNK)
            def _():
                load_tiles(i + TILE_SLOTS).start()

    for p in parts:
        first, second, _ = PART_AXES[p]
        send_both(p, {}, first, send1.at[p], recv1.at[p])
        send_both(p, {}, second, send2.at[p], recv2.at[p, 0])

    sums_ref[...] = jnp.zeros_like(sums_ref)
    border_go(1, 65)
    own.wait()
    for side, offset in ((0, 3), (1, 1)):
        unit = OFFSETS.index(offset)
        for p in parts:
            first, second, _ = PART_AXES[p]
            where = {first: offset}
            arrived(p, where, first, recv1.at[p, side])
            pass_on(p, where, first, send1.at[p], recv1.at[p], side)
            send_both(p, where, second, send2.at[p], recv2.at[p, unit])
    border_go(65, 128)
    border_go(128, 129)
    for p in parts:
        first, second, third = PART_AXES[p]
        where = {first: 2}
        arrived(p, where, first, recv1.at[p, 2], 0)
        arrived(p, where, first, recv1.at[p, 3], 1)
        send_both(p, where, second, send2.at[p], recv2.at[p, 3])
        line = {first: "all"}
        send_both(p, line, third, send3.at[p], recv3.at[p, 0])
        to_sibling(p, line)
    self_high, self_low = split(w_self_ref[...])
    self_k[0:256, :] = self_high
    self_k[256:512, :] = self_high
    self_k[512:768, :] = self_low

    for unit in range(4):
        for side, offset in ((0, 3), (1, 1)):
            for p in parts:
                first, second, _ = PART_AXES[p]
                where = {first: OFFSETS[unit], second: offset}
                arrived(p, where, second, recv2.at[p, unit, side])
                pass_on(p, where, second, send2.at[p], recv2.at[p, unit], side)
    for side, offset in ((0, 3), (1, 1)):
        for p in parts:
            first, second, third = PART_AXES[p]
            line = {first: "all", second: offset}
            send_both(p, line, third, send3.at[p], recv3.at[p, 1 + side])
            to_sibling(p, line)
    for p in parts:
        first, second, third = PART_AXES[p]
        for unit in range(4):
            where = {first: OFFSETS[unit], second: 2}
            arrived(p, where, second, recv2.at[p, unit, 2], 0)
            arrived(p, where, second, recv2.at[p, unit, 3], 1)
        line = {first: "all", second: 2}
        send_both(p, line, third, send3.at[p], recv3.at[p, 3])
        to_sibling(p, line)

    for unit in range(4):
        pre_chunks(4 * unit, 4 * unit + 4)
        for side, offset in ((0, 3), (1, 1)):
            for p in parts:
                first, second, third = PART_AXES[p]
                line = {first: "all", second: OFFSETS[unit], third: offset}
                arrived(p, line, third, recv3.at[p, unit, side])
                pass_on(p, line, third, send3.at[p], recv3.at[p, unit], side)
                to_sibling(p, line)
        if unit < 2:
            tile_chunks(8 * unit, 8 * unit + 8)
        if unit == 2:
            border_end()
    for unit in range(4):
        for p in parts:
            first, second, third = PART_AXES[p]
            line = {first: "all", second: OFFSETS[unit], third: 2}
            arrived(p, line, third, recv3.at[p, unit, 2], 0)
            arrived(p, line, third, recv3.at[p, unit, 3], 1)
            to_sibling(p, line)

    for p in parts:
        rows = pl.ds(PART_START[p], PART_ROWS[p])
        for sem, ref in (
            (send1.at[p], table_ref.at[core, 0, 0, pl.ds(0, 3), rows, :]),
            (send2.at[p], table_ref.at[core, 0, pl.ds(0, 3), pl.ds(0, 4), rows, :]),
            (send3.at[p], table_ref.at[core, pl.ds(0, 3), pl.ds(0, 4), pl.ds(0, 4), rows, :]),
        ):
            pltpu.make_async_copy(ref, ref, sem).wait()
    sent = outbox.at[pl.ds(0, 127)]
    pltpu.make_async_copy(sent, sent, border_send).wait()
    mine, theirs = table_ref.at[core], table_ref.at[1 - core]
    pltpu.make_async_copy(mine, mine, pair_send).wait()
    pltpu.make_async_copy(theirs, theirs, pair_recv).wait()


def gather(hub_block, send_rows, send_count, features, weights, w_self, bias):
    dma = pltpu.SemaphoreType.DMA
    smem = pl.BlockSpec(memory_space=pltpu.SMEM)
    vmem = pl.BlockSpec(memory_space=pltpu.VMEM)
    hbm = pl.BlockSpec(memory_space=pl.ANY)
    far = pl.BlockSpec(memory_space=pltpu.HBM)
    border = pltpu.VMEM((128, 2, 8, 128), F32)
    pin = functools.partial(pltpu.with_memory_space_constraint, memory_space=pltpu.HBM)
    return pl.pallas_call(
        gather_kernel,
        out_shape=(
            pltpu.VMEM((2, 4, 4, 4, 256, 128), F32),
            pltpu.VMEM((72, 256, 128), F32),
            pltpu.VMEM((128, 128, 256), BF16),
            pltpu.VMEM((128, 128), F32),
        ),
        in_specs=[smem] + [far] * 2 + [hbm] * 2 + [far] * 2,
        out_specs=(vmem,) * 4,
        scratch_shapes=[
            pltpu.SMEM(send_rows.shape, jnp.int32),
            pltpu.SMEM(send_count.shape, jnp.int32),
            pltpu.VMEM(w_self.shape, F32),
            pltpu.VMEM(bias.shape, F32),
            dma((4,)),
            pltpu.VMEM((256, 128), F32),
            pltpu.VMEM((768, 256), BF16),
            pltpu.VMEM((TILE_SLOTS, TILE_CHUNK, 128, 128), F32),
            border, border,
            dma, dma((2,)), dma((TILE_SLOTS,)), dma((3, 4)), dma((3, 4, 4)), dma((3, 4, 4)),
            dma((3,)), dma((3,)), dma((3,)), dma, dma,
            dma, dma,
        ],
        compiler_params=pltpu.CompilerParams(
            collective_id=0, has_side_effects=True, vmem_limit_bytes=GATHER_VMEM * 2**20
        ),
        name="gather",
    )(hub_block, pin(send_rows), pin(send_count), features, weights, pin(w_self), pin(bias))


GROUP = 4


def tiles_kernel(
    dst_ref, src_ref, count_ref,
    table_ref, local_ref, split_ref, sums_ref, dst_row_ref,
    total, scales_ref,
    near_tiles, hub_tiles,
):
    tiles = split_ref.shape[0]
    blocks = total.shape[0] - 1
    first_hub = blocks + 8
    count = count_ref[0]

    total[...] = jnp.zeros_like(total)

    def sort_tile(tile, ends):
        near = jnp.where(src_ref[tile] < first_hub, 1, 0)
        for listed, end in zip((near_tiles, hub_tiles), ends):
            listed[end] = tile
        return ends[0] + near, ends[1] + (1 - near)

    amounts = lax.fori_loop(0, count, sort_tile, (0, 0))

    def wide(block):
        return jnp.concatenate([block[0:128], block[128:256]], axis=1)

    def near_source(src):
        return wide(local_ref[src])

    def hub_source(src):
        number = src - first_hub
        return wide(table_ref[
            lax.shift_right_logical(number, 1) & 1,
            lax.shift_right_logical(number, 5),
            (lax.shift_right_logical(number, 4) & 1) * 2 + (number & 1),
            lax.shift_right_logical(number, 2) & 3,
        ])

    by_lanes = (((1,), (1,)), ((), ()))
    tile_lane = lax.broadcasted_iota(jnp.int32, (blocks, tiles), 1)
    block_row = lax.broadcasted_iota(jnp.int32, (blocks, tiles), 0)
    chosen = (dst_row_ref[...] == block_row) & (tile_lane < count)
    chosen = jnp.where(chosen, 1.0, 0.0).astype(BF16)
    sums_high, sums_low = split(sums_ref[...])
    sums_rest = (sums_ref[...] - sums_high.astype(F32) - sums_low.astype(F32)).astype(BF16)
    scales_ref[...] = 1.0 / (
        1.0 + (dot(sums_high, chosen, by_lanes) + dot(sums_low, chosen, by_lanes) + dot(sums_rest, chosen, by_lanes))
    )

    work = ((near_tiles, near_source), (hub_tiles, hub_source))
    for (listed, source), amount in zip(work, amounts):
        @pl.loop(0, lax.div(amount + (GROUP - 1), GROUP))
        def _(group):
            products, targets = [], []
            for k in range(GROUP):
                at = group * GROUP + k
                tile = listed[jnp.minimum(at, amount - 1)]
                targets.append(jnp.where(at < amount, dst_ref[tile], blocks))
                weight = split_ref[tile]
                high, low = split(source(src_ref[tile]))
                products.append(
                    dot(
                        jnp.concatenate([weight, weight[:, 0:128]], axis=1),
                        jnp.concatenate([high, high, low], axis=0),
                    )
                )
            for k in range(GROUP):
                total[targets[k]] += products[k]


def add_tiles(dst, src, count, table, local, weights, sums, blocks):
    smem = pl.BlockSpec(memory_space=pltpu.SMEM)
    vmem = pl.BlockSpec(memory_space=pltpu.VMEM)
    listed = pltpu.SMEM((dst.shape[0] + 1,), jnp.int32)
    return pl.pallas_call(
        tiles_kernel,
        out_shape=(pltpu.VMEM((blocks + 1, 128, 256), F32), pltpu.VMEM((128, blocks), F32)),
        in_specs=[smem] * 3 + [vmem] * 5,
        out_specs=(vmem, vmem),
        scratch_shapes=[
            listed, listed,
        ],
        compiler_params=pltpu.CompilerParams(vmem_limit_bytes=TILES_VMEM * 2**20),
        name="add_tiles",
    )(dst, src, count, *(pltpu.with_memory_space_constraint(v, pltpu.VMEM) for v in (table, local, weights)), sums, dst.reshape(1, -1))


LAYER_CHUNK = 1024


def layer_kernel(
    loss_scale, total, scales_ref, local_ref, w_neigh_ref, head_ref, labels_ref,
    whole,
    neigh_k, grad_self, grad_neigh, grad_small, grads, pair_in, lots_in, small_in,
    send_sem, recv_sem,
):
    place, core = my_place()
    number = (place["z"] * 4 + place["y"]) * 4 + place["x"]
    sibling = device_at(place, 1 - core)

    def peer(step):
        other = lax.rem(number + step, 64)
        at = {"x": lax.rem(other, 4), "y": lax.rem(lax.div(other, 4), 4), "z": lax.div(other, 16)}
        return other, device_at(at, core)

    barrier = pltpu.get_barrier_semaphore()
    pl.semaphore_signal(barrier, inc=1, device_id=sibling, device_id_type=MESH)

    @pl.loop(1, 64)
    def _(step):
        pl.semaphore_signal(barrier, inc=1, device_id=peer(step)[1], device_id_type=MESH)

    blocks = labels_ref.shape[0]
    neigh_high, neigh_low = split(w_neigh_ref[...])
    neigh_k[0:256, :] = neigh_high
    neigh_k[256:512, :] = neigh_high
    neigh_k[512:768, :] = neigh_low
    target_columns = (2.0 * labels_ref[...].astype(F32) - 1.0).T
    lane = lax.broadcasted_iota(jnp.int32, target_columns.shape, 1)
    grad_self[...] = jnp.zeros_like(grad_self)
    grad_neigh[...] = jnp.zeros_like(grad_neigh)
    grad_small[...] = jnp.zeros_like(grad_small)
    per_chunk = LAYER_CHUNK // 128

    def wide(block):
        return jnp.concatenate([block[0:128], block[128:256]], axis=1)

    @pl.loop(0, blocks // per_chunk)
    def _(chunk):
        own, mean, target, pre = [], [], [], []
        for i in range(per_chunk):
            b = chunk * per_chunk + i
            block = wide(local_ref[b])
            scale = jnp.sum(jnp.where(lane == b, scales_ref[...], 0.0), axis=1, keepdims=True)
            own.append(block)
            pre.append(wide(local_ref[blocks + 8 + b]))
            mean.append((block + total[b]) * scale)
            target.append(jnp.sum(jnp.where(lane == b, target_columns, 0.0), axis=1, keepdims=True))
        own, mean, target, pre = (jnp.concatenate(v, axis=0) for v in (own, mean, target, pre))
        own_high, own_low = split(own)
        mean_high, mean_low = split(mean)
        pre = pre + dot(jnp.concatenate([mean_high, mean_low, mean_high], axis=1), neigh_k[...])
        gate = jax.nn.sigmoid(pre)
        hidden = pre * gate
        score = jnp.sum(hidden * head_ref[...], axis=1, keepdims=True)
        dscore = (score - target) * loss_scale
        dpre = dscore * head_ref[...] * (gate * (1.0 + pre * (1.0 - gate)))
        d_high, d_low = split(dpre)
        by_rows = (((0,), (0,)), ((), ()))
        right = jnp.concatenate([d_high, d_high, d_low], axis=0)
        grad_self[...] += dot(jnp.concatenate([own_high, own_low, own_high], axis=0), right, by_rows)
        grad_neigh[...] += dot(jnp.concatenate([mean_high, mean_low, mean_high], axis=0), right, by_rows)
        grad_small[0:1, :] += jnp.sum(dpre, axis=0, keepdims=True)
        grad_small[1:2, :] += jnp.sum(hidden * dscore, axis=0, keepdims=True)

    for i, ref in enumerate((grad_self, grad_neigh)):
        for side in range(2):
            grads[pl.ds(512 * i + 256 * side, 256), :] = ref[:, 128 * side:128 * side + 128]
    grads[1024:1032, :] = jnp.zeros((8, 128), F32)
    for i in range(4):
        side = 128 * (i % 2)
        grads[1024 + i:1025 + i, :] = grad_small[i // 2:i // 2 + 1, side:side + 128]

    pl.semaphore_wait(barrier, 64)

    def send(stage, src, dst, target):
        pltpu.make_async_remote_copy(
            src_ref=src, dst_ref=dst, send_sem=send_sem.at[stage], recv_sem=recv_sem.at[stage],
            device_id=target, device_id_type=MESH,
        ).start()

    def received(stage, ref):
        pltpu.make_async_copy(ref, ref, recv_sem.at[stage]).wait()

    def sent(stage, ref):
        pltpu.make_async_copy(ref, ref, send_sem.at[stage]).wait()

    half, other_half = core * 512, (1 - core) * 512
    small = pl.ds(1024, 8)
    send(0, grads.at[pl.ds(other_half, 512)], pair_in.at[pl.ds(0, 512)], sibling)
    send(0, grads.at[small], pair_in.at[pl.ds(512, 8)], sibling)
    received(0, pair_in)
    pair_in[0:512, :] += grads[pl.ds(half, 512), :]
    pair_in[512:520, :] += grads[1024:1032, :]

    def lot(other):
        return pl.ds(pl.multiple_of(other * 8, 8), 8)

    first = (core == 0) & (number == 0)
    feeds_first = (core == 0) & (number != 0)

    @pl.when(feeds_first)
    def _():
        send(4, pair_in.at[pl.ds(512, 8)], small_in.at[number], device_at({"x": 0, "y": 0, "z": 0}, core))

    @pl.loop(1, 64)
    def _(step):
        other, target = peer(step)
        send(1, pair_in.at[lot(other)], lots_in.at[number], target)

    lots_in[number] = pair_in[lot(number), :]
    received(1, lots_in.at[pl.ds(0, 63)])
    mine = pl.ds(pl.multiple_of(half + number * 8, 8), 8)
    whole[mine, :] = jnp.sum(lots_in[...], axis=0)

    def from_plane(z):
        return recv_sem.at[7 + z]

    @pl.loop(1, 64)
    def _(step):
        pltpu.make_async_remote_copy(
            src_ref=whole.at[mine], dst_ref=whole.at[mine], send_sem=send_sem.at[2],
            recv_sem=from_plane(place["z"]), device_id=peer(step)[1], device_id_type=MESH,
        ).start()

    @pl.when(first)
    def _():
        small_in[0] = pair_in[512:520, :]
        received(4, small_in.at[pl.ds(0, 63)])
        whole[1024:1032, :] = jnp.sum(small_in[...], axis=0)

        @pl.loop(1, 64)
        def _(step):
            send(5, whole.at[small], whole.at[small], peer(step)[1])

    for step in (0, 1, 3, 2):
        z = lax.rem(place["z"] + step, 4)
        amount = whole.at[pl.ds(0, 128 if step else 120)]
        pltpu.make_async_copy(amount, amount, from_plane(z)).wait()
        plane = pl.ds(pl.multiple_of(half + z * 128, 128), 128)
        send(3, whole.at[plane], whole.at[plane], sibling)

    @pl.when(feeds_first)
    def _():
        received(5, whole.at[small])

    @pl.when(core == 0)
    def _():
        send(6, whole.at[small], whole.at[small], sibling)

    @pl.when(core == 1)
    def _():
        received(6, whole.at[small])

    received(3, whole.at[pl.ds(0, 512)])
    sent(0, pair_in)
    sent(1, lots_in.at[pl.ds(0, 63)])
    sent(2, whole.at[pl.ds(0, 504)])
    sent(3, whole.at[pl.ds(0, 512)])

    @pl.when(feeds_first)
    def _():
        sent(4, small_in.at[0])

    @pl.when(first)
    def _():
        sent(5, small_in.at[pl.ds(0, 63)])

    @pl.when(core == 0)
    def _():
        sent(6, whole.at[small])


def layer(loss_scale, total, scales, local, w_neigh, head, labels):
    vmem = pl.BlockSpec(memory_space=pltpu.VMEM)
    dma = pltpu.SemaphoreType.DMA
    width = w_neigh.shape[0]
    return pl.pallas_call(
        functools.partial(layer_kernel, loss_scale),
        out_shape=pltpu.VMEM((1032, 128), F32),
        in_specs=[vmem] * 6,
        out_specs=vmem,
        scratch_shapes=[
            pltpu.VMEM((3 * width, width), BF16),
            pltpu.VMEM((width, width), F32),
            pltpu.VMEM((width, width), F32),
            pltpu.VMEM((8, width), F32),
            pltpu.VMEM((1032, 128), F32),
            pltpu.VMEM((520, 128), F32),
            pltpu.VMEM((64, 8, 128), F32),
            pltpu.VMEM((64, 8, 128), F32),
            dma((7,)),
            dma((11,)),
        ],
        compiler_params=pltpu.CompilerParams(
            collective_id=1, has_side_effects=True, vmem_limit_bytes=LAYER_VMEM * 2**20
        ),
        name="layer",
    )(total, scales, local, w_neigh, head, labels)


def unpack_kernel(whole, self_ref, neigh_ref, bias_ref, head_ref):
    for i, ref in enumerate((self_ref, neigh_ref)):
        for side in range(2):
            ref[:, 128 * side:128 * side + 128] = whole[pl.ds(512 * i + 256 * side, 256), :]
    for i in range(4):
        ref = (bias_ref, head_ref)[i // 2]
        ref[128 * (i % 2):128 * (i % 2) + 128] = whole[1024 + i, :]


def unpack(whole):
    vmem = pl.BlockSpec(memory_space=pltpu.VMEM)
    return pl.pallas_call(
        unpack_kernel,
        out_shape=(
            jax.ShapeDtypeStruct((256, 256), F32),
            jax.ShapeDtypeStruct((256, 256), F32),
            jax.ShapeDtypeStruct((256,), F32),
            jax.ShapeDtypeStruct((256,), F32),
        ),
        in_specs=[vmem],
        out_specs=(vmem,) * 4,
        compiler_params=pltpu.CompilerParams(vmem_limit_bytes=4 * 2**20),
        name="unpack",
    )(whole)


def on_device(
    features,
    w_self,
    w_neigh,
    bias,
    w_head,
    tile_weights,
    tile_dst,
    tile_src,
    tile_count,
    hub_block,
    send_rows,
    send_count,
    labels,
):
    width = features.shape[1]
    blocks = features.shape[0] // 128
    vertex_total = features.shape[0] * lax.axis_size(("vert", "row"))
    loss_scale = 1.0 / math.sqrt(vertex_total)
    table, local, weights, sums = gather(
        hub_block, send_rows[0].T, send_count, features.reshape(blocks, 128, width), tile_weights,
        w_self, bias.reshape(1, width),
    )
    total, scales = add_tiles(tile_dst, tile_src, tile_count, table, local, weights, sums, blocks)
    return unpack(layer(loss_scale, total, scales, local, w_neigh, w_head.reshape(1, width), labels.reshape(blocks, 128)))


def solution(mesh):
    in_specs = (
        P(("vert", "row"), None),
        P(),
        P(),
        P(),
        P(),
        P(("vert", "row"), None, None),
        P(("vert", "row")),
        P(("vert", "row")),
        P(("vert", "row")),
        P(("vert", "row")),
        P(("vert", "row"), None, None),
        P(("vert", "row"), None),
        P(("vert", "row")),
    )
    out_specs = (P(), P(), P(), P())
    return jax.shard_map(
        on_device, mesh=mesh, in_specs=in_specs, out_specs=out_specs, check_vma=False
    )
```

```python
import functools
import itertools
import math

import jax
import jax.numpy as jnp
from jax import lax
from jax.experimental import pallas as pl
from jax.experimental.pallas import tpu as pltpu
from jax.sharding import PartitionSpec as P

MESH = pl.DeviceIdType.MESH
BF16 = jnp.bfloat16
F32 = jnp.float32

PART_START = (0, 88, 176)
PART_ROWS = (88, 88, 80)
PART_HALF = (48, 40, 40)
PART_AXES = ("xyz", "yzx", "zxy")
OFFSETS = (0, 3, 1, 2)


def my_place():
    vert = lax.axis_index("vert")
    row = lax.axis_index("row")
    core = lax.rem(vert, 2)
    x = lax.rem(lax.div(vert, 2), 4)
    y = lax.rem(lax.div(vert, 8), 2) * 2 + row
    z = lax.div(vert, 16)
    return {"x": x, "y": y, "z": z}, core


def device_at(place, core):
    x, y, z = place["x"], place["y"], place["z"]
    vert = ((z * 2 + lax.div(y, 2)) * 4 + x) * 2 + core
    return (vert, lax.rem(y, 2))


def shifted(place, axis, step):
    moved = dict(place)
    moved[axis] = lax.rem(place[axis] + step, 4)
    return moved


def split(value):
    high = value.astype(BF16)
    low = (value - high.astype(F32)).astype(BF16)
    return high, low


def dot(a, b, dims=(((1,), (0,)), ((), ()))):
    return lax.dot_general(a, b, dims, preferred_element_type=F32)


GATHER_VMEM, TILES_VMEM, LAYER_VMEM = 20, 12, 20
CHUNK = 256
TILE_CHUNK = 8
TILE_SLOTS = 4


def gather_kernel(
    hub_block_ref, rows_hbm, count_hbm, feat_hbm, weights_hbm, self_hbm, bias_hbm,
    table_ref, local_ref, split_ref, sums_ref,
    rows_ref, count_ref, w_self_ref, bias_ref, small_sem, hub, self_k, ring, outbox, inbox,
    own_sem, feat_sem, ring_sem, recv1, recv2, recv3, send1, send2, send3, pair_send, pair_recv,
    border_send, border_recv,
):
    place, core = my_place()
    x, y, z = place["x"], place["y"], place["z"]
    near = {}
    for axis in "xyz":
        for step in (1, 3):
            near[axis, step] = device_at(shifted(place, axis, step), core)
    sibling = device_at(place, 1 - core)
    me = lax.axis_index("vert") * 2 + lax.axis_index("row")

    def other(step):
        number = lax.rem(me + step, 128)
        return number, (lax.div(number, 2), lax.rem(number, 2))

    small_loads = [
        pltpu.make_async_copy(src, dst, small_sem.at[i])
        for i, (src, dst) in enumerate((
            (rows_hbm, rows_ref), (count_hbm, count_ref), (self_hbm, w_self_ref), (bias_hbm, bias_ref),
        ))
    ]
    loads = []
    for side in range(2):
        load = pltpu.make_async_copy(
            feat_hbm.at[:, :, pl.ds(128 * side, 128)],
            local_ref.at[pl.ds(0, 32), pl.ds(128 * side, 128), :],
            feat_sem.at[side],
        )
        load.start()
        loads.append(load)

    def load_tiles(i):
        spot = lax.rem(i, TILE_SLOTS)
        return pltpu.make_async_copy(
            weights_hbm.at[pl.ds(i * TILE_CHUNK, TILE_CHUNK)], ring.at[spot], ring_sem.at[spot]
        )

    for load in small_loads:
        load.start()
    for i in range(TILE_SLOTS):
        load_tiles(i).start()

    barrier = pltpu.get_barrier_semaphore()

    @pl.loop(1, 128)
    def _(step):
        pl.semaphore_signal(barrier, inc=1, device_id=other(step)[1], device_id_type=MESH)


    for load in loads:
        load.wait()
    hub[...] = local_ref[hub_block_ref[0]]
    for load in small_loads:
        load.wait()
    own = pltpu.make_async_copy(hub, table_ref.at[core, z, y, x], own_sem)
    own.start()
    pl.semaphore_wait(barrier, 127)

    def slot(part, where, half=None):
        start, rows = PART_START[part], PART_ROWS[part]
        if half == 0:
            rows = PART_HALF[part]
        elif half == 1:
            start, rows = start + PART_HALF[part], rows - PART_HALF[part]
        at = []
        for axis in "zyx":
            offset = where.get(axis, 0)
            at.append(pl.ds(0, 4) if offset == "all" else lax.rem(place[axis] + offset, 4))
        return table_ref.at[(core, *at, pl.ds(start, rows), slice(None))]

    def remote(src, dst, send_sem, recv_sem, target):
        return pltpu.make_async_remote_copy(
            src_ref=src, dst_ref=dst, send_sem=send_sem, recv_sem=recv_sem,
            device_id=target, device_id_type=MESH,
        )

    def send_both(part, where, axis, send_sem, recv):
        dst = slot(part, where)
        src = dst if where else hub.at[pl.ds(PART_START[part], PART_ROWS[part])]
        remote(src, dst, send_sem, recv.at[0], near[axis, 1]).start()
        remote(src, dst, send_sem, recv.at[1], near[axis, 3]).start()

    def arrived(part, where, axis, sem, half=None):
        ref = slot(part, where, half)
        remote(ref, ref, sem, sem, near[axis, 1]).wait_recv()

    def pass_on(part, where, axis, send_sem, recv, half):
        ref = slot(part, where, half)
        remote(ref, ref, send_sem, recv.at[2 + half], near[axis, 1 if half == 0 else 3]).start()

    def to_sibling(part, where):
        ref = slot(part, where)
        remote(ref, ref, pair_send, pair_recv, sibling).start()

    parts = range(3)

    slot_row = lax.broadcasted_iota(jnp.int32, (8, 128), 0)

    def border_go(first, stop):
        @pl.loop(first, stop)
        def _(step):
            number, target = other(step)
            alive = slot_row < count_ref[0, number]
            for k in range(8):
                row = rows_ref[k, number]
                block = lax.shift_right_logical(row, 7)
                inside = row & 127
                for side in range(2):
                    outbox[number, side, pl.ds(k, 1), :] = local_ref[block, pl.ds(inside + 128 * side, 1), :]
            for side in range(2):
                outbox[number, side] = jnp.where(alive, outbox[number, side], 0.0)
            if first == 128:
                inbox[number] = outbox[number]
            else:
                remote(outbox.at[number], inbox.at[me], border_send, border_recv, target).start()

    def border_end():
        arrived_all = inbox.at[pl.ds(0, 127)]
        pltpu.make_async_copy(arrived_all, arrived_all, border_recv).wait()

        @pl.loop(0, 8)
        def _(i):
            for k in range(16):
                for side in range(2):
                    local_ref[32 + i, 128 * side + 8 * k:128 * side + 8 * k + 8, :] = inbox[16 * i + k, side]

    def pre_chunks(start, stop):
        @pl.loop(start, stop)
        def _(chunk):
            own = []
            for i in range(CHUNK // 128):
                block = local_ref[chunk * (CHUNK // 128) + i]
                own.append(jnp.concatenate([block[0:128], block[128:256]], axis=1))
            high, low = split(jnp.concatenate(own, axis=0))
            value = dot(jnp.concatenate([high, low, high], axis=1), self_k[...]) + bias_ref[...]
            for i in range(CHUNK // 128):
                for side in range(2):
                    local_ref[40 + chunk * (CHUNK // 128) + i, 128 * side:128 * side + 128, :] = value[
                        128 * i:128 * i + 128, 128 * side:128 * side + 128
                    ]

    lane = lax.broadcasted_iota(jnp.int32, (128, 128), 1)

    def tile_chunks(start, stop):
        @pl.loop(start, stop)
        def _(i):
            load_tiles(i).wait()
            spot = lax.rem(i, TILE_SLOTS)
            sums = sums_ref[...]
            for k in range(TILE_CHUNK):
                tile = i * TILE_CHUNK + k
                weight = ring[spot, k]
                high, low = split(weight)
                split_ref[tile, :, 0:128] = high
                split_ref[tile, :, 128:256] = low
                sums = jnp.where(lane == tile, jnp.sum(weight, axis=1, keepdims=True), sums)
            sums_ref[...] = sums

            @pl.when(i + TILE_SLOTS < 128 // TILE_CHUNK)
            def _():
                load_tiles(i + TILE_SLOTS).start()

    for p in parts:
        first, second, _ = PART_AXES[p]
        send_both(p, {}, first, send1.at[p], recv1.at[p])
        send_both(p, {}, second, send2.at[p], recv2.at[p, 0])

    sums_ref[...] = jnp.zeros_like(sums_ref)
    border_go(1, 65)
    own.wait()
    for side, offset in ((0, 3), (1, 1)):
        unit = OFFSETS.index(offset)
        for p in parts:
            first, second, _ = PART_AXES[p]
            where = {first: offset}
            arrived(p, where, first, recv1.at[p, side])
            pass_on(p, where, first, send1.at[p], recv1.at[p], side)
            send_both(p, where, second, send2.at[p], recv2.at[p, unit])
    border_go(65, 128)
    border_go(128, 129)
    for p in parts:
        first, second, third = PART_AXES[p]
        where = {first: 2}
        arrived(p, where, first, recv1.at[p, 2], 0)
        arrived(p, where, first, recv1.at[p, 3], 1)
        send_both(p, where, second, send2.at[p], recv2.at[p, 3])
        line = {first: "all"}
        send_both(p, line, third, send3.at[p], recv3.at[p, 0])
        to_sibling(p, line)
    self_high, self_low = split(w_self_ref[...])
    self_k[0:256, :] = self_high
    self_k[256:512, :] = self_high
    self_k[512:768, :] = self_low

    for unit in range(4):
        for side, offset in ((0, 3), (1, 1)):
            for p in parts:
                first, second, _ = PART_AXES[p]
                where = {first: OFFSETS[unit], second: offset}
                arrived(p, where, second, recv2.at[p, unit, side])
                pass_on(p, where, second, send2.at[p], recv2.at[p, unit], side)
    for side, offset in ((0, 3), (1, 1)):
        for p in parts:
            first, second, third = PART_AXES[p]
            line = {first: "all", second: offset}
            send_both(p, line, third, send3.at[p], recv3.at[p, 1 + side])
            to_sibling(p, line)
    for p in parts:
        first, second, third = PART_AXES[p]
        for unit in range(4):
            where = {first: OFFSETS[unit], second: 2}
            arrived(p, where, second, recv2.at[p, unit, 2], 0)
            arrived(p, where, second, recv2.at[p, unit, 3], 1)
        line = {first: "all", second: 2}
        send_both(p, line, third, send3.at[p], recv3.at[p, 3])
        to_sibling(p, line)

    for unit in range(4):
        pre_chunks(4 * unit, 4 * unit + 4)
        for side, offset in ((0, 3), (1, 1)):
            for p in parts:
                first, second, third = PART_AXES[p]
                line = {first: "all", second: OFFSETS[unit], third: offset}
                arrived(p, line, third, recv3.at[p, unit, side])
                pass_on(p, line, third, send3.at[p], recv3.at[p, unit], side)
                to_sibling(p, line)
        if unit < 2:
            tile_chunks(8 * unit, 8 * unit + 8)
        if unit == 2:
            border_end()
    for unit in range(4):
        for p in parts:
            first, second, third = PART_AXES[p]
            line = {first: "all", second: OFFSETS[unit], third: 2}
            arrived(p, line, third, recv3.at[p, unit, 2], 0)
            arrived(p, line, third, recv3.at[p, unit, 3], 1)
            to_sibling(p, line)

    for p in parts:
        rows = pl.ds(PART_START[p], PART_ROWS[p])
        for sem, ref in (
            (send1.at[p], table_ref.at[core, 0, 0, pl.ds(0, 3), rows, :]),
            (send2.at[p], table_ref.at[core, 0, pl.ds(0, 3), pl.ds(0, 4), rows, :]),
            (send3.at[p], table_ref.at[core, pl.ds(0, 3), pl.ds(0, 4), pl.ds(0, 4), rows, :]),
        ):
            pltpu.make_async_copy(ref, ref, sem).wait()
    sent = outbox.at[pl.ds(0, 127)]
    pltpu.make_async_copy(sent, sent, border_send).wait()
    mine, theirs = table_ref.at[core], table_ref.at[1 - core]
    pltpu.make_async_copy(mine, mine, pair_send).wait()
    pltpu.make_async_copy(theirs, theirs, pair_recv).wait()


def gather(hub_block, send_rows, send_count, features, weights, w_self, bias):
    dma = pltpu.SemaphoreType.DMA
    smem = pl.BlockSpec(memory_space=pltpu.SMEM)
    vmem = pl.BlockSpec(memory_space=pltpu.VMEM)
    hbm = pl.BlockSpec(memory_space=pl.ANY)
    far = pl.BlockSpec(memory_space=pltpu.HBM)
    border = pltpu.VMEM((128, 2, 8, 128), F32)
    pin = functools.partial(pltpu.with_memory_space_constraint, memory_space=pltpu.HBM)
    return pl.pallas_call(
        gather_kernel,
        out_shape=(
            pltpu.VMEM((2, 4, 4, 4, 256, 128), F32),
            pltpu.VMEM((72, 256, 128), F32),
            pltpu.VMEM((128, 128, 256), BF16),
            pltpu.VMEM((128, 128), F32),
        ),
        in_specs=[smem] + [far] * 2 + [hbm] * 2 + [far] * 2,
        out_specs=(vmem,) * 4,
        scratch_shapes=[
            pltpu.SMEM(send_rows.shape, jnp.int32),
            pltpu.SMEM(send_count.shape, jnp.int32),
            pltpu.VMEM(w_self.shape, F32),
            pltpu.VMEM(bias.shape, F32),
            dma((4,)),
            pltpu.VMEM((256, 128), F32),
            pltpu.VMEM((768, 256), BF16),
            pltpu.VMEM((TILE_SLOTS, TILE_CHUNK, 128, 128), F32),
            border, border,
            dma, dma((2,)), dma((TILE_SLOTS,)), dma((3, 4)), dma((3, 4, 4)), dma((3, 4, 4)),
            dma((3,)), dma((3,)), dma((3,)), dma, dma,
            dma, dma,
        ],
        compiler_params=pltpu.CompilerParams(
            collective_id=0, has_side_effects=True, vmem_limit_bytes=GATHER_VMEM * 2**20
        ),
        name="gather",
    )(hub_block, pin(send_rows), pin(send_count), features, weights, pin(w_self), pin(bias))


GROUP = 16


def tiles_kernel(
    dst_ref, src_ref, count_ref,
    table_ref, local_ref, split_ref, sums_ref, dst_row_ref,
    total, scales_ref,
    near_tiles, hub_tiles,
):
    tiles = split_ref.shape[0]
    blocks = total.shape[0] - 1
    first_hub = blocks + 8
    count = count_ref[0]

    total[...] = jnp.zeros_like(total)

    def sort_tile(tile, ends):
        near = jnp.where(src_ref[tile] < first_hub, 1, 0)
        for listed, end in zip((near_tiles, hub_tiles), ends):
            listed[end] = tile
        return ends[0] + near, ends[1] + (1 - near)

    amounts = lax.fori_loop(0, count, sort_tile, (0, 0))

    def wide(block):
        return jnp.concatenate([block[0:128], block[128:256]], axis=1)

    def near_source(src):
        return wide(local_ref[src])

    def hub_source(src):
        number = src - first_hub
        return wide(table_ref[
            lax.shift_right_logical(number, 1) & 1,
            lax.shift_right_logical(number, 5),
            (lax.shift_right_logical(number, 4) & 1) * 2 + (number & 1),
            lax.shift_right_logical(number, 2) & 3,
        ])

    by_lanes = (((1,), (1,)), ((), ()))
    tile_lane = lax.broadcasted_iota(jnp.int32, (blocks, tiles), 1)
    block_row = lax.broadcasted_iota(jnp.int32, (blocks, tiles), 0)
    chosen = (dst_row_ref[...] == block_row) & (tile_lane < count)
    chosen = jnp.where(chosen, 1.0, 0.0).astype(BF16)
    sums_high, sums_low = split(sums_ref[...])
    sums_rest = (sums_ref[...] - sums_high.astype(F32) - sums_low.astype(F32)).astype(BF16)
    scales_ref[...] = 1.0 / (
        1.0 + (dot(sums_high, chosen, by_lanes) + dot(sums_low, chosen, by_lanes) + dot(sums_rest, chosen, by_lanes))
    )

    work = ((near_tiles, near_source), (hub_tiles, hub_source))
    for (listed, source), amount in zip(work, amounts):
        @pl.loop(0, lax.div(amount + (GROUP - 1), GROUP))
        def _(group):
            products, targets = [], []
            for k in range(GROUP):
                at = group * GROUP + k
                tile = listed[jnp.minimum(at, amount - 1)]
                targets.append(jnp.where(at < amount, dst_ref[tile], blocks))
                weight = split_ref[tile]
                high, low = split(source(src_ref[tile]))
                products.append(
                    dot(
                        jnp.concatenate([weight, weight[:, 0:128]], axis=1),
                        jnp.concatenate([high, high, low], axis=0),
                    )
                )
            for k in range(GROUP):
                total[targets[k]] += products[k]


def add_tiles(dst, src, count, table, local, weights, sums, blocks):
    smem = pl.BlockSpec(memory_space=pltpu.SMEM)
    vmem = pl.BlockSpec(memory_space=pltpu.VMEM)
    listed = pltpu.SMEM((dst.shape[0] + 1,), jnp.int32)
    return pl.pallas_call(
        tiles_kernel,
        out_shape=(pltpu.VMEM((blocks + 1, 128, 256), F32), pltpu.VMEM((128, blocks), F32)),
        in_specs=[smem] * 3 + [vmem] * 5,
        out_specs=(vmem, vmem),
        scratch_shapes=[
            listed, listed,
        ],
        compiler_params=pltpu.CompilerParams(vmem_limit_bytes=TILES_VMEM * 2**20),
        name="add_tiles",
    )(dst, src, count, *(pltpu.with_memory_space_constraint(v, pltpu.VMEM) for v in (table, local, weights)), sums, dst.reshape(1, -1))


LAYER_CHUNK = 2048


def layer_kernel(
    loss_scale, total, scales_ref, local_ref, w_neigh_ref, head_ref, labels_ref,
    whole,
    neigh_k, grad_self, grad_neigh, grad_small, grads, pair_in, lots_in, small_in,
    send_sem, recv_sem,
):
    place, core = my_place()
    number = (place["z"] * 4 + place["y"]) * 4 + place["x"]
    sibling = device_at(place, 1 - core)

    away = {
        axis: [lax.rem(place[axis] + step, 4) for step in range(4)] for axis in "xyz"
    }
    along_y = [lax.div(y, 2) * 8 + core for y in away["y"]]
    row_y = [lax.rem(y, 2) for y in away["y"]]
    peers = []
    for dz, dy, dx in itertools.product(range(4), repeat=3):
        if dz + dy + dx:
            vert = away["z"][dz] * 16 + along_y[dy] + away["x"][dx] * 2
            other = away["z"][dz] * 16 + away["y"][dy] * 4 + away["x"][dx]
            peers.append((other, (vert, row_y[dy])))

    barrier = pltpu.get_barrier_semaphore()
    pl.semaphore_signal(barrier, inc=1, device_id=sibling, device_id_type=MESH)

    for _, target in peers:
        pl.semaphore_signal(barrier, inc=1, device_id=target, device_id_type=MESH)

    blocks = labels_ref.shape[0]
    neigh_high, neigh_low = split(w_neigh_ref[...])
    neigh_k[0:256, :] = neigh_high
    neigh_k[256:512, :] = neigh_high
    neigh_k[512:768, :] = neigh_low
    target_columns = (2.0 * labels_ref[...].astype(F32) - 1.0).T
    lane = lax.broadcasted_iota(jnp.int32, target_columns.shape, 1)
    grad_self[...] = jnp.zeros_like(grad_self)
    grad_neigh[...] = jnp.zeros_like(grad_neigh)
    grad_small[...] = jnp.zeros_like(grad_small)
    per_chunk = LAYER_CHUNK // 128

    def wide(block):
        return jnp.concatenate([block[0:128], block[128:256]], axis=1)

    @pl.loop(0, blocks // per_chunk)
    def _(chunk):
        own, mean, target, pre = [], [], [], []
        for i in range(per_chunk):
            b = chunk * per_chunk + i
            block = wide(local_ref[b])
            scale = jnp.sum(jnp.where(lane == b, scales_ref[...], 0.0), axis=1, keepdims=True)
            own.append(block)
            pre.append(wide(local_ref[blocks + 8 + b]))
            mean.append((block + total[b]) * scale)
            target.append(jnp.sum(jnp.where(lane == b, target_columns, 0.0), axis=1, keepdims=True))
        own, mean, target, pre = (jnp.concatenate(v, axis=0) for v in (own, mean, target, pre))
        own_high, own_low = split(own)
        mean_high, mean_low = split(mean)
        pre = pre + dot(jnp.concatenate([mean_high, mean_low, mean_high], axis=1), neigh_k[...])
        gate = jax.nn.sigmoid(pre)
        hidden = pre * gate
        score = jnp.sum(hidden * head_ref[...], axis=1, keepdims=True)
        dscore = (score - target) * loss_scale
        dpre = dscore * head_ref[...] * (gate * (1.0 + pre * (1.0 - gate)))
        d_high, d_low = split(dpre)
        by_rows = (((0,), (0,)), ((), ()))
        right = jnp.concatenate([d_high, d_high, d_low], axis=0)
        grad_self[...] += dot(jnp.concatenate([own_high, own_low, own_high], axis=0), right, by_rows)
        grad_neigh[...] += dot(jnp.concatenate([mean_high, mean_low, mean_high], axis=0), right, by_rows)
        grad_small[0:1, :] += jnp.sum(dpre, axis=0, keepdims=True)
        grad_small[1:2, :] += jnp.sum(hidden * dscore, axis=0, keepdims=True)

    for i, ref in enumerate((grad_self, grad_neigh)):
        for side in range(2):
            grads[pl.ds(512 * i + 256 * side, 256), :] = ref[:, 128 * side:128 * side + 128]
    grads[1024:1032, :] = jnp.zeros((8, 128), F32)
    for i in range(4):
        side = 128 * (i % 2)
        grads[1024 + i:1025 + i, :] = grad_small[i // 2:i // 2 + 1, side:side + 128]

    pl.semaphore_wait(barrier, 64)

    def send(stage, src, dst, target):
        pltpu.make_async_remote_copy(
            src_ref=src, dst_ref=dst, send_sem=send_sem.at[stage], recv_sem=recv_sem.at[stage],
            device_id=target, device_id_type=MESH,
        ).start()

    def received(stage, ref):
        pltpu.make_async_copy(ref, ref, recv_sem.at[stage]).wait()

    def sent(stage, ref):
        pltpu.make_async_copy(ref, ref, send_sem.at[stage]).wait()

    half, other_half = core * 512, (1 - core) * 512
    small = pl.ds(1024, 8)
    send(0, grads.at[pl.ds(other_half, 512)], pair_in.at[pl.ds(0, 512)], sibling)
    send(0, grads.at[small], pair_in.at[pl.ds(512, 8)], sibling)
    received(0, pair_in)
    pair_in[0:512, :] += grads[pl.ds(half, 512), :]
    pair_in[512:520, :] += grads[1024:1032, :]

    def lot(other):
        return pl.ds(pl.multiple_of(other * 8, 8), 8)

    first = (core == 0) & (number == 0)
    feeds_first = (core == 0) & (number != 0)

    @pl.when(feeds_first)
    def _():
        send(4, pair_in.at[pl.ds(512, 8)], small_in.at[number], device_at({"x": 0, "y": 0, "z": 0}, core))

    for other, target in peers:
        send(1, pair_in.at[lot(other)], lots_in.at[number], target)

    lots_in[number] = pair_in[lot(number), :]
    received(1, lots_in.at[pl.ds(0, 63)])
    mine = pl.ds(pl.multiple_of(half + number * 8, 8), 8)
    whole[mine, :] = jnp.sum(lots_in[...], axis=0)

    def from_plane(z):
        return recv_sem.at[7 + z]

    for _, target in peers:
        pltpu.make_async_remote_copy(
            src_ref=whole.at[mine], dst_ref=whole.at[mine], send_sem=send_sem.at[2],
            recv_sem=from_plane(place["z"]), device_id=target, device_id_type=MESH,
        ).start()

    @pl.when(first)
    def _():
        small_in[0] = pair_in[512:520, :]
        received(4, small_in.at[pl.ds(0, 63)])
        whole[1024:1032, :] = jnp.sum(small_in[...], axis=0)

        for _, target in peers:
            send(5, whole.at[small], whole.at[small], target)

    for step in (0, 1, 3, 2):
        z = lax.rem(place["z"] + step, 4)
        amount = whole.at[pl.ds(0, 128 if step else 120)]
        pltpu.make_async_copy(amount, amount, from_plane(z)).wait()
        plane = pl.ds(pl.multiple_of(half + z * 128, 128), 128)
        send(3, whole.at[plane], whole.at[plane], sibling)

    @pl.when(feeds_first)
    def _():
        received(5, whole.at[small])

    @pl.when(core == 0)
    def _():
        send(6, whole.at[small], whole.at[small], sibling)

    @pl.when(core == 1)
    def _():
        received(6, whole.at[small])

    received(3, whole.at[pl.ds(0, 512)])
    sent(0, pair_in)
    sent(1, lots_in.at[pl.ds(0, 63)])
    sent(2, whole.at[pl.ds(0, 504)])
    sent(3, whole.at[pl.ds(0, 512)])

    @pl.when(feeds_first)
    def _():
        sent(4, small_in.at[0])

    @pl.when(first)
    def _():
        sent(5, small_in.at[pl.ds(0, 63)])

    @pl.when(core == 0)
    def _():
        sent(6, whole.at[small])


def layer(loss_scale, total, scales, local, w_neigh, head, labels):
    vmem = pl.BlockSpec(memory_space=pltpu.VMEM)
    dma = pltpu.SemaphoreType.DMA
    width = w_neigh.shape[0]
    return pl.pallas_call(
        functools.partial(layer_kernel, loss_scale),
        out_shape=pltpu.VMEM((1032, 128), F32),
        in_specs=[vmem] * 6,
        out_specs=vmem,
        scratch_shapes=[
            pltpu.VMEM((3 * width, width), BF16),
            pltpu.VMEM((width, width), F32),
            pltpu.VMEM((width, width), F32),
            pltpu.VMEM((8, width), F32),
            pltpu.VMEM((1032, 128), F32),
            pltpu.VMEM((520, 128), F32),
            pltpu.VMEM((64, 8, 128), F32),
            pltpu.VMEM((64, 8, 128), F32),
            dma((7,)),
            dma((11,)),
        ],
        compiler_params=pltpu.CompilerParams(
            collective_id=1, has_side_effects=True, vmem_limit_bytes=LAYER_VMEM * 2**20
        ),
        name="layer",
    )(total, scales, local, w_neigh, head, labels)


def unpack_kernel(whole, self_ref, neigh_ref, bias_ref, head_ref):
    for i, ref in enumerate((self_ref, neigh_ref)):
        for side in range(2):
            ref[:, 128 * side:128 * side + 128] = whole[pl.ds(512 * i + 256 * side, 256), :]
    for i in range(4):
        ref = (bias_ref, head_ref)[i // 2]
        ref[128 * (i % 2):128 * (i % 2) + 128] = whole[1024 + i, :]


def unpack(whole):
    vmem = pl.BlockSpec(memory_space=pltpu.VMEM)
    return pl.pallas_call(
        unpack_kernel,
        out_shape=(
            jax.ShapeDtypeStruct((256, 256), F32),
            jax.ShapeDtypeStruct((256, 256), F32),
            jax.ShapeDtypeStruct((256,), F32),
            jax.ShapeDtypeStruct((256,), F32),
        ),
        in_specs=[vmem],
        out_specs=(vmem,) * 4,
        compiler_params=pltpu.CompilerParams(vmem_limit_bytes=4 * 2**20),
        name="unpack",
    )(whole)


def on_device(
    features,
    w_self,
    w_neigh,
    bias,
    w_head,
    tile_weights,
    tile_dst,
    tile_src,
    tile_count,
    hub_block,
    send_rows,
    send_count,
    labels,
):
    width = features.shape[1]
    blocks = features.shape[0] // 128
    vertex_total = features.shape[0] * lax.axis_size(("vert", "row"))
    loss_scale = 1.0 / math.sqrt(vertex_total)
    table, local, weights, sums = gather(
        hub_block, send_rows[0].T, send_count, features.reshape(blocks, 128, width), tile_weights,
        w_self, bias.reshape(1, width),
    )
    total, scales = add_tiles(tile_dst, tile_src, tile_count, table, local, weights, sums, blocks)
    return unpack(layer(loss_scale, total, scales, local, w_neigh, w_head.reshape(1, width), labels.reshape(blocks, 128)))


def solution(mesh):
    in_specs = (
        P(("vert", "row"), None),
        P(),
        P(),
        P(),
        P(),
        P(("vert", "row"), None, None),
        P(("vert", "row")),
        P(("vert", "row")),
        P(("vert", "row")),
        P(("vert", "row")),
        P(("vert", "row"), None, None),
        P(("vert", "row"), None),
        P(("vert", "row")),
    )
    out_specs = (P(), P(), P(), P())
    return jax.shard_map(
        on_device, mesh=mesh, in_specs=in_specs, out_specs=out_specs, check_vma=False
    )
```

```python
import functools
import itertools
import math

import jax
import jax.numpy as jnp
from jax import lax
from jax.experimental import pallas as pl
from jax.experimental.pallas import tpu as pltpu
from jax.sharding import PartitionSpec as P

MESH = pl.DeviceIdType.MESH
BF16 = jnp.bfloat16
F32 = jnp.float32

PART_START = (0, 88, 176)
PART_ROWS = (88, 88, 80)
PART_HALF = (48, 40, 40)
PART_AXES = ("xyz", "yzx", "zxy")
OFFSETS = (0, 3, 1, 2)


def my_place():
    vert = lax.axis_index("vert")
    row = lax.axis_index("row")
    core = lax.rem(vert, 2)
    x = lax.rem(lax.div(vert, 2), 4)
    y = lax.rem(lax.div(vert, 8), 2) * 2 + row
    z = lax.div(vert, 16)
    return {"x": x, "y": y, "z": z}, core


def device_at(place, core):
    x, y, z = place["x"], place["y"], place["z"]
    vert = ((z * 2 + lax.div(y, 2)) * 4 + x) * 2 + core
    return (vert, lax.rem(y, 2))


def shifted(place, axis, step):
    moved = dict(place)
    moved[axis] = lax.rem(place[axis] + step, 4)
    return moved


def split(value):
    high = value.astype(BF16)
    low = (value - high.astype(F32)).astype(BF16)
    return high, low


def dot(a, b, dims=(((1,), (0,)), ((), ()))):
    return lax.dot_general(a, b, dims, preferred_element_type=F32)


GATHER_VMEM, TILES_VMEM, LAYER_VMEM = 20, 12, 20
CHUNK = 256
TILE_CHUNK = 8
TILE_SLOTS = 4


def gather_kernel(
    hub_block_ref, rows_hbm, count_hbm, feat_hbm, weights_hbm, self_hbm, bias_hbm,
    table_ref, local_ref, split_ref, sums_ref,
    rows_ref, count_ref, w_self_ref, bias_ref, small_sem, hub, self_k, ring, outbox, inbox,
    own_sem, feat_sem, ring_sem, recv1, recv2, recv3, send1, send2, send3, pair_send, pair_recv,
    border_send, border_recv, ready,
):
    place, core = my_place()
    x, y, z = place["x"], place["y"], place["z"]
    near = {}
    for axis in "xyz":
        for step in (1, 2, 3):
            near[axis, step] = device_at(shifted(place, axis, step), core)
    sibling = device_at(place, 1 - core)
    me = lax.axis_index("vert") * 2 + lax.axis_index("row")

    def other(step):
        number = lax.rem(me + step, 128)
        return number, (lax.div(number, 2), lax.rem(number, 2))

    small_loads = [
        pltpu.make_async_copy(src, dst, small_sem.at[i])
        for i, (src, dst) in enumerate((
            (rows_hbm, rows_ref), (count_hbm, count_ref), (self_hbm, w_self_ref), (bias_hbm, bias_ref),
        ))
    ]
    loads = []
    for side in range(2):
        load = pltpu.make_async_copy(
            feat_hbm.at[:, :, pl.ds(128 * side, 128)],
            local_ref.at[pl.ds(0, 32), pl.ds(128 * side, 128), :],
            feat_sem.at[side],
        )
        load.start()
        loads.append(load)

    def load_tiles(i):
        spot = lax.rem(i, TILE_SLOTS)
        return pltpu.make_async_copy(
            weights_hbm.at[pl.ds(i * TILE_CHUNK, TILE_CHUNK)], ring.at[spot], ring_sem.at[spot]
        )

    for load in small_loads:
        load.start()
    for i in range(TILE_SLOTS):
        load_tiles(i).start()

    barrier = pltpu.get_barrier_semaphore()
    close = list(near.values()) + [sibling]
    for target in close:
        pl.semaphore_signal(barrier, inc=1, device_id=target, device_id_type=MESH)


    for load in loads:
        load.wait()
    hub[...] = local_ref[hub_block_ref[0]]
    for load in small_loads:
        load.wait()
    own = pltpu.make_async_copy(hub, table_ref.at[core, z, y, x], own_sem)
    own.start()
    pl.semaphore_wait(barrier, len(close))

    def tell(n):
        for target in close:
            pl.semaphore_signal(ready.at[n], inc=1, device_id=target, device_id_type=MESH)

    def hear(n):
        pl.semaphore_wait(ready.at[n], len(close))

    tell(0)

    def slot(part, where, half=None):
        start, rows = PART_START[part], PART_ROWS[part]
        if half == 0:
            rows = PART_HALF[part]
        elif half == 1:
            start, rows = start + PART_HALF[part], rows - PART_HALF[part]
        at = []
        for axis in "zyx":
            offset = where.get(axis, 0)
            at.append(pl.ds(0, 4) if offset == "all" else lax.rem(place[axis] + offset, 4))
        return table_ref.at[(core, *at, pl.ds(start, rows), slice(None))]

    def remote(src, dst, send_sem, recv_sem, target):
        return pltpu.make_async_remote_copy(
            src_ref=src, dst_ref=dst, send_sem=send_sem, recv_sem=recv_sem,
            device_id=target, device_id_type=MESH,
        )

    def send_both(part, where, axis, send_sem, recv):
        dst = slot(part, where)
        src = dst if where else hub.at[pl.ds(PART_START[part], PART_ROWS[part])]
        remote(src, dst, send_sem, recv.at[0], near[axis, 1]).start()
        remote(src, dst, send_sem, recv.at[1], near[axis, 3]).start()

    def arrived(part, where, axis, sem, half=None):
        ref = slot(part, where, half)
        remote(ref, ref, sem, sem, near[axis, 1]).wait_recv()

    def pass_on(part, where, axis, send_sem, recv, half):
        ref = slot(part, where, half)
        remote(ref, ref, send_sem, recv.at[2 + half], near[axis, 1 if half == 0 else 3]).start()

    def to_sibling(part, where):
        ref = slot(part, where)
        remote(ref, ref, pair_send, pair_recv, sibling).start()

    parts = range(3)

    slot_row = lax.broadcasted_iota(jnp.int32, (8, 128), 0)

    def border_go(first, stop):
        @pl.loop(first, stop)
        def _(step):
            number, target = other(step)
            alive = slot_row < count_ref[0, number]
            for k in range(8):
                row = rows_ref[k, number]
                block = lax.shift_right_logical(row, 7)
                inside = row & 127
                for side in range(2):
                    outbox[number, side, pl.ds(k, 1), :] = local_ref[block, pl.ds(inside + 128 * side, 1), :]
            for side in range(2):
                outbox[number, side] = jnp.where(alive, outbox[number, side], 0.0)
            if first == 128:
                inbox[number] = outbox[number]
            else:
                remote(outbox.at[number], inbox.at[me], border_send, border_recv, target).start()

    def border_end():
        arrived_all = inbox.at[pl.ds(0, 127)]
        pltpu.make_async_copy(arrived_all, arrived_all, border_recv).wait()

        @pl.loop(0, 8)
        def _(i):
            for k in range(16):
                for side in range(2):
                    local_ref[32 + i, 128 * side + 8 * k:128 * side + 8 * k + 8, :] = inbox[16 * i + k, side]

    def pre_chunks(start, stop):
        @pl.loop(start, stop)
        def _(chunk):
            own = []
            for i in range(CHUNK // 128):
                block = local_ref[chunk * (CHUNK // 128) + i]
                own.append(jnp.concatenate([block[0:128], block[128:256]], axis=1))
            high, low = split(jnp.concatenate(own, axis=0))
            value = dot(jnp.concatenate([high, low, high], axis=1), self_k[...]) + bias_ref[...]
            for i in range(CHUNK // 128):
                for side in range(2):
                    local_ref[40 + chunk * (CHUNK // 128) + i, 128 * side:128 * side + 128, :] = value[
                        128 * i:128 * i + 128, 128 * side:128 * side + 128
                    ]

    lane = lax.broadcasted_iota(jnp.int32, (128, 128), 1)

    def tile_chunks(start, stop):
        @pl.loop(start, stop)
        def _(i):
            load_tiles(i).wait()
            spot = lax.rem(i, TILE_SLOTS)
            sums = sums_ref[...]
            for k in range(TILE_CHUNK):
                tile = i * TILE_CHUNK + k
                weight = ring[spot, k]
                high, low = split(weight)
                split_ref[tile, :, 0:128] = high
                split_ref[tile, :, 128:256] = low
                sums = jnp.where(lane == tile, jnp.sum(weight, axis=1, keepdims=True), sums)
            sums_ref[...] = sums

            @pl.when(i + TILE_SLOTS < 128 // TILE_CHUNK)
            def _():
                load_tiles(i + TILE_SLOTS).start()

    for p in parts:
        first, second, _ = PART_AXES[p]
        send_both(p, {}, first, send1.at[p], recv1.at[p])
        send_both(p, {}, second, send2.at[p], recv2.at[p, 0])

    sums_ref[...] = jnp.zeros_like(sums_ref)
    own.wait()
    for side, offset in ((0, 3), (1, 1)):
        unit = OFFSETS.index(offset)
        for p in parts:
            first, second, _ = PART_AXES[p]
            where = {first: offset}
            arrived(p, where, first, recv1.at[p, side])
            pass_on(p, where, first, send1.at[p], recv1.at[p], side)
            send_both(p, where, second, send2.at[p], recv2.at[p, unit])
        if side == 0:
            hear(0)
            tell(1)
    hear(1)
    tell(2)
    for p in parts:
        first, second, third = PART_AXES[p]
        where = {first: 2}
        arrived(p, where, first, recv1.at[p, 2], 0)
        arrived(p, where, first, recv1.at[p, 3], 1)
        send_both(p, where, second, send2.at[p], recv2.at[p, 3])
        line = {first: "all"}
        send_both(p, line, third, send3.at[p], recv3.at[p, 0])
        to_sibling(p, line)
    self_high, self_low = split(w_self_ref[...])
    self_k[0:256, :] = self_high
    self_k[256:512, :] = self_high
    self_k[512:768, :] = self_low

    hear(2)
    border_go(1, 65)
    for unit in range(4):
        for side, offset in ((0, 3), (1, 1)):
            for p in parts:
                first, second, _ = PART_AXES[p]
                where = {first: OFFSETS[unit], second: offset}
                arrived(p, where, second, recv2.at[p, unit, side])
                pass_on(p, where, second, send2.at[p], recv2.at[p, unit], side)
    for side, offset in ((0, 3), (1, 1)):
        for p in parts:
            first, second, third = PART_AXES[p]
            line = {first: "all", second: offset}
            send_both(p, line, third, send3.at[p], recv3.at[p, 1 + side])
            to_sibling(p, line)
    border_go(65, 128)
    border_go(128, 129)
    for p in parts:
        first, second, third = PART_AXES[p]
        for unit in range(4):
            where = {first: OFFSETS[unit], second: 2}
            arrived(p, where, second, recv2.at[p, unit, 2], 0)
            arrived(p, where, second, recv2.at[p, unit, 3], 1)
        line = {first: "all", second: 2}
        send_both(p, line, third, send3.at[p], recv3.at[p, 3])
        to_sibling(p, line)

    for unit in range(4):
        pre_chunks(4 * unit, 4 * unit + 4)
        for side, offset in ((0, 3), (1, 1)):
            for p in parts:
                first, second, third = PART_AXES[p]
                line = {first: "all", second: OFFSETS[unit], third: offset}
                arrived(p, line, third, recv3.at[p, unit, side])
                pass_on(p, line, third, send3.at[p], recv3.at[p, unit], side)
                to_sibling(p, line)
        if unit < 2:
            tile_chunks(8 * unit, 8 * unit + 8)
        if unit == 2:
            border_end()
    for unit in range(4):
        for p in parts:
            first, second, third = PART_AXES[p]
            line = {first: "all", second: OFFSETS[unit], third: 2}
            arrived(p, line, third, recv3.at[p, unit, 2], 0)
            arrived(p, line, third, recv3.at[p, unit, 3], 1)
            to_sibling(p, line)

    for p in parts:
        rows = pl.ds(PART_START[p], PART_ROWS[p])
        for sem, ref in (
            (send1.at[p], table_ref.at[core, 0, 0, pl.ds(0, 3), rows, :]),
            (send2.at[p], table_ref.at[core, 0, pl.ds(0, 3), pl.ds(0, 4), rows, :]),
            (send3.at[p], table_ref.at[core, pl.ds(0, 3), pl.ds(0, 4), pl.ds(0, 4), rows, :]),
        ):
            pltpu.make_async_copy(ref, ref, sem).wait()
    sent = outbox.at[pl.ds(0, 127)]
    pltpu.make_async_copy(sent, sent, border_send).wait()
    mine, theirs = table_ref.at[core], table_ref.at[1 - core]
    pltpu.make_async_copy(mine, mine, pair_send).wait()
    pltpu.make_async_copy(theirs, theirs, pair_recv).wait()


def gather(hub_block, send_rows, send_count, features, weights, w_self, bias):
    dma = pltpu.SemaphoreType.DMA
    smem = pl.BlockSpec(memory_space=pltpu.SMEM)
    vmem = pl.BlockSpec(memory_space=pltpu.VMEM)
    hbm = pl.BlockSpec(memory_space=pl.ANY)
    far = pl.BlockSpec(memory_space=pltpu.HBM)
    border = pltpu.VMEM((128, 2, 8, 128), F32)
    pin = functools.partial(pltpu.with_memory_space_constraint, memory_space=pltpu.HBM)
    return pl.pallas_call(
        gather_kernel,
        out_shape=(
            pltpu.VMEM((2, 4, 4, 4, 256, 128), F32),
            pltpu.VMEM((72, 256, 128), F32),
            pltpu.VMEM((128, 128, 256), BF16),
            pltpu.VMEM((128, 128), F32),
        ),
        in_specs=[smem] + [far] * 2 + [hbm] * 2 + [far] * 2,
        out_specs=(vmem,) * 4,
        scratch_shapes=[
            pltpu.SMEM(send_rows.shape, jnp.int32),
            pltpu.SMEM(send_count.shape, jnp.int32),
            pltpu.VMEM(w_self.shape, F32),
            pltpu.VMEM(bias.shape, F32),
            dma((4,)),
            pltpu.VMEM((256, 128), F32),
            pltpu.VMEM((768, 256), BF16),
            pltpu.VMEM((TILE_SLOTS, TILE_CHUNK, 128, 128), F32),
            border, border,
            dma, dma((2,)), dma((TILE_SLOTS,)), dma((3, 4)), dma((3, 4, 4)), dma((3, 4, 4)),
            dma((3,)), dma((3,)), dma((3,)), dma, dma,
            dma, dma, pltpu.SemaphoreType.REGULAR((3,)),
        ],
        compiler_params=pltpu.CompilerParams(
            collective_id=0, has_side_effects=True, vmem_limit_bytes=GATHER_VMEM * 2**20
        ),
        name="gather",
    )(hub_block, pin(send_rows), pin(send_count), features, weights, pin(w_self), pin(bias))


GROUP = 16


def tiles_kernel(
    dst_ref, src_ref, count_ref,
    table_ref, local_ref, split_ref, sums_ref, dst_row_ref,
    total, scales_ref,
    near_tiles, hub_tiles,
):
    tiles = split_ref.shape[0]
    blocks = total.shape[0] - 1
    first_hub = blocks + 8
    count = count_ref[0]

    total[...] = jnp.zeros_like(total)

    def sort_tile(tile, ends):
        near = jnp.where(src_ref[tile] < first_hub, 1, 0)
        for listed, end in zip((near_tiles, hub_tiles), ends):
            listed[end] = tile
        return ends[0] + near, ends[1] + (1 - near)

    amounts = lax.fori_loop(0, count, sort_tile, (0, 0))

    def wide(block):
        return jnp.concatenate([block[0:128], block[128:256]], axis=1)

    def near_source(src):
        return wide(local_ref[src])

    def hub_source(src):
        number = src - first_hub
        return wide(table_ref[
            lax.shift_right_logical(number, 1) & 1,
            lax.shift_right_logical(number, 5),
            (lax.shift_right_logical(number, 4) & 1) * 2 + (number & 1),
            lax.shift_right_logical(number, 2) & 3,
        ])

    by_lanes = (((1,), (1,)), ((), ()))
    tile_lane = lax.broadcasted_iota(jnp.int32, (blocks, tiles), 1)
    block_row = lax.broadcasted_iota(jnp.int32, (blocks, tiles), 0)
    chosen = (dst_row_ref[...] == block_row) & (tile_lane < count)
    chosen = jnp.where(chosen, 1.0, 0.0).astype(BF16)
    sums_high, sums_low = split(sums_ref[...])
    sums_rest = (sums_ref[...] - sums_high.astype(F32) - sums_low.astype(F32)).astype(BF16)
    scales_ref[...] = 1.0 / (
        1.0 + (dot(sums_high, chosen, by_lanes) + dot(sums_low, chosen, by_lanes) + dot(sums_rest, chosen, by_lanes))
    )

    work = ((near_tiles, near_source), (hub_tiles, hub_source))
    for (listed, source), amount in zip(work, amounts):
        @pl.loop(0, lax.div(amount + (GROUP - 1), GROUP))
        def _(group):
            products, targets = [], []
            for k in range(GROUP):
                at = group * GROUP + k
                tile = listed[jnp.minimum(at, amount - 1)]
                targets.append(jnp.where(at < amount, dst_ref[tile], blocks))
                weight = split_ref[tile]
                high, low = split(source(src_ref[tile]))
                products.append(
                    dot(
                        jnp.concatenate([weight, weight[:, 0:128]], axis=1),
                        jnp.concatenate([high, high, low], axis=0),
                    )
                )
            for k in range(GROUP):
                total[targets[k]] += products[k]


def add_tiles(dst, src, count, table, local, weights, sums, blocks):
    smem = pl.BlockSpec(memory_space=pltpu.SMEM)
    vmem = pl.BlockSpec(memory_space=pltpu.VMEM)
    listed = pltpu.SMEM((dst.shape[0] + 1,), jnp.int32)
    return pl.pallas_call(
        tiles_kernel,
        out_shape=(pltpu.VMEM((blocks + 1, 128, 256), F32), pltpu.VMEM((128, blocks), F32)),
        in_specs=[smem] * 3 + [vmem] * 5,
        out_specs=(vmem, vmem),
        scratch_shapes=[
            listed, listed,
        ],
        compiler_params=pltpu.CompilerParams(vmem_limit_bytes=TILES_VMEM * 2**20),
        name="add_tiles",
    )(dst, src, count, *(pltpu.with_memory_space_constraint(v, pltpu.VMEM) for v in (table, local, weights)), sums, dst.reshape(1, -1))


LAYER_CHUNK = 2048


def layer_kernel(
    loss_scale, total, scales_ref, local_ref, w_neigh_ref, head_ref, labels_ref,
    whole,
    neigh_k, grad_self, grad_neigh, grad_small, grads, pair_in, lots_in, small_in,
    send_sem, recv_sem,
):
    place, core = my_place()
    number = (place["z"] * 4 + place["y"]) * 4 + place["x"]
    sibling = device_at(place, 1 - core)

    away = {
        axis: [lax.rem(place[axis] + step, 4) for step in range(4)] for axis in "xyz"
    }
    along_y = [lax.div(y, 2) * 8 + core for y in away["y"]]
    row_y = [lax.rem(y, 2) for y in away["y"]]
    peers = []
    for dz, dy, dx in itertools.product(range(4), repeat=3):
        if dz + dy + dx:
            vert = away["z"][dz] * 16 + along_y[dy] + away["x"][dx] * 2
            other = away["z"][dz] * 16 + away["y"][dy] * 4 + away["x"][dx]
            peers.append((other, (vert, row_y[dy])))

    barrier = pltpu.get_barrier_semaphore()
    pl.semaphore_signal(barrier, inc=1, device_id=sibling, device_id_type=MESH)

    for _, target in peers:
        pl.semaphore_signal(barrier, inc=1, device_id=target, device_id_type=MESH)

    blocks = labels_ref.shape[0]
    neigh_high, neigh_low = split(w_neigh_ref[...])
    neigh_k[0:256, :] = neigh_high
    neigh_k[256:512, :] = neigh_high
    neigh_k[512:768, :] = neigh_low
    target_columns = (2.0 * labels_ref[...].astype(F32) - 1.0).T
    lane = lax.broadcasted_iota(jnp.int32, target_columns.shape, 1)
    grad_self[...] = jnp.zeros_like(grad_self)
    grad_neigh[...] = jnp.zeros_like(grad_neigh)
    grad_small[...] = jnp.zeros_like(grad_small)
    per_chunk = LAYER_CHUNK // 128

    def wide(block):
        return jnp.concatenate([block[0:128], block[128:256]], axis=1)

    @pl.loop(0, blocks // per_chunk)
    def _(chunk):
        own, mean, target, pre = [], [], [], []
        for i in range(per_chunk):
            b = chunk * per_chunk + i
            block = wide(local_ref[b])
            scale = jnp.sum(jnp.where(lane == b, scales_ref[...], 0.0), axis=1, keepdims=True)
            own.append(block)
            pre.append(wide(local_ref[blocks + 8 + b]))
            mean.append((block + total[b]) * scale)
            target.append(jnp.sum(jnp.where(lane == b, target_columns, 0.0), axis=1, keepdims=True))
        own, mean, target, pre = (jnp.concatenate(v, axis=0) for v in (own, mean, target, pre))
        own_high, own_low = split(own)
        mean_high, mean_low = split(mean)
        pre = pre + dot(jnp.concatenate([mean_high, mean_low, mean_high], axis=1), neigh_k[...])
        gate = jax.nn.sigmoid(pre)
        hidden = pre * gate
        score = jnp.sum(hidden * head_ref[...], axis=1, keepdims=True)
        dscore = (score - target) * loss_scale
        dpre = dscore * head_ref[...] * (gate * (1.0 + pre * (1.0 - gate)))
        d_high, d_low = split(dpre)
        by_rows = (((0,), (0,)), ((), ()))
        right = jnp.concatenate([d_high, d_high, d_low], axis=0)
        grad_self[...] += dot(jnp.concatenate([own_high, own_low, own_high], axis=0), right, by_rows)
        grad_neigh[...] += dot(jnp.concatenate([mean_high, mean_low, mean_high], axis=0), right, by_rows)
        grad_small[0:1, :] += jnp.sum(dpre, axis=0, keepdims=True)
        grad_small[1:2, :] += jnp.sum(hidden * dscore, axis=0, keepdims=True)

    for i, ref in enumerate((grad_self, grad_neigh)):
        for side in range(2):
            grads[pl.ds(512 * i + 256 * side, 256), :] = ref[:, 128 * side:128 * side + 128]
    grads[1024:1032, :] = jnp.zeros((8, 128), F32)
    for i in range(4):
        side = 128 * (i % 2)
        grads[1024 + i:1025 + i, :] = grad_small[i // 2:i // 2 + 1, side:side + 128]

    pl.semaphore_wait(barrier, 64)

    def send(stage, src, dst, target):
        pltpu.make_async_remote_copy(
            src_ref=src, dst_ref=dst, send_sem=send_sem.at[stage], recv_sem=recv_sem.at[stage],
            device_id=target, device_id_type=MESH,
        ).start()

    def received(stage, ref):
        pltpu.make_async_copy(ref, ref, recv_sem.at[stage]).wait()

    def sent(stage, ref):
        pltpu.make_async_copy(ref, ref, send_sem.at[stage]).wait()

    half, other_half = core * 512, (1 - core) * 512
    small = pl.ds(1024, 8)
    send(0, grads.at[pl.ds(other_half, 512)], pair_in.at[pl.ds(0, 512)], sibling)
    send(0, grads.at[small], pair_in.at[pl.ds(512, 8)], sibling)
    received(0, pair_in)
    pair_in[0:512, :] += grads[pl.ds(half, 512), :]
    pair_in[512:520, :] += grads[1024:1032, :]

    def lot(other):
        return pl.ds(pl.multiple_of(other * 8, 8), 8)

    first = (core == 0) & (number == 0)
    feeds_first = (core == 0) & (number != 0)

    @pl.when(feeds_first)
    def _():
        send(4, pair_in.at[pl.ds(512, 8)], small_in.at[number], device_at({"x": 0, "y": 0, "z": 0}, core))

    for other, target in peers:
        send(1, pair_in.at[lot(other)], lots_in.at[number], target)

    lots_in[number] = pair_in[lot(number), :]
    received(1, lots_in.at[pl.ds(0, 63)])
    mine = pl.ds(pl.multiple_of(half + number * 8, 8), 8)
    whole[mine, :] = jnp.sum(lots_in[...], axis=0)

    def from_plane(z):
        return recv_sem.at[7 + z]

    for _, target in peers:
        pltpu.make_async_remote_copy(
            src_ref=whole.at[mine], dst_ref=whole.at[mine], send_sem=send_sem.at[2],
            recv_sem=from_plane(place["z"]), device_id=target, device_id_type=MESH,
        ).start()

    @pl.when(first)
    def _():
        small_in[0] = pair_in[512:520, :]
        received(4, small_in.at[pl.ds(0, 63)])
        whole[1024:1032, :] = jnp.sum(small_in[...], axis=0)

        for _, target in peers:
            send(5, whole.at[small], whole.at[small], target)

    for step in (0, 1, 3, 2):
        z = lax.rem(place["z"] + step, 4)
        amount = whole.at[pl.ds(0, 128 if step else 120)]
        pltpu.make_async_copy(amount, amount, from_plane(z)).wait()
        plane = pl.ds(pl.multiple_of(half + z * 128, 128), 128)
        send(3, whole.at[plane], whole.at[plane], sibling)

    @pl.when(feeds_first)
    def _():
        received(5, whole.at[small])

    @pl.when(core == 0)
    def _():
        send(6, whole.at[small], whole.at[small], sibling)

    @pl.when(core == 1)
    def _():
        received(6, whole.at[small])

    received(3, whole.at[pl.ds(0, 512)])
    sent(0, pair_in)
    sent(1, lots_in.at[pl.ds(0, 63)])
    sent(2, whole.at[pl.ds(0, 504)])
    sent(3, whole.at[pl.ds(0, 512)])

    @pl.when(feeds_first)
    def _():
        sent(4, small_in.at[0])

    @pl.when(first)
    def _():
        sent(5, small_in.at[pl.ds(0, 63)])

    @pl.when(core == 0)
    def _():
        sent(6, whole.at[small])


def layer(loss_scale, total, scales, local, w_neigh, head, labels):
    vmem = pl.BlockSpec(memory_space=pltpu.VMEM)
    dma = pltpu.SemaphoreType.DMA
    width = w_neigh.shape[0]
    return pl.pallas_call(
        functools.partial(layer_kernel, loss_scale),
        out_shape=pltpu.VMEM((1032, 128), F32),
        in_specs=[vmem] * 6,
        out_specs=vmem,
        scratch_shapes=[
            pltpu.VMEM((3 * width, width), BF16),
            pltpu.VMEM((width, width), F32),
            pltpu.VMEM((width, width), F32),
            pltpu.VMEM((8, width), F32),
            pltpu.VMEM((1032, 128), F32),
            pltpu.VMEM((520, 128), F32),
            pltpu.VMEM((64, 8, 128), F32),
            pltpu.VMEM((64, 8, 128), F32),
            dma((7,)),
            dma((11,)),
        ],
        compiler_params=pltpu.CompilerParams(
            collective_id=1, has_side_effects=True, vmem_limit_bytes=LAYER_VMEM * 2**20
        ),
        name="layer",
    )(total, scales, local, w_neigh, head, labels)


def unpack_kernel(whole, self_ref, neigh_ref, bias_ref, head_ref):
    for i, ref in enumerate((self_ref, neigh_ref)):
        for side in range(2):
            ref[:, 128 * side:128 * side + 128] = whole[pl.ds(512 * i + 256 * side, 256), :]
    for i in range(4):
        ref = (bias_ref, head_ref)[i // 2]
        ref[128 * (i % 2):128 * (i % 2) + 128] = whole[1024 + i, :]


def unpack(whole):
    vmem = pl.BlockSpec(memory_space=pltpu.VMEM)
    return pl.pallas_call(
        unpack_kernel,
        out_shape=(
            jax.ShapeDtypeStruct((256, 256), F32),
            jax.ShapeDtypeStruct((256, 256), F32),
            jax.ShapeDtypeStruct((256,), F32),
            jax.ShapeDtypeStruct((256,), F32),
        ),
        in_specs=[vmem],
        out_specs=(vmem,) * 4,
        compiler_params=pltpu.CompilerParams(vmem_limit_bytes=4 * 2**20),
        name="unpack",
    )(whole)


def on_device(
    features,
    w_self,
    w_neigh,
    bias,
    w_head,
    tile_weights,
    tile_dst,
    tile_src,
    tile_count,
    hub_block,
    send_rows,
    send_count,
    labels,
):
    width = features.shape[1]
    blocks = features.shape[0] // 128
    vertex_total = features.shape[0] * lax.axis_size(("vert", "row"))
    loss_scale = 1.0 / math.sqrt(vertex_total)
    table, local, weights, sums = gather(
        hub_block, send_rows[0].T, send_count, features.reshape(blocks, 128, width), tile_weights,
        w_self, bias.reshape(1, width),
    )
    total, scales = add_tiles(tile_dst, tile_src, tile_count, table, local, weights, sums, blocks)
    return unpack(layer(loss_scale, total, scales, local, w_neigh, w_head.reshape(1, width), labels.reshape(blocks, 128)))


def solution(mesh):
    in_specs = (
        P(("vert", "row"), None),
        P(),
        P(),
        P(),
        P(),
        P(("vert", "row"), None, None),
        P(("vert", "row")),
        P(("vert", "row")),
        P(("vert", "row")),
        P(("vert", "row")),
        P(("vert", "row"), None, None),
        P(("vert", "row"), None),
        P(("vert", "row")),
    )
    out_specs = (P(), P(), P(), P())
    return jax.shard_map(
        on_device, mesh=mesh, in_specs=in_specs, out_specs=out_specs, check_vma=False
    )
```

```python
import functools
import itertools
import math

import jax
import jax.numpy as jnp
from jax import lax
from jax.experimental import pallas as pl
from jax.experimental.pallas import tpu as pltpu
from jax.sharding import PartitionSpec as P

MESH = pl.DeviceIdType.MESH
BF16 = jnp.bfloat16
F32 = jnp.float32

PART_START = (0, 88, 176)
PART_ROWS = (88, 88, 80)
PART_HALF = (48, 40, 40)
PART_AXES = ("xyz", "yzx", "zxy")
OFFSETS = (0, 3, 1, 2)


def my_place():
    vert = lax.axis_index("vert")
    row = lax.axis_index("row")
    core = lax.rem(vert, 2)
    x = lax.rem(lax.div(vert, 2), 4)
    y = lax.rem(lax.div(vert, 8), 2) * 2 + row
    z = lax.div(vert, 16)
    return {"x": x, "y": y, "z": z}, core


def device_at(place, core):
    x, y, z = place["x"], place["y"], place["z"]
    vert = ((z * 2 + lax.div(y, 2)) * 4 + x) * 2 + core
    return (vert, lax.rem(y, 2))


def shifted(place, axis, step):
    moved = dict(place)
    moved[axis] = lax.rem(place[axis] + step, 4)
    return moved


def split(value):
    high = value.astype(BF16)
    low = (value - high.astype(F32)).astype(BF16)
    return high, low


def dot(a, b, dims=(((1,), (0,)), ((), ()))):
    return lax.dot_general(a, b, dims, preferred_element_type=F32)


GATHER_VMEM, TILES_VMEM, LAYER_VMEM = 20, 12, 20
CHUNK = 256
TILE_CHUNK = 8
TILE_SLOTS = 4


def gather_kernel(
    hub_block_ref, rows_hbm, count_hbm, feat_hbm, weights_hbm, self_hbm, bias_hbm,
    table_ref, local_ref, split_ref, sums_ref,
    rows_ref, count_ref, w_self_ref, bias_ref, small_sem, hub, self_k, ring, outbox, inbox,
    own_sem, feat_sem, ring_sem, recv1, recv2, recv3, send1, send2, send3, pair_send, pair_recv,
    border_send, border_recv, ready,
):
    place, core = my_place()
    x, y, z = place["x"], place["y"], place["z"]
    near = {}
    for axis in "xyz":
        for step in (1, 2, 3):
            near[axis, step] = device_at(shifted(place, axis, step), core)
    sibling = device_at(place, 1 - core)
    me = lax.axis_index("vert") * 2 + lax.axis_index("row")

    def other(step):
        number = lax.rem(me + step, 128)
        return number, (lax.div(number, 2), lax.rem(number, 2))

    small_loads = [
        pltpu.make_async_copy(src, dst, small_sem.at[i])
        for i, (src, dst) in enumerate((
            (rows_hbm, rows_ref), (count_hbm, count_ref), (self_hbm, w_self_ref), (bias_hbm, bias_ref),
        ))
    ]
    loads = []
    for side in range(2):
        load = pltpu.make_async_copy(
            feat_hbm.at[:, :, pl.ds(128 * side, 128)],
            local_ref.at[pl.ds(0, 32), pl.ds(128 * side, 128), :],
            feat_sem.at[side],
        )
        load.start()
        loads.append(load)

    def load_tiles(i):
        spot = lax.rem(i, TILE_SLOTS)
        return pltpu.make_async_copy(
            weights_hbm.at[pl.ds(i * TILE_CHUNK, TILE_CHUNK)], ring.at[spot], ring_sem.at[spot]
        )

    for load in small_loads:
        load.start()
    for i in range(TILE_SLOTS):
        load_tiles(i).start()

    barrier = pltpu.get_barrier_semaphore()
    close = list(near.values()) + [sibling]
    for target in close:
        pl.semaphore_signal(barrier, inc=1, device_id=target, device_id_type=MESH)


    for load in loads:
        load.wait()
    hub[...] = local_ref[hub_block_ref[0]]
    for load in small_loads:
        load.wait()
    own = pltpu.make_async_copy(hub, table_ref.at[core, z, y, x], own_sem)
    own.start()
    pl.semaphore_wait(barrier, len(close))

    def tell(n):
        for target in close:
            pl.semaphore_signal(ready.at[n], inc=1, device_id=target, device_id_type=MESH)

    def hear(n):
        pl.semaphore_wait(ready.at[n], len(close))

    tell(0)

    def slot(part, where, half=None):
        start, rows = PART_START[part], PART_ROWS[part]
        if half == 0:
            rows = PART_HALF[part]
        elif half == 1:
            start, rows = start + PART_HALF[part], rows - PART_HALF[part]
        at = []
        for axis in "zyx":
            offset = where.get(axis, 0)
            at.append(pl.ds(0, 4) if offset == "all" else lax.rem(place[axis] + offset, 4))
        return table_ref.at[(core, *at, pl.ds(start, rows), slice(None))]

    def remote(src, dst, send_sem, recv_sem, target):
        return pltpu.make_async_remote_copy(
            src_ref=src, dst_ref=dst, send_sem=send_sem, recv_sem=recv_sem,
            device_id=target, device_id_type=MESH,
        )

    def send_both(part, where, axis, send_sem, recv):
        dst = slot(part, where)
        src = dst if where else hub.at[pl.ds(PART_START[part], PART_ROWS[part])]
        remote(src, dst, send_sem, recv.at[0], near[axis, 1]).start()
        remote(src, dst, send_sem, recv.at[1], near[axis, 3]).start()

    def arrived(part, where, axis, sem, half=None):
        ref = slot(part, where, half)
        remote(ref, ref, sem, sem, near[axis, 1]).wait_recv()

    def pass_on(part, where, axis, send_sem, recv, half):
        ref = slot(part, where, half)
        remote(ref, ref, send_sem, recv.at[2 + half], near[axis, 1 if half == 0 else 3]).start()

    def to_sibling(part, where):
        ref = slot(part, where)
        remote(ref, ref, pair_send, pair_recv, sibling).start()

    parts = range(3)

    slot_row = lax.broadcasted_iota(jnp.int32, (8, 128), 0)

    def border_go(first, stop):
        @pl.loop(first, stop)
        def _(step):
            number, target = other(step)
            alive = slot_row < count_ref[0, number]
            for k in range(8):
                row = rows_ref[k, number]
                block = lax.shift_right_logical(row, 7)
                inside = row & 127
                for side in range(2):
                    outbox[number, side, pl.ds(k, 1), :] = local_ref[block, pl.ds(inside + 128 * side, 1), :]
            for side in range(2):
                outbox[number, side] = jnp.where(alive, outbox[number, side], 0.0)
            if first == 128:
                inbox[number] = outbox[number]
            else:
                remote(outbox.at[number], inbox.at[me], border_send, border_recv, target).start()

    def border_end():
        arrived_all = inbox.at[pl.ds(0, 127)]
        pltpu.make_async_copy(arrived_all, arrived_all, border_recv).wait()

        @pl.loop(0, 8)
        def _(i):
            for k in range(16):
                for side in range(2):
                    local_ref[32 + i, 128 * side + 8 * k:128 * side + 8 * k + 8, :] = inbox[16 * i + k, side]

    def pre_chunks(start, stop):
        @pl.loop(start, stop)
        def _(chunk):
            own = []
            for i in range(CHUNK // 128):
                block = local_ref[chunk * (CHUNK // 128) + i]
                own.append(jnp.concatenate([block[0:128], block[128:256]], axis=1))
            high, low = split(jnp.concatenate(own, axis=0))
            value = dot(jnp.concatenate([high, low, high], axis=1), self_k[...]) + bias_ref[...]
            for i in range(CHUNK // 128):
                for side in range(2):
                    local_ref[40 + chunk * (CHUNK // 128) + i, 128 * side:128 * side + 128, :] = value[
                        128 * i:128 * i + 128, 128 * side:128 * side + 128
                    ]

    lane = lax.broadcasted_iota(jnp.int32, (128, 128), 1)

    def tile_chunks(start, stop):
        @pl.loop(start, stop)
        def _(i):
            load_tiles(i).wait()
            spot = lax.rem(i, TILE_SLOTS)
            sums = sums_ref[...]
            for k in range(TILE_CHUNK):
                tile = i * TILE_CHUNK + k
                weight = ring[spot, k]
                high, low = split(weight)
                split_ref[tile, :, 0:128] = high
                split_ref[tile, :, 128:256] = low
                sums = jnp.where(lane == tile, jnp.sum(weight, axis=1, keepdims=True), sums)
            sums_ref[...] = sums

            @pl.when(i + TILE_SLOTS < 128 // TILE_CHUNK)
            def _():
                load_tiles(i + TILE_SLOTS).start()

    for p in parts:
        first, second, _ = PART_AXES[p]
        send_both(p, {}, first, send1.at[p], recv1.at[p])
        send_both(p, {}, second, send2.at[p], recv2.at[p, 0])

    sums_ref[...] = jnp.zeros_like(sums_ref)
    own.wait()
    for side, offset in ((0, 3), (1, 1)):
        unit = OFFSETS.index(offset)
        for p in parts:
            first, second, _ = PART_AXES[p]
            where = {first: offset}
            arrived(p, where, first, recv1.at[p, side])
            pass_on(p, where, first, send1.at[p], recv1.at[p], side)
            send_both(p, where, second, send2.at[p], recv2.at[p, unit])
        if side == 0:
            hear(0)
            tell(1)
    hear(1)
    tell(2)
    for p in parts:
        first, second, third = PART_AXES[p]
        where = {first: 2}
        arrived(p, where, first, recv1.at[p, 2], 0)
        arrived(p, where, first, recv1.at[p, 3], 1)
        send_both(p, where, second, send2.at[p], recv2.at[p, 3])
        line = {first: "all"}
        send_both(p, line, third, send3.at[p], recv3.at[p, 0])
        to_sibling(p, line)
    self_high, self_low = split(w_self_ref[...])
    self_k[0:256, :] = self_high
    self_k[256:512, :] = self_high
    self_k[512:768, :] = self_low

    hear(2)
    border_go(1, 65)
    for unit in range(4):
        for side, offset in ((0, 3), (1, 1)):
            for p in parts:
                first, second, _ = PART_AXES[p]
                where = {first: OFFSETS[unit], second: offset}
                arrived(p, where, second, recv2.at[p, unit, side])
                pass_on(p, where, second, send2.at[p], recv2.at[p, unit], side)
    for side, offset in ((0, 3), (1, 1)):
        for p in parts:
            first, second, third = PART_AXES[p]
            line = {first: "all", second: offset}
            send_both(p, line, third, send3.at[p], recv3.at[p, 1 + side])
            to_sibling(p, line)
    border_go(65, 128)
    border_go(128, 129)
    for p in parts:
        first, second, third = PART_AXES[p]
        for unit in range(4):
            where = {first: OFFSETS[unit], second: 2}
            arrived(p, where, second, recv2.at[p, unit, 2], 0)
            arrived(p, where, second, recv2.at[p, unit, 3], 1)
        line = {first: "all", second: 2}
        send_both(p, line, third, send3.at[p], recv3.at[p, 3])
        to_sibling(p, line)

    for unit in range(4):
        pre_chunks(4 * unit, 4 * unit + 4)
        for side, offset in ((0, 3), (1, 1)):
            for p in parts:
                first, second, third = PART_AXES[p]
                line = {first: "all", second: OFFSETS[unit], third: offset}
                arrived(p, line, third, recv3.at[p, unit, side])
                pass_on(p, line, third, send3.at[p], recv3.at[p, unit], side)
                to_sibling(p, line)
        if unit < 2:
            tile_chunks(8 * unit, 8 * unit + 8)
        if unit == 2:
            border_end()
    for unit in range(4):
        for p in parts:
            first, second, third = PART_AXES[p]
            line = {first: "all", second: OFFSETS[unit], third: 2}
            arrived(p, line, third, recv3.at[p, unit, 2], 0)
            arrived(p, line, third, recv3.at[p, unit, 3], 1)
            to_sibling(p, line)

    for p in parts:
        rows = pl.ds(PART_START[p], PART_ROWS[p])
        for sem, ref in (
            (send1.at[p], table_ref.at[core, 0, 0, pl.ds(0, 3), rows, :]),
            (send2.at[p], table_ref.at[core, 0, pl.ds(0, 3), pl.ds(0, 4), rows, :]),
            (send3.at[p], table_ref.at[core, pl.ds(0, 3), pl.ds(0, 4), pl.ds(0, 4), rows, :]),
        ):
            pltpu.make_async_copy(ref, ref, sem).wait()
    sent = outbox.at[pl.ds(0, 127)]
    pltpu.make_async_copy(sent, sent, border_send).wait()
    mine, theirs = table_ref.at[core], table_ref.at[1 - core]
    pltpu.make_async_copy(mine, mine, pair_send).wait()
    pltpu.make_async_copy(theirs, theirs, pair_recv).wait()


def gather(hub_block, send_rows, send_count, features, weights, w_self, bias):
    dma = pltpu.SemaphoreType.DMA
    smem = pl.BlockSpec(memory_space=pltpu.SMEM)
    vmem = pl.BlockSpec(memory_space=pltpu.VMEM)
    hbm = pl.BlockSpec(memory_space=pl.ANY)
    far = pl.BlockSpec(memory_space=pltpu.HBM)
    border = pltpu.VMEM((128, 2, 8, 128), F32)
    pin = functools.partial(pltpu.with_memory_space_constraint, memory_space=pltpu.HBM)
    return pl.pallas_call(
        gather_kernel,
        out_shape=(
            pltpu.VMEM((2, 4, 4, 4, 256, 128), F32),
            pltpu.VMEM((72, 256, 128), F32),
            pltpu.VMEM((128, 128, 256), BF16),
            pltpu.VMEM((128, 128), F32),
        ),
        in_specs=[smem] + [far] * 2 + [hbm] * 2 + [far] * 2,
        out_specs=(vmem,) * 4,
        scratch_shapes=[
            pltpu.SMEM(send_rows.shape, jnp.int32),
            pltpu.SMEM(send_count.shape, jnp.int32),
            pltpu.VMEM(w_self.shape, F32),
            pltpu.VMEM(bias.shape, F32),
            dma((4,)),
            pltpu.VMEM((256, 128), F32),
            pltpu.VMEM((768, 256), BF16),
            pltpu.VMEM((TILE_SLOTS, TILE_CHUNK, 128, 128), F32),
            border, border,
            dma, dma((2,)), dma((TILE_SLOTS,)), dma((3, 4)), dma((3, 4, 4)), dma((3, 4, 4)),
            dma((3,)), dma((3,)), dma((3,)), dma, dma,
            dma, dma, pltpu.SemaphoreType.REGULAR((3,)),
        ],
        compiler_params=pltpu.CompilerParams(
            collective_id=0, has_side_effects=True, vmem_limit_bytes=GATHER_VMEM * 2**20
        ),
        name="gather",
    )(hub_block, pin(send_rows), pin(send_count), features, weights, pin(w_self), pin(bias))


GROUP = 16


def tiles_kernel(
    dst_ref, src_ref, count_ref,
    table_ref, local_ref, split_ref, sums_ref, dst_row_ref,
    total, scales_ref,
    near_tiles, hub_tiles,
):
    tiles = split_ref.shape[0]
    blocks = total.shape[0] - 1
    first_hub = blocks + 8
    count = count_ref[0]

    total[...] = jnp.zeros_like(total)

    def sort_tile(tile, ends):
        used = jnp.where(tile < count, 1, 0)
        near = jnp.where(src_ref[tile] < first_hub, used, 0)
        for listed, end in zip((near_tiles, hub_tiles), ends):
            listed[end] = tile
        return ends[0] + near, ends[1] + (used - near)

    amounts = lax.fori_loop(0, tiles, sort_tile, (0, 0), unroll=8)

    def wide(block):
        return jnp.concatenate([block[0:128], block[128:256]], axis=1)

    def near_source(src):
        return wide(local_ref[src])

    def hub_source(src):
        number = src - first_hub
        return wide(table_ref[
            lax.shift_right_logical(number, 1) & 1,
            lax.shift_right_logical(number, 5),
            (lax.shift_right_logical(number, 4) & 1) * 2 + (number & 1),
            lax.shift_right_logical(number, 2) & 3,
        ])

    by_lanes = (((1,), (1,)), ((), ()))
    tile_lane = lax.broadcasted_iota(jnp.int32, (blocks, tiles), 1)
    block_row = lax.broadcasted_iota(jnp.int32, (blocks, tiles), 0)
    chosen = (dst_row_ref[...] == block_row) & (tile_lane < count)
    chosen = jnp.where(chosen, 1.0, 0.0).astype(BF16)
    sums_high, sums_low = split(sums_ref[...])
    sums_rest = (sums_ref[...] - sums_high.astype(F32) - sums_low.astype(F32)).astype(BF16)
    scales_ref[...] = 1.0 / (
        1.0 + (dot(sums_high, chosen, by_lanes) + dot(sums_low, chosen, by_lanes) + dot(sums_rest, chosen, by_lanes))
    )

    work = ((near_tiles, near_source), (hub_tiles, hub_source))
    for (listed, source), amount in zip(work, amounts):
        @pl.loop(0, lax.div(amount + (GROUP - 1), GROUP))
        def _(group):
            products, targets = [], []
            for k in range(GROUP):
                at = group * GROUP + k
                tile = listed[jnp.minimum(at, amount - 1)]
                targets.append(jnp.where(at < amount, dst_ref[tile], blocks))
                weight = split_ref[tile]
                high, low = split(source(src_ref[tile]))
                products.append(
                    dot(
                        jnp.concatenate([weight, weight[:, 0:128]], axis=1),
                        jnp.concatenate([high, high, low], axis=0),
                    )
                )
            for k in range(GROUP):
                total[targets[k]] += products[k]


def add_tiles(dst, src, count, table, local, weights, sums, blocks):
    smem = pl.BlockSpec(memory_space=pltpu.SMEM)
    vmem = pl.BlockSpec(memory_space=pltpu.VMEM)
    listed = pltpu.SMEM((dst.shape[0] + 1,), jnp.int32)
    return pl.pallas_call(
        tiles_kernel,
        out_shape=(pltpu.VMEM((blocks + 1, 128, 256), F32), pltpu.VMEM((128, blocks), F32)),
        in_specs=[smem] * 3 + [vmem] * 5,
        out_specs=(vmem, vmem),
        scratch_shapes=[
            listed, listed,
        ],
        compiler_params=pltpu.CompilerParams(vmem_limit_bytes=TILES_VMEM * 2**20),
        name="add_tiles",
    )(dst, src, count, *(pltpu.with_memory_space_constraint(v, pltpu.VMEM) for v in (table, local, weights)), sums, dst.reshape(1, -1))


LAYER_CHUNK = 2048


def layer_kernel(
    loss_scale, total, scales_ref, local_ref, w_neigh_ref, head_ref, labels_ref,
    whole,
    neigh_k, grad_self, grad_neigh, grad_small, grads, pair_in, lots_in, small_in,
    send_sem, recv_sem,
):
    place, core = my_place()
    number = (place["z"] * 4 + place["y"]) * 4 + place["x"]
    sibling = device_at(place, 1 - core)

    away = {
        axis: [lax.rem(place[axis] + step, 4) for step in range(4)] for axis in "xyz"
    }
    along_y = [lax.div(y, 2) * 8 + core for y in away["y"]]
    row_y = [lax.rem(y, 2) for y in away["y"]]
    peers = []
    for dz, dy, dx in itertools.product(range(4), repeat=3):
        if dz + dy + dx:
            vert = away["z"][dz] * 16 + along_y[dy] + away["x"][dx] * 2
            other = away["z"][dz] * 16 + away["y"][dy] * 4 + away["x"][dx]
            peers.append((other, (vert, row_y[dy])))

    barrier = pltpu.get_barrier_semaphore()
    pl.semaphore_signal(barrier, inc=1, device_id=sibling, device_id_type=MESH)

    for _, target in peers:
        pl.semaphore_signal(barrier, inc=1, device_id=target, device_id_type=MESH)

    blocks = labels_ref.shape[0]
    neigh_high, neigh_low = split(w_neigh_ref[...])
    neigh_k[0:256, :] = neigh_high
    neigh_k[256:512, :] = neigh_high
    neigh_k[512:768, :] = neigh_low
    target_columns = (2.0 * labels_ref[...].astype(F32) - 1.0).T
    lane = lax.broadcasted_iota(jnp.int32, target_columns.shape, 1)
    grad_self[...] = jnp.zeros_like(grad_self)
    grad_neigh[...] = jnp.zeros_like(grad_neigh)
    grad_small[...] = jnp.zeros_like(grad_small)
    per_chunk = LAYER_CHUNK // 128

    def wide(block):
        return jnp.concatenate([block[0:128], block[128:256]], axis=1)

    @pl.loop(0, blocks // per_chunk)
    def _(chunk):
        own, mean, target, pre = [], [], [], []
        for i in range(per_chunk):
            b = chunk * per_chunk + i
            block = wide(local_ref[b])
            scale = jnp.sum(jnp.where(lane == b, scales_ref[...], 0.0), axis=1, keepdims=True)
            own.append(block)
            pre.append(wide(local_ref[blocks + 8 + b]))
            mean.append((block + total[b]) * scale)
            target.append(jnp.sum(jnp.where(lane == b, target_columns, 0.0), axis=1, keepdims=True))
        own, mean, target, pre = (jnp.concatenate(v, axis=0) for v in (own, mean, target, pre))
        own_high, own_low = split(own)
        mean_high, mean_low = split(mean)
        pre = pre + dot(jnp.concatenate([mean_high, mean_low, mean_high], axis=1), neigh_k[...])
        gate = jax.nn.sigmoid(pre)
        hidden = pre * gate
        score = jnp.sum(hidden * head_ref[...], axis=1, keepdims=True)
        dscore = (score - target) * loss_scale
        dpre = dscore * head_ref[...] * (gate * (1.0 + pre * (1.0 - gate)))
        d_high, d_low = split(dpre)
        by_rows = (((0,), (0,)), ((), ()))
        right = jnp.concatenate([d_high, d_high, d_low], axis=0)
        grad_self[...] += dot(jnp.concatenate([own_high, own_low, own_high], axis=0), right, by_rows)
        grad_neigh[...] += dot(jnp.concatenate([mean_high, mean_low, mean_high], axis=0), right, by_rows)
        grad_small[0:1, :] += jnp.sum(dpre, axis=0, keepdims=True)
        grad_small[1:2, :] += jnp.sum(hidden * dscore, axis=0, keepdims=True)

    for i, ref in enumerate((grad_self, grad_neigh)):
        for side in range(2):
            grads[pl.ds(512 * i + 256 * side, 256), :] = ref[:, 128 * side:128 * side + 128]
    grads[1024:1032, :] = jnp.zeros((8, 128), F32)
    for i in range(4):
        side = 128 * (i % 2)
        grads[1024 + i:1025 + i, :] = grad_small[i // 2:i // 2 + 1, side:side + 128]

    pl.semaphore_wait(barrier, 64)

    def send(stage, src, dst, target):
        pltpu.make_async_remote_copy(
            src_ref=src, dst_ref=dst, send_sem=send_sem.at[stage], recv_sem=recv_sem.at[stage],
            device_id=target, device_id_type=MESH,
        ).start()

    def received(stage, ref):
        pltpu.make_async_copy(ref, ref, recv_sem.at[stage]).wait()

    def sent(stage, ref):
        pltpu.make_async_copy(ref, ref, send_sem.at[stage]).wait()

    half, other_half = core * 512, (1 - core) * 512
    small = pl.ds(1024, 8)
    send(0, grads.at[pl.ds(other_half, 512)], pair_in.at[pl.ds(0, 512)], sibling)
    send(0, grads.at[small], pair_in.at[pl.ds(512, 8)], sibling)
    received(0, pair_in)
    pair_in[0:512, :] += grads[pl.ds(half, 512), :]
    pair_in[512:520, :] += grads[1024:1032, :]

    def lot(other):
        return pl.ds(pl.multiple_of(other * 8, 8), 8)

    first = (core == 0) & (number == 0)
    feeds_first = (core == 0) & (number != 0)

    @pl.when(feeds_first)
    def _():
        send(4, pair_in.at[pl.ds(512, 8)], small_in.at[number], device_at({"x": 0, "y": 0, "z": 0}, core))

    for other, target in peers:
        send(1, pair_in.at[lot(other)], lots_in.at[number], target)

    lots_in[number] = pair_in[lot(number), :]
    received(1, lots_in.at[pl.ds(0, 63)])
    mine = pl.ds(pl.multiple_of(half + number * 8, 8), 8)
    whole[mine, :] = jnp.sum(lots_in[...], axis=0)

    def from_plane(z):
        return recv_sem.at[7 + z]

    for _, target in peers:
        pltpu.make_async_remote_copy(
            src_ref=whole.at[mine], dst_ref=whole.at[mine], send_sem=send_sem.at[2],
            recv_sem=from_plane(place["z"]), device_id=target, device_id_type=MESH,
        ).start()

    @pl.when(first)
    def _():
        small_in[0] = pair_in[512:520, :]
        received(4, small_in.at[pl.ds(0, 63)])
        whole[1024:1032, :] = jnp.sum(small_in[...], axis=0)

        for _, target in peers:
            send(5, whole.at[small], whole.at[small], target)

    for step in (0, 1, 3, 2):
        z = lax.rem(place["z"] + step, 4)
        amount = whole.at[pl.ds(0, 128 if step else 120)]
        pltpu.make_async_copy(amount, amount, from_plane(z)).wait()
        plane = pl.ds(pl.multiple_of(half + z * 128, 128), 128)
        send(3, whole.at[plane], whole.at[plane], sibling)

    @pl.when(feeds_first)
    def _():
        received(5, whole.at[small])

    @pl.when(core == 0)
    def _():
        send(6, whole.at[small], whole.at[small], sibling)

    @pl.when(core == 1)
    def _():
        received(6, whole.at[small])

    received(3, whole.at[pl.ds(0, 512)])
    sent(0, pair_in)
    sent(1, lots_in.at[pl.ds(0, 63)])
    sent(2, whole.at[pl.ds(0, 504)])
    sent(3, whole.at[pl.ds(0, 512)])

    @pl.when(feeds_first)
    def _():
        sent(4, small_in.at[0])

    @pl.when(first)
    def _():
        sent(5, small_in.at[pl.ds(0, 63)])

    @pl.when(core == 0)
    def _():
        sent(6, whole.at[small])


def layer(loss_scale, total, scales, local, w_neigh, head, labels):
    vmem = pl.BlockSpec(memory_space=pltpu.VMEM)
    dma = pltpu.SemaphoreType.DMA
    width = w_neigh.shape[0]
    return pl.pallas_call(
        functools.partial(layer_kernel, loss_scale),
        out_shape=pltpu.VMEM((1032, 128), F32),
        in_specs=[vmem] * 6,
        out_specs=vmem,
        scratch_shapes=[
            pltpu.VMEM((3 * width, width), BF16),
            pltpu.VMEM((width, width), F32),
            pltpu.VMEM((width, width), F32),
            pltpu.VMEM((8, width), F32),
            pltpu.VMEM((1032, 128), F32),
            pltpu.VMEM((520, 128), F32),
            pltpu.VMEM((64, 8, 128), F32),
            pltpu.VMEM((64, 8, 128), F32),
            dma((7,)),
            dma((11,)),
        ],
        compiler_params=pltpu.CompilerParams(
            collective_id=1, has_side_effects=True, vmem_limit_bytes=LAYER_VMEM * 2**20
        ),
        name="layer",
    )(total, scales, local, w_neigh, head, labels)


def unpack_kernel(whole, self_ref, neigh_ref, bias_ref, head_ref):
    for i, ref in enumerate((self_ref, neigh_ref)):
        for side in range(2):
            ref[:, 128 * side:128 * side + 128] = whole[pl.ds(512 * i + 256 * side, 256), :]
    for i in range(4):
        ref = (bias_ref, head_ref)[i // 2]
        ref[128 * (i % 2):128 * (i % 2) + 128] = whole[1024 + i, :]


def unpack(whole):
    vmem = pl.BlockSpec(memory_space=pltpu.VMEM)
    return pl.pallas_call(
        unpack_kernel,
        out_shape=(
            jax.ShapeDtypeStruct((256, 256), F32),
            jax.ShapeDtypeStruct((256, 256), F32),
            jax.ShapeDtypeStruct((256,), F32),
            jax.ShapeDtypeStruct((256,), F32),
        ),
        in_specs=[vmem],
        out_specs=(vmem,) * 4,
        compiler_params=pltpu.CompilerParams(vmem_limit_bytes=4 * 2**20),
        name="unpack",
    )(whole)


def on_device(
    features,
    w_self,
    w_neigh,
    bias,
    w_head,
    tile_weights,
    tile_dst,
    tile_src,
    tile_count,
    hub_block,
    send_rows,
    send_count,
    labels,
):
    width = features.shape[1]
    blocks = features.shape[0] // 128
    vertex_total = features.shape[0] * lax.axis_size(("vert", "row"))
    loss_scale = 1.0 / math.sqrt(vertex_total)
    table, local, weights, sums = gather(
        hub_block, send_rows[0].T, send_count, features.reshape(blocks, 128, width), tile_weights,
        w_self, bias.reshape(1, width),
    )
    total, scales = add_tiles(tile_dst, tile_src, tile_count, table, local, weights, sums, blocks)
    return unpack(layer(loss_scale, total, scales, local, w_neigh, w_head.reshape(1, width), labels.reshape(blocks, 128)))


def solution(mesh):
    in_specs = (
        P(("vert", "row"), None),
        P(),
        P(),
        P(),
        P(),
        P(("vert", "row"), None, None),
        P(("vert", "row")),
        P(("vert", "row")),
        P(("vert", "row")),
        P(("vert", "row")),
        P(("vert", "row"), None, None),
        P(("vert", "row"), None),
        P(("vert", "row")),
    )
    out_specs = (P(), P(), P(), P())
    return jax.shard_map(
        on_device, mesh=mesh, in_specs=in_specs, out_specs=out_specs, check_vma=False
    )
```
